32 devices in a mesh: gx: 4 (over y, x), gy: 4 (over z), gz: 2 (over core).
Axes of the slice: x: 2, y: 2, z: 4, core: 2. Of those that a mesh axis runs over, the one named last changes fastest.
Arguments:
- viscosity: float32 [32, 64, 512], P('gz', 'gy', 'gx'), may hold values from 0.1 to 10
- adjoint_source: float32 [32, 64, 512], P('gz', 'gy', 'gx'), may hold values from -6 to 6
- forward_velocity: float32 [32, 64, 512], P('gz', 'gy', 'gx'), may hold values from -6 to 6
- friction: float32 [64, 512], P('gy', 'gx'), may hold values from 0.1 to 10
- ice_mask: int32 [64, 512], P('gy', 'gx'), may hold values 0 or 1
- grounded_mask: int32 [64, 512], P('gy', 'gx'), may hold values 0 or 1
Outputs:
- adjoint: float32 [32, 64, 512], P('gz', 'gy', 'gx')
- gradient: float32 [64, 512], P('gy', ('gx', 'gz'))
The draws below stay inside these ranges and needn't reach their ends.
All inputs are finite; a program needn't handle non-finite values. No bound on the sum of `ice_mask` or of `grounded_mask` on one device may be relied on, other than what follows from the above.
Results may differ from the reference program's by a relative error of at most 0.00002.
Values sent between devices are 32-bit elements; how exact they have to be, the bound alone decides.
No kernel may reach another device: no remote copies, remote signals or barrier semaphores. Data moves between devices by JAX's collectives and lax.ppermute only.
A program may use at most 64 MiB of HBM per device.

```python
import math
import jax
import jax.numpy as jnp

S0 = 4
S1 = 4
S2 = 8
NX = 512
NY = 64
NZ = 32


def touch_ends(drawn, stream_key, low, high):
    dims = drawn.shape
    index_at = [jax.random.randint(jax.random.fold_in(stream_key, axis), (), 0, dims[axis]) for axis in range(len(dims))]
    drawn = drawn.at[tuple(index_at)].set(low)
    longest = dims.index(max(dims))
    index_at[longest] = (index_at[longest] + 1) % dims[longest]
    return drawn.at[tuple(index_at)].set(high)


def block_levels(own_key, dims, cuts, low, largest):
    def one(axis_at, blocks):
        steps = jax.random.uniform(jax.random.fold_in(jax.random.fold_in(own_key, 6), axis_at), (blocks,), jnp.float32, low / len(cuts), largest / len(cuts))
        return jnp.repeat(jnp.exp(steps), dims[axis_at] // blocks).reshape((-1,) + (1,) * (len(dims) - axis_at - 1))

    loudness = one(*cuts[0])
    for cut in cuts[1:]:
        loudness = loudness * one(*cut)
    return loudness


def scatter_about(rng, dims, width, bound, split=(), kind=jnp.bfloat16):
    values = jax.random.normal(rng, dims, jnp.float32) * width
    if len(split) > 0:
        values = block_levels(rng, dims, split, -0.22, 0.18) * values
    return jnp.clip(values, min=-bound, max=bound).astype(kind)


def setup_inputs(seed: int = 0) -> dict:
    seeds = jax.random.split(jax.random.key(seed), 7)
    viscosity = jnp.clip(jnp.exp(math.log(10.0) - 4.6051702 * jax.random.uniform(seeds[0], (NZ, NY, NX), jnp.float32) ** block_levels(seeds[0], (NZ, NY, NX), ((0, 2), (1, 4), (2, 4)), -0.2, 0.2)), 0.1, 10.0)
    adjoint_source = scatter_about(seeds[1], (NZ, NY, NX), 1.0, 6.0, ((0, 2), (1, 4), (2, 4)), jnp.float32)
    forward_velocity = scatter_about(seeds[2], (NZ, NY, NX), 1.0, 6.0, ((0, 2), (1, 4), (2, 4)), jnp.float32)
    friction = jnp.clip(jnp.exp(math.log(10.0) - 4.6051702 * jax.random.uniform(seeds[3], (NY, NX), jnp.float32) ** block_levels(seeds[3], (NY, NX), ((0, 4), (1, 4)), -0.2, 0.2)), 0.1, 10.0)
    ice_mask = touch_ends((jax.random.randint(seeds[4], (NY, NX), 0, 4) < 3).astype(jnp.int32), jax.random.fold_in(seeds[4], 1), 0, 1)
    grounded_mask = touch_ends((jax.random.randint(seeds[5], (NY, NX), 0, 2) < 1).astype(jnp.int32), jax.random.fold_in(seeds[5], 1), 0, 1)
    return {"viscosity": viscosity, "adjoint_source": adjoint_source, "forward_velocity": forward_velocity, "friction": friction, "ice_mask": ice_mask, "grounded_mask": grounded_mask}


OMEGA = 0.8
VERT = 4.0


def face_set(eta_pad):
    centre = eta_pad[1:-1, 1:-1, 1:-1]
    zlo = VERT * (0.5 * (centre + eta_pad[:-2, 1:-1, 1:-1]))
    zhi = VERT * (0.5 * (centre + eta_pad[2:, 1:-1, 1:-1]))
    ylo = 0.5 * (centre + eta_pad[1:-1, :-2, 1:-1])
    yhi = 0.5 * (centre + eta_pad[1:-1, 2:, 1:-1])
    xlo = 0.5 * (centre + eta_pad[1:-1, 1:-1, :-2])
    xhi = 0.5 * (centre + eta_pad[1:-1, 1:-1, 2:])
    return (zlo, zhi, ylo, yhi, xlo, xhi)


def operate(u_pad, coef):
    zlo, zhi, ylo, yhi, xlo, xhi, extra = coef
    u = u_pad[1:-1, 1:-1, 1:-1]
    out = zlo * (u - u_pad[:-2, 1:-1, 1:-1]) + zhi * (u - u_pad[2:, 1:-1, 1:-1])
    out = out + ylo * (u - u_pad[1:-1, :-2, 1:-1]) + yhi * (u - u_pad[1:-1, 2:, 1:-1])
    out = out + xlo * (u - u_pad[1:-1, 1:-1, :-2]) + xhi * (u - u_pad[1:-1, 1:-1, 2:])
    return out + extra * u


def diagonal(coef):
    zlo, zhi, ylo, yhi, xlo, xhi, extra = coef
    return zlo + zhi + ylo + yhi + xlo + xhi + extra


def mean_four(a):
    return 0.25 * (a[:, 0::2, 0::2] + a[:, 1::2, 0::2] + a[:, 0::2, 1::2] + a[:, 1::2, 1::2])


def coarsen(coef):
    zlo, zhi, ylo, yhi, xlo, xhi, extra = coef
    cxlo = 0.125 * (xlo[:, 0::2, 0::2] + xlo[:, 1::2, 0::2])
    cxhi = 0.125 * (xhi[:, 0::2, 1::2] + xhi[:, 1::2, 1::2])
    cylo = 0.125 * (ylo[:, 0::2, 0::2] + ylo[:, 0::2, 1::2])
    cyhi = 0.125 * (yhi[:, 1::2, 0::2] + yhi[:, 1::2, 1::2])
    return (mean_four(zlo), mean_four(zhi), cylo, cyhi, cxlo, cxhi, mean_four(extra))


def prolong(e):
    return jnp.repeat(jnp.repeat(e, 2, axis=1), 2, axis=2)


def sweep(u, rhs, coef, diag):
    return u + OMEGA * (rhs - operate(jnp.pad(u, 1), coef)) / diag


def reference(viscosity, adjoint_source, forward_velocity, friction, ice_mask, grounded_mask):
    depth = viscosity.shape[0]
    layer = jnp.arange(depth).astype(jnp.float32)
    profile = (jnp.float32(depth) - layer) / jnp.float32(depth)
    wsq = profile * profile
    icef = ice_mask.astype(jnp.float32)
    groundf = grounded_mask.astype(jnp.float32)
    base = 0.05 + 2.0 * (1.0 - icef)
    extra = base[None, :, :] + (groundf * friction)[None, :, :] * wsq[:, None, None]
    fine = face_set(jnp.pad(viscosity, 1)) + (extra,)
    dfine = diagonal(fine)
    middle = coarsen(fine)
    dmid = diagonal(middle)
    coarse = coarsen(middle)
    dcoarse = diagonal(coarse)
    lam = jnp.zeros_like(adjoint_source)
    for i in range(S0):
        lam = sweep(lam, adjoint_source, fine, dfine)
    b1 = mean_four(adjoint_source - operate(jnp.pad(lam, 1), fine))
    e1 = jnp.zeros_like(b1)
    for i in range(S1):
        e1 = sweep(e1, b1, middle, dmid)
    b2 = mean_four(b1 - operate(jnp.pad(e1, 1), middle))
    e2 = jnp.zeros_like(b2)
    for i in range(S2):
        e2 = sweep(e2, b2, coarse, dcoarse)
    e1 = e1 + prolong(e2)
    for i in range(S1):
        e1 = sweep(e1, b1, middle, dmid)
    lam = lam + prolong(e1)
    for i in range(S0):
        lam = sweep(lam, adjoint_source, fine, dfine)
    column = jnp.sum(wsq[:, None, None] * forward_velocity * lam, axis=0)
    gradient = -(groundf * friction) * column
    return lam, gradient
```

```python
import jax
import jax.numpy as jnp
from jax import lax
from jax.sharding import PartitionSpec as P

S0 = 4
S1 = 4
S2 = 8


OMEGA = 0.8
VERT = 4.0


def face_halos(cells, axis, dim):
    count = lax.axis_size(axis)
    head = lax.slice_in_dim(cells, 0, 1, axis=dim)
    tail = lax.slice_in_dim(cells, cells.shape[dim] - 1, cells.shape[dim], axis=dim)
    lo = lax.ppermute(tail, axis, [(i, i + 1) for i in range(count - 1)])
    hi = lax.ppermute(head, axis, [(i + 1, i) for i in range(count - 1)])
    return lo, hi


def shifted(cells, lo, hi, dim):
    n = cells.shape[dim]
    down = jnp.concatenate([lo, lax.slice_in_dim(cells, 0, n - 1, axis=dim)], axis=dim)
    up = jnp.concatenate([lax.slice_in_dim(cells, 1, n, axis=dim), hi], axis=dim)
    return down, up


def neighbours(u):
    ylo, yhi = face_halos(u, "gy", 1)
    xlo, xhi = face_halos(u, "gx", 2)
    zeros = jnp.zeros_like(u[:1])
    zm, zp = shifted(u, zeros, zeros, 0)
    ym, yp = shifted(u, ylo, yhi, 1)
    xm, xp = shifted(u, xlo, xhi, 2)
    return zm, zp, ym, yp, xm, xp


def face_set(eta):
    zm, zp, ym, yp, xm, xp = neighbours(eta)
    zlo = VERT * (0.5 * (eta + zm))
    zhi = VERT * (0.5 * (eta + zp))
    ylo = 0.5 * (eta + ym)
    yhi = 0.5 * (eta + yp)
    xlo = 0.5 * (eta + xm)
    xhi = 0.5 * (eta + xp)
    return (zlo, zhi, ylo, yhi, xlo, xhi)


def operate(u, coef):
    zlo, zhi, ylo, yhi, xlo, xhi, extra = coef
    zm, zp, ym, yp, xm, xp = neighbours(u)
    out = zlo * (u - zm) + zhi * (u - zp)
    out = out + ylo * (u - ym) + yhi * (u - yp)
    out = out + xlo * (u - xm) + xhi * (u - xp)
    return out + extra * u


def diagonal(coef):
    zlo, zhi, ylo, yhi, xlo, xhi, extra = coef
    return zlo + zhi + ylo + yhi + xlo + xhi + extra


def mean_four(a):
    return 0.25 * (a[:, 0::2, 0::2] + a[:, 1::2, 0::2] + a[:, 0::2, 1::2] + a[:, 1::2, 1::2])


def coarsen(coef):
    zlo, zhi, ylo, yhi, xlo, xhi, extra = coef
    cxlo = 0.125 * (xlo[:, 0::2, 0::2] + xlo[:, 1::2, 0::2])
    cxhi = 0.125 * (xhi[:, 0::2, 1::2] + xhi[:, 1::2, 1::2])
    cylo = 0.125 * (ylo[:, 0::2, 0::2] + ylo[:, 0::2, 1::2])
    cyhi = 0.125 * (yhi[:, 1::2, 0::2] + yhi[:, 1::2, 1::2])
    return (mean_four(zlo), mean_four(zhi), cylo, cyhi, cxlo, cxhi, mean_four(extra))


def prolong(field):
    return jnp.repeat(jnp.repeat(field, 2, axis=1), 2, axis=2)


def sweep(field, rhs, coef, diag):
    return field + OMEGA * (rhs - operate(field, coef)) / diag


def body(viscosity, adjoint_source, forward_velocity, friction, ice_mask, grounded_mask):
    layers = viscosity.shape[0]
    half_cols = viscosity.shape[2] // 2
    gz = lax.axis_index("gz")
    viscosity = lax.all_gather(viscosity, "gz", axis=0, tiled=True)
    adjoint_source = lax.all_gather(adjoint_source, "gz", axis=0, tiled=True)
    forward_velocity = lax.all_gather(forward_velocity, "gz", axis=0, tiled=True)
    total_layers = viscosity.shape[0]
    layer = jnp.arange(total_layers).astype(jnp.float32)
    profile = (jnp.float32(total_layers) - layer) / jnp.float32(total_layers)
    wsq = profile * profile
    icef = ice_mask.astype(jnp.float32)
    groundf = grounded_mask.astype(jnp.float32)
    base = 0.05 + 2.0 * (1.0 - icef)
    extra = base[None, :, :] + (groundf * friction)[None, :, :] * wsq[:, None, None]
    fine = face_set(viscosity) + (extra,)
    dfine = diagonal(fine)
    middle = coarsen(fine)
    dmid = diagonal(middle)
    coarse = coarsen(middle)
    dcoarse = diagonal(coarse)
    lam = OMEGA * adjoint_source / dfine
    for i in range(S0 - 1):
        lam = sweep(lam, adjoint_source, fine, dfine)
    b_mid = mean_four(adjoint_source - operate(lam, fine))
    e_mid = OMEGA * b_mid / dmid
    for i in range(S1 - 1):
        e_mid = sweep(e_mid, b_mid, middle, dmid)
    b_low = mean_four(b_mid - operate(e_mid, middle))
    e_low = OMEGA * b_low / dcoarse
    for i in range(S2 - 1):
        e_low = sweep(e_low, b_low, coarse, dcoarse)
    e_mid = e_mid + prolong(e_low)
    for i in range(S1):
        e_mid = sweep(e_mid, b_mid, middle, dmid)
    lam = lam + prolong(e_mid)
    for i in range(S0):
        lam = sweep(lam, adjoint_source, fine, dfine)
    column = jnp.sum(wsq[:, None, None] * forward_velocity * lam, axis=0)
    terms = -(groundf * friction) * column
    gradient = lax.dynamic_slice_in_dim(terms, gz * half_cols, half_cols, 1)
    own = lax.dynamic_slice_in_dim(lam, gz * layers, layers, 0)
    return (own, gradient)


def solution(mesh):
    placed = (
        P("gz", "gy", "gx"),
        P("gz", "gy", "gx"),
        P("gz", "gy", "gx"),
        P("gy", "gx"),
        P("gy", "gx"),
        P("gy", "gx"),
    )
    return jax.shard_map(
        body,
        mesh=mesh,
        in_specs=placed,
        out_specs=(P("gz", "gy", "gx"), P("gy", ("gx", "gz"))),
        check_vma=False,
    )
```

```python
import jax
import jax.numpy as jnp
from jax import lax
from jax.sharding import PartitionSpec as P

S0 = 4
S1 = 4
S2 = 8


OMEGA = 0.8
VERT = 4.0
HI = lax.Precision.HIGHEST


def layer_halos(u):
    count = lax.axis_size("gz")
    head = u[:1]
    tail = u[-1:]
    if count == 2:
        first = lax.axis_index("gz") == 0
        got = lax.ppermute(jnp.where(first, tail, head), "gz", [(0, 1), (1, 0)])
        zero = jnp.zeros_like(got)
        return jnp.where(first, zero, got), jnp.where(first, got, zero)
    lo = lax.ppermute(tail, "gz", [(i, i + 1) for i in range(count - 1)])
    hi = lax.ppermute(head, "gz", [(i + 1, i) for i in range(count - 1)])
    return lo, hi


def row_halos(u):
    count = lax.axis_size("gy")
    lo = lax.ppermute(u[:, -1:], "gy", [(i, i + 1) for i in range(count - 1)])
    hi = lax.ppermute(u[:, :1], "gy", [(i + 1, i) for i in range(count - 1)])
    return lo, hi


def neighbours(u):
    zlo, zhi = layer_halos(u)
    ylo, yhi = row_halos(u)
    zero = jnp.zeros_like(u[:, :, :1])
    zm = jnp.concatenate([zlo, u[:-1]], axis=0)
    zp = jnp.concatenate([u[1:], zhi], axis=0)
    ym = jnp.concatenate([ylo, u[:, :-1]], axis=1)
    yp = jnp.concatenate([u[:, 1:], yhi], axis=1)
    xm = jnp.concatenate([zero, u[:, :, :-1]], axis=2)
    xp = jnp.concatenate([u[:, :, 1:], zero], axis=2)
    return zm, zp, ym, yp, xm, xp


def face_set(eta):
    zm, zp, ym, yp, xm, xp = neighbours(eta)
    zlo = VERT * (0.5 * (eta + zm))
    zhi = VERT * (0.5 * (eta + zp))
    ylo = 0.5 * (eta + ym)
    yhi = 0.5 * (eta + yp)
    xlo = 0.5 * (eta + xm)
    xhi = 0.5 * (eta + xp)
    return (zlo, zhi, ylo, yhi, xlo, xhi)


def operate(u, coef):
    zlo, zhi, ylo, yhi, xlo, xhi, extra = coef
    zm, zp, ym, yp, xm, xp = neighbours(u)
    out = zlo * (u - zm) + zhi * (u - zp)
    out = out + ylo * (u - ym) + yhi * (u - yp)
    out = out + xlo * (u - xm) + xhi * (u - xp)
    return out + extra * u


def diagonal(coef):
    zlo, zhi, ylo, yhi, xlo, xhi, extra = coef
    return zlo + zhi + ylo + yhi + xlo + xhi + extra


def pick_matrix(cols):
    half = cols // 2
    src = lax.broadcasted_iota(jnp.int32, (cols, cols), 0)
    dst = lax.broadcasted_iota(jnp.int32, (cols, cols), 1)
    want = jnp.where(dst < half, 2 * dst, 2 * (dst - half) + 1)
    return (src == want).astype(jnp.float32)


def split_x(a):
    cols = a.shape[-1]
    both = jnp.dot(a, pick_matrix(cols), precision=HI)
    return both[..., : cols // 2], both[..., cols // 2 :]


def mean_four(a):
    e0, o0 = split_x(a[:, 0::2])
    e1, o1 = split_x(a[:, 1::2])
    return 0.25 * (e0 + e1 + o0 + o1)


def coarsen(coef):
    zlo, zhi, ylo, yhi, xlo, xhi, extra = coef
    xlo_e, _ = split_x(xlo[:, 0::2] + xlo[:, 1::2])
    _, xhi_o = split_x(xhi[:, 0::2] + xhi[:, 1::2])
    ylo_e, ylo_o = split_x(ylo[:, 0::2])
    yhi_e, yhi_o = split_x(yhi[:, 1::2])
    cxlo = 0.125 * xlo_e
    cxhi = 0.125 * xhi_o
    cylo = 0.125 * (ylo_e + ylo_o)
    cyhi = 0.125 * (yhi_e + yhi_o)
    return (mean_four(zlo), mean_four(zhi), cylo, cyhi, cxlo, cxhi, mean_four(extra))


def prolong(field):
    cols = field.shape[-1]
    src = lax.broadcasted_iota(jnp.int32, (cols, 2 * cols), 0)
    dst = lax.broadcasted_iota(jnp.int32, (cols, 2 * cols), 1)
    spread = (src == dst // 2).astype(jnp.float32)
    wide = jnp.dot(field, spread, precision=HI)
    return jnp.repeat(wide, 2, axis=1)


def sweep(field, rhs, coef, diag):
    return field + OMEGA * (rhs - operate(field, coef)) / diag


def body(viscosity, adjoint_source, forward_velocity, friction, ice_mask, grounded_mask):
    layers = viscosity.shape[0]
    cols = viscosity.shape[2]
    half_cols = cols // 2
    gz = lax.axis_index("gz")
    total_layers = layers * lax.axis_size("gz")
    layer = (gz * layers + jnp.arange(layers)).astype(jnp.float32)
    profile = (jnp.float32(total_layers) - layer) / jnp.float32(total_layers)
    wsq = profile * profile
    icef = ice_mask.astype(jnp.float32)
    groundf = grounded_mask.astype(jnp.float32)
    base = 0.05 + 2.0 * (1.0 - icef)
    ground_fric = groundf * friction
    stacked = jnp.concatenate([viscosity, adjoint_source, base[None], ground_fric[None]], axis=0)
    gathered = lax.all_gather(stacked, "gx", axis=0, tiled=False)
    count_x = gathered.shape[0]
    gathered = jnp.concatenate([gathered[i] for i in range(count_x)], axis=2)
    visc_all = gathered[:layers]
    source_all = gathered[layers : 2 * layers]
    base_all = gathered[2 * layers]
    gfr_all = gathered[2 * layers + 1]
    extra = base_all[None, :, :] + gfr_all[None, :, :] * wsq[:, None, None]
    fine = face_set(visc_all) + (extra,)
    dfine = diagonal(fine)
    middle = coarsen(fine)
    dmid = diagonal(middle)
    coarse = coarsen(middle)
    dcoarse = diagonal(coarse)
    lam = OMEGA * source_all / dfine
    for i in range(S0 - 1):
        lam = sweep(lam, source_all, fine, dfine)
    b_mid = mean_four(source_all - operate(lam, fine))
    e_mid = OMEGA * b_mid / dmid
    for i in range(S1 - 1):
        e_mid = sweep(e_mid, b_mid, middle, dmid)
    b_low = mean_four(b_mid - operate(e_mid, middle))
    e_low = OMEGA * b_low / dcoarse
    for i in range(S2 - 1):
        e_low = sweep(e_low, b_low, coarse, dcoarse)
    e_mid = e_mid + prolong(e_low)
    for i in range(S1):
        e_mid = sweep(e_mid, b_mid, middle, dmid)
    lam = lam + prolong(e_mid)
    for i in range(S0):
        lam = sweep(lam, source_all, fine, dfine)
    own = lax.dynamic_slice_in_dim(lam, lax.axis_index("gx") * cols, cols, 2)
    column = jnp.sum(wsq[:, None, None] * forward_velocity * own, axis=0)
    summed = lax.psum(column, "gz")
    terms = -ground_fric * summed
    gradient = lax.dynamic_slice_in_dim(terms, gz * half_cols, half_cols, 1)
    return (own, gradient)


def solution(mesh):
    placed = (
        P("gz", "gy", "gx"),
        P("gz", "gy", "gx"),
        P("gz", "gy", "gx"),
        P("gy", "gx"),
        P("gy", "gx"),
        P("gy", "gx"),
    )
    return jax.shard_map(
        body,
        mesh=mesh,
        in_specs=placed,
        out_specs=(P("gz", "gy", "gx"), P("gy", ("gx", "gz"))),
        check_vma=False,
    )
```

```python
import jax
import jax.numpy as jnp
from jax import lax
from jax.sharding import PartitionSpec as P

S0 = 4
S1 = 4
S2 = 8


OMEGA = 0.8
VERT = 4.0
HI = lax.Precision.HIGHEST
FINE_HALO = 12
MID_HALO = 6
POST_HALO = 4


def layer_halos(u):
    count = lax.axis_size("gz")
    head = u[:1]
    tail = u[-1:]
    if count == 2:
        first = lax.axis_index("gz") == 0
        got = lax.ppermute(jnp.where(first, tail, head), "gz", [(0, 1), (1, 0)])
        zero = jnp.zeros_like(got)
        return jnp.where(first, zero, got), jnp.where(first, got, zero)
    lo = lax.ppermute(tail, "gz", [(i, i + 1) for i in range(count - 1)])
    hi = lax.ppermute(head, "gz", [(i + 1, i) for i in range(count - 1)])
    return lo, hi


def extend_rows(a, h):
    count = lax.axis_size("gy")
    lo = lax.ppermute(a[:, -h:], "gy", [(i, i + 1) for i in range(count - 1)])
    hi = lax.ppermute(a[:, :h], "gy", [(i + 1, i) for i in range(count - 1)])
    return jnp.concatenate([lo, a, hi], axis=1)


def crop(a, h_from, h_to):
    cut = h_from - h_to
    return a[:, cut : a.shape[1] - cut]


def row_mask(own_rows, h):
    g = lax.axis_index("gy") * own_rows - h + lax.broadcasted_iota(jnp.int32, (1, own_rows + 2 * h, 1), 1)
    return (g >= 0) & (g < own_rows * lax.axis_size("gy"))


def neighbours(u):
    zlo, zhi = layer_halos(u)
    zero_row = jnp.zeros_like(u[:, :1])
    zero_col = jnp.zeros_like(u[:, :, :1])
    zm = jnp.concatenate([zlo, u[:-1]], axis=0)
    zp = jnp.concatenate([u[1:], zhi], axis=0)
    ym = jnp.concatenate([zero_row, u[:, :-1]], axis=1)
    yp = jnp.concatenate([u[:, 1:], zero_row], axis=1)
    xm = jnp.concatenate([zero_col, u[:, :, :-1]], axis=2)
    xp = jnp.concatenate([u[:, :, 1:], zero_col], axis=2)
    return zm, zp, ym, yp, xm, xp


def face_set(eta):
    zm, zp, ym, yp, xm, xp = neighbours(eta)
    zlo = VERT * (0.5 * (eta + zm))
    zhi = VERT * (0.5 * (eta + zp))
    ylo = 0.5 * (eta + ym)
    yhi = 0.5 * (eta + yp)
    xlo = 0.5 * (eta + xm)
    xhi = 0.5 * (eta + xp)
    return (zlo, zhi, ylo, yhi, xlo, xhi)


def operate(u, coef):
    zlo, zhi, ylo, yhi, xlo, xhi, extra = coef
    zm, zp, ym, yp, xm, xp = neighbours(u)
    out = zlo * (u - zm) + zhi * (u - zp)
    out = out + ylo * (u - ym) + yhi * (u - yp)
    out = out + xlo * (u - xm) + xhi * (u - xp)
    return out + extra * u


def diagonal(coef):
    zlo, zhi, ylo, yhi, xlo, xhi, extra = coef
    return zlo + zhi + ylo + yhi + xlo + xhi + extra


def pick(n, parity):
    src = lax.broadcasted_iota(jnp.int32, (n, n // 2), 0)
    dst = lax.broadcasted_iota(jnp.int32, (n, n // 2), 1)
    return (src == 2 * dst + parity).astype(jnp.float32)


def cols(a, parity):
    return jnp.dot(a, pick(a.shape[-1], parity), precision=HI)


def rows(a, parity):
    return jnp.einsum("yr,zyx->zrx", pick(a.shape[1], parity), a, precision=HI)


def mean_four(a):
    r0 = rows(a, 0)
    r1 = rows(a, 1)
    return 0.25 * (cols(r0, 0) + cols(r1, 0) + cols(r0, 1) + cols(r1, 1))


def coarsen(coef):
    zlo, zhi, ylo, yhi, xlo, xhi, extra = coef
    cxlo = 0.125 * cols(rows(xlo, 0) + rows(xlo, 1), 0)
    cxhi = 0.125 * cols(rows(xhi, 0) + rows(xhi, 1), 1)
    ylo0 = rows(ylo, 0)
    yhi1 = rows(yhi, 1)
    cylo = 0.125 * (cols(ylo0, 0) + cols(ylo0, 1))
    cyhi = 0.125 * (cols(yhi1, 0) + cols(yhi1, 1))
    return (mean_four(zlo), mean_four(zhi), cylo, cyhi, cxlo, cxhi, mean_four(extra))


def spread(n):
    src = lax.broadcasted_iota(jnp.int32, (n, 2 * n), 0)
    dst = lax.broadcasted_iota(jnp.int32, (n, 2 * n), 1)
    return (src == dst // 2).astype(jnp.float32)


def prolong(field):
    wide = jnp.dot(field, spread(field.shape[-1]), precision=HI)
    return jnp.einsum("ry,zrx->zyx", spread(field.shape[1]), wide, precision=HI)


def sweep(field, rhs, coef, diag, inside):
    new = field + OMEGA * (rhs - operate(field, coef)) / diag
    return jnp.where(inside, new, 0.0)


def smooth(field, rhs, coef, diag, inside, count):
    for i in range(count):
        field = sweep(field, rhs, coef, diag, inside)
    return field


def crop_all(arrs, h_from, h_to):
    return tuple(crop(a, h_from, h_to) for a in arrs)


def body_wide(viscosity, adjoint_source, forward_velocity, friction, ice_mask, grounded_mask):
    layers = viscosity.shape[0]
    own_rows = viscosity.shape[1]
    mid_rows = own_rows // 2
    cols_own = viscosity.shape[2]
    half_cols = cols_own // 2
    gz = lax.axis_index("gz")
    gy = lax.axis_index("gy")
    total_layers = layers * lax.axis_size("gz")
    layer = (gz * layers + jnp.arange(layers)).astype(jnp.float32)
    profile = (jnp.float32(total_layers) - layer) / jnp.float32(total_layers)
    wsq = profile * profile
    icef = ice_mask.astype(jnp.float32)
    groundf = grounded_mask.astype(jnp.float32)
    base = 0.05 + 2.0 * (1.0 - icef)
    ground_fric = groundf * friction
    stacked = jnp.concatenate([viscosity, adjoint_source, base[None], ground_fric[None]], axis=0)
    gathered = lax.all_gather(stacked, "gx", axis=0, tiled=False)
    gathered = jnp.concatenate([gathered[i] for i in range(gathered.shape[0])], axis=2)
    hv = FINE_HALO + 1
    ext = extend_rows(gathered, hv)
    visc_e = ext[:layers]
    src_e = crop(ext[layers : 2 * layers], hv, FINE_HALO)
    base_e = crop(ext[2 * layers : 2 * layers + 1], hv, FINE_HALO)[0]
    gfr_e = crop(ext[2 * layers + 1 : 2 * layers + 2], hv, FINE_HALO)[0]
    extra = base_e[None, :, :] + gfr_e[None, :, :] * wsq[:, None, None]
    fine = crop_all(face_set(visc_e), hv, FINE_HALO) + (extra,)
    dfine = diagonal(fine)
    middle = coarsen(fine)
    dmid = diagonal(middle)
    coarse_own = coarsen(crop_all(middle, FINE_HALO // 2, 0))
    coarse_all = lax.all_gather(jnp.concatenate(coarse_own, axis=0), "gy", axis=1, tiled=True)
    coarse = tuple(coarse_all[i * layers : (i + 1) * layers] for i in range(7))
    dcoarse = diagonal(coarse)
    in_fine = row_mask(own_rows, FINE_HALO)
    in_mid = row_mask(mid_rows, FINE_HALO // 2)

    lam = jnp.where(in_fine, OMEGA * src_e / dfine, 0.0)
    lam = smooth(lam, src_e, fine, dfine, in_fine, S0 - 1)
    b_mid = mean_four(src_e - operate(lam, fine))
    e_mid = jnp.where(in_mid, OMEGA * b_mid / dmid, 0.0)
    e_mid = smooth(e_mid, b_mid, middle, dmid, in_mid, S1 - 1)
    hm = FINE_HALO // 2
    res_mid = crop(b_mid - operate(e_mid, middle), hm, 0)
    b_low = lax.all_gather(mean_four(res_mid), "gy", axis=1, tiled=True)
    e_low = OMEGA * b_low / dcoarse
    ones = jnp.ones((1, b_low.shape[1], 1), dtype=bool)
    e_low = smooth(e_low, b_low, coarse, dcoarse, ones, S2 - 1)

    pair = jnp.concatenate([crop(e_mid, hm, 0), crop(b_mid, hm, 0)], axis=0)
    pair = extend_rows(pair, MID_HALO)
    e_mid = pair[:layers]
    b_mid = pair[layers:]
    low_rows = own_rows // 4
    ch = MID_HALO // 2
    padded = jnp.pad(e_low, ((0, 0), (ch, ch), (0, 0)))
    e_near = lax.dynamic_slice_in_dim(padded, gy * low_rows, low_rows + 2 * ch, 1)
    e_mid = e_mid + prolong(e_near)
    middle_p = crop_all(middle, hm, MID_HALO)
    dmid_p = crop(dmid, hm, MID_HALO)
    in_mid_p = row_mask(mid_rows, MID_HALO)
    e_mid = smooth(e_mid, b_mid, middle_p, dmid_p, in_mid_p, S1)

    lam = crop(lam, FINE_HALO, POST_HALO) + prolong(crop(e_mid, MID_HALO, POST_HALO // 2))
    fine_p = crop_all(fine, FINE_HALO, POST_HALO)
    dfine_p = crop(dfine, FINE_HALO, POST_HALO)
    src_p = crop(src_e, FINE_HALO, POST_HALO)
    in_fine_p = row_mask(own_rows, POST_HALO)
    lam = smooth(lam, src_p, fine_p, dfine_p, in_fine_p, S0)
    lam = crop(lam, POST_HALO, 0)

    own = lax.dynamic_slice_in_dim(lam, lax.axis_index("gx") * cols_own, cols_own, 2)
    column = jnp.sum(wsq[:, None, None] * forward_velocity * own, axis=0)
    summed = lax.psum(column, "gz")
    terms = -ground_fric * summed
    gradient = lax.dynamic_slice_in_dim(terms, gz * half_cols, half_cols, 1)
    return (own, gradient)


def n_layer_halos(u):
    count = lax.axis_size("gz")
    head = u[:1]
    tail = u[-1:]
    if count == 2:
        first = lax.axis_index("gz") == 0
        got = lax.ppermute(jnp.where(first, tail, head), "gz", [(0, 1), (1, 0)])
        zero = jnp.zeros_like(got)
        return jnp.where(first, zero, got), jnp.where(first, got, zero)
    lo = lax.ppermute(tail, "gz", [(i, i + 1) for i in range(count - 1)])
    hi = lax.ppermute(head, "gz", [(i + 1, i) for i in range(count - 1)])
    return lo, hi


def n_row_halos(u):
    count = lax.axis_size("gy")
    lo = lax.ppermute(u[:, -1:], "gy", [(i, i + 1) for i in range(count - 1)])
    hi = lax.ppermute(u[:, :1], "gy", [(i + 1, i) for i in range(count - 1)])
    return lo, hi


def n_neighbours(u):
    zlo, zhi = n_layer_halos(u)
    ylo, yhi = n_row_halos(u)
    zero = jnp.zeros_like(u[:, :, :1])
    zm = jnp.concatenate([zlo, u[:-1]], axis=0)
    zp = jnp.concatenate([u[1:], zhi], axis=0)
    ym = jnp.concatenate([ylo, u[:, :-1]], axis=1)
    yp = jnp.concatenate([u[:, 1:], yhi], axis=1)
    xm = jnp.concatenate([zero, u[:, :, :-1]], axis=2)
    xp = jnp.concatenate([u[:, :, 1:], zero], axis=2)
    return zm, zp, ym, yp, xm, xp


def n_face_set(eta):
    zm, zp, ym, yp, xm, xp = n_neighbours(eta)
    zlo = VERT * (0.5 * (eta + zm))
    zhi = VERT * (0.5 * (eta + zp))
    ylo = 0.5 * (eta + ym)
    yhi = 0.5 * (eta + yp)
    xlo = 0.5 * (eta + xm)
    xhi = 0.5 * (eta + xp)
    return (zlo, zhi, ylo, yhi, xlo, xhi)


def n_operate(u, coef):
    zlo, zhi, ylo, yhi, xlo, xhi, extra = coef
    zm, zp, ym, yp, xm, xp = n_neighbours(u)
    out = zlo * (u - zm) + zhi * (u - zp)
    out = out + ylo * (u - ym) + yhi * (u - yp)
    out = out + xlo * (u - xm) + xhi * (u - xp)
    return out + extra * u


def n_diagonal(coef):
    zlo, zhi, ylo, yhi, xlo, xhi, extra = coef
    return zlo + zhi + ylo + yhi + xlo + xhi + extra


def n_pick_matrix(cols):
    half = cols // 2
    src = lax.broadcasted_iota(jnp.int32, (cols, cols), 0)
    dst = lax.broadcasted_iota(jnp.int32, (cols, cols), 1)
    want = jnp.where(dst < half, 2 * dst, 2 * (dst - half) + 1)
    return (src == want).astype(jnp.float32)


def n_split_x(a):
    cols = a.shape[-1]
    both = jnp.dot(a, n_pick_matrix(cols), precision=HI)
    return both[..., : cols // 2], both[..., cols // 2 :]


def n_mean_four(a):
    e0, o0 = n_split_x(a[:, 0::2])
    e1, o1 = n_split_x(a[:, 1::2])
    return 0.25 * (e0 + e1 + o0 + o1)


def n_coarsen(coef):
    zlo, zhi, ylo, yhi, xlo, xhi, extra = coef
    xlo_e, _ = n_split_x(xlo[:, 0::2] + xlo[:, 1::2])
    _, xhi_o = n_split_x(xhi[:, 0::2] + xhi[:, 1::2])
    ylo_e, ylo_o = n_split_x(ylo[:, 0::2])
    yhi_e, yhi_o = n_split_x(yhi[:, 1::2])
    cxlo = 0.125 * xlo_e
    cxhi = 0.125 * xhi_o
    cylo = 0.125 * (ylo_e + ylo_o)
    cyhi = 0.125 * (yhi_e + yhi_o)
    return (n_mean_four(zlo), n_mean_four(zhi), cylo, cyhi, cxlo, cxhi, n_mean_four(extra))


def n_prolong(field):
    cols = field.shape[-1]
    src = lax.broadcasted_iota(jnp.int32, (cols, 2 * cols), 0)
    dst = lax.broadcasted_iota(jnp.int32, (cols, 2 * cols), 1)
    spread = (src == dst // 2).astype(jnp.float32)
    wide = jnp.dot(field, spread, precision=HI)
    return jnp.repeat(wide, 2, axis=1)


def n_sweep(field, rhs, coef, diag):
    return field + OMEGA * (rhs - n_operate(field, coef)) / diag


def n_body(viscosity, adjoint_source, forward_velocity, friction, ice_mask, grounded_mask):
    layers = viscosity.shape[0]
    cols = viscosity.shape[2]
    half_cols = cols // 2
    gz = lax.axis_index("gz")
    total_layers = layers * lax.axis_size("gz")
    layer = (gz * layers + jnp.arange(layers)).astype(jnp.float32)
    profile = (jnp.float32(total_layers) - layer) / jnp.float32(total_layers)
    wsq = profile * profile
    icef = ice_mask.astype(jnp.float32)
    groundf = grounded_mask.astype(jnp.float32)
    base = 0.05 + 2.0 * (1.0 - icef)
    ground_fric = groundf * friction
    stacked = jnp.concatenate([viscosity, adjoint_source, base[None], ground_fric[None]], axis=0)
    gathered = lax.all_gather(stacked, "gx", axis=0, tiled=False)
    count_x = gathered.shape[0]
    gathered = jnp.concatenate([gathered[i] for i in range(count_x)], axis=2)
    visc_all = gathered[:layers]
    source_all = gathered[layers : 2 * layers]
    base_all = gathered[2 * layers]
    gfr_all = gathered[2 * layers + 1]
    extra = base_all[None, :, :] + gfr_all[None, :, :] * wsq[:, None, None]
    fine = n_face_set(visc_all) + (extra,)
    dfine = n_diagonal(fine)
    middle = n_coarsen(fine)
    dmid = n_diagonal(middle)
    coarse = n_coarsen(middle)
    dcoarse = n_diagonal(coarse)
    lam = OMEGA * source_all / dfine
    for i in range(S0 - 1):
        lam = n_sweep(lam, source_all, fine, dfine)
    b_mid = n_mean_four(source_all - n_operate(lam, fine))
    e_mid = OMEGA * b_mid / dmid
    for i in range(S1 - 1):
        e_mid = n_sweep(e_mid, b_mid, middle, dmid)
    b_low = n_mean_four(b_mid - n_operate(e_mid, middle))
    e_low = OMEGA * b_low / dcoarse
    for i in range(S2 - 1):
        e_low = n_sweep(e_low, b_low, coarse, dcoarse)
    e_mid = e_mid + n_prolong(e_low)
    for i in range(S1):
        e_mid = n_sweep(e_mid, b_mid, middle, dmid)
    lam = lam + n_prolong(e_mid)
    for i in range(S0):
        lam = n_sweep(lam, source_all, fine, dfine)
    own = lax.dynamic_slice_in_dim(lam, lax.axis_index("gx") * cols, cols, 2)
    column = jnp.sum(wsq[:, None, None] * forward_velocity * own, axis=0)
    summed = lax.psum(column, "gz")
    terms = -ground_fric * summed
    gradient = lax.dynamic_slice_in_dim(terms, gz * half_cols, half_cols, 1)
    return (own, gradient)


def body(viscosity, *rest):
    layers, own_rows, cols_own = viscosity.shape
    cols_all = cols_own * lax.axis_size("gx")
    wide_bytes = 4 * layers * (own_rows + 2 * FINE_HALO + 2) * cols_all
    if FINE_HALO + 1 <= own_rows and MID_HALO <= own_rows // 2 and 20 * wide_bytes <= 40 * 2**20:
        return body_wide(viscosity, *rest)
    return n_body(viscosity, *rest)


def solution(mesh):
    placed = (
        P("gz", "gy", "gx"),
        P("gz", "gy", "gx"),
        P("gz", "gy", "gx"),
        P("gy", "gx"),
        P("gy", "gx"),
        P("gy", "gx"),
    )
    return jax.shard_map(
        body,
        mesh=mesh,
        in_specs=placed,
        out_specs=(P("gz", "gy", "gx"), P("gy", ("gx", "gz"))),
        check_vma=False,
    )
```

```python
import jax
import jax.numpy as jnp
from jax import lax
from jax.sharding import PartitionSpec as P

S0 = 4
S1 = 4
S2 = 8


OMEGA = 0.8
VERT = 4.0
HI = lax.Precision.HIGHEST
FINE_HALO = 12
MID_HALO = 6
POST_HALO = 4


def layer_halos(u):
    count = lax.axis_size("gz")
    head = u[:1]
    tail = u[-1:]
    if count == 2:
        first = lax.axis_index("gz") == 0
        got = lax.ppermute(jnp.where(first, tail, head), "gz", [(0, 1), (1, 0)])
        zero = jnp.zeros_like(got)
        return jnp.where(first, zero, got), jnp.where(first, got, zero)
    lo = lax.ppermute(tail, "gz", [(i, i + 1) for i in range(count - 1)])
    hi = lax.ppermute(head, "gz", [(i + 1, i) for i in range(count - 1)])
    return lo, hi


def extend_rows(a, h):
    count = lax.axis_size("gy")
    lo = lax.ppermute(a[:, -h:], "gy", [(i, i + 1) for i in range(count - 1)])
    hi = lax.ppermute(a[:, :h], "gy", [(i + 1, i) for i in range(count - 1)])
    return jnp.concatenate([lo, a, hi], axis=1)


def gather_blocks(a, axis):
    count = lax.axis_size(axis)
    got = [a]
    for s in range(1, count):
        got.append(lax.ppermute(a, axis, [(i, (i + s) % count) for i in range(count)]))
    rev = jnp.stack(got[::-1], axis=0)
    return jnp.roll(rev, lax.axis_index(axis) + 1, axis=0)


def crop(a, h_from, h_to):
    cut = h_from - h_to
    return a[:, cut : a.shape[1] - cut]


def row_mask(own_rows, h):
    g = lax.axis_index("gy") * own_rows - h + lax.broadcasted_iota(jnp.int32, (1, own_rows + 2 * h, 1), 1)
    return (g >= 0) & (g < own_rows * lax.axis_size("gy"))


def neighbours(u):
    zlo, zhi = layer_halos(u)
    zero_row = jnp.zeros_like(u[:, :1])
    zero_col = jnp.zeros_like(u[:, :, :1])
    zm = jnp.concatenate([zlo, u[:-1]], axis=0)
    zp = jnp.concatenate([u[1:], zhi], axis=0)
    ym = jnp.concatenate([zero_row, u[:, :-1]], axis=1)
    yp = jnp.concatenate([u[:, 1:], zero_row], axis=1)
    xm = jnp.concatenate([zero_col, u[:, :, :-1]], axis=2)
    xp = jnp.concatenate([u[:, :, 1:], zero_col], axis=2)
    return zm, zp, ym, yp, xm, xp


def face_set(eta):
    zm, zp, ym, yp, xm, xp = neighbours(eta)
    zlo = VERT * (0.5 * (eta + zm))
    zhi = VERT * (0.5 * (eta + zp))
    ylo = 0.5 * (eta + ym)
    yhi = 0.5 * (eta + yp)
    xlo = 0.5 * (eta + xm)
    xhi = 0.5 * (eta + xp)
    return (zlo, zhi, ylo, yhi, xlo, xhi)


def operate(u, coef):
    zlo, zhi, ylo, yhi, xlo, xhi, extra = coef
    zm, zp, ym, yp, xm, xp = neighbours(u)
    out = zlo * (u - zm) + zhi * (u - zp)
    out = out + ylo * (u - ym) + yhi * (u - yp)
    out = out + xlo * (u - xm) + xhi * (u - xp)
    return out + extra * u


def diagonal(coef):
    zlo, zhi, ylo, yhi, xlo, xhi, extra = coef
    return zlo + zhi + ylo + yhi + xlo + xhi + extra


def pick(n, parity):
    src = lax.broadcasted_iota(jnp.int32, (n, n // 2), 0)
    dst = lax.broadcasted_iota(jnp.int32, (n, n // 2), 1)
    return (src == 2 * dst + parity).astype(jnp.float32)


def cols(a, parity):
    return jnp.dot(a, pick(a.shape[-1], parity), precision=HI)


def rows(a, parity):
    return jnp.einsum("yr,zyx->zrx", pick(a.shape[1], parity), a, precision=HI)


def mean_four(a):
    r0 = rows(a, 0)
    r1 = rows(a, 1)
    return 0.25 * (cols(r0, 0) + cols(r1, 0) + cols(r0, 1) + cols(r1, 1))


def coarsen(coef):
    zlo, zhi, ylo, yhi, xlo, xhi, extra = coef
    cxlo = 0.125 * cols(rows(xlo, 0) + rows(xlo, 1), 0)
    cxhi = 0.125 * cols(rows(xhi, 0) + rows(xhi, 1), 1)
    ylo0 = rows(ylo, 0)
    yhi1 = rows(yhi, 1)
    cylo = 0.125 * (cols(ylo0, 0) + cols(ylo0, 1))
    cyhi = 0.125 * (cols(yhi1, 0) + cols(yhi1, 1))
    return (mean_four(zlo), mean_four(zhi), cylo, cyhi, cxlo, cxhi, mean_four(extra))


def spread(n):
    src = lax.broadcasted_iota(jnp.int32, (n, 2 * n), 0)
    dst = lax.broadcasted_iota(jnp.int32, (n, 2 * n), 1)
    return (src == dst // 2).astype(jnp.float32)


def prolong(field):
    wide = jnp.dot(field, spread(field.shape[-1]), precision=HI)
    return jnp.einsum("ry,zrx->zyx", spread(field.shape[1]), wide, precision=HI)


def sweep(field, rhs, coef, diag, inside):
    new = field + OMEGA * (rhs - operate(field, coef)) / diag
    return jnp.where(inside, new, 0.0)


def smooth(field, rhs, coef, diag, inside, count):
    for i in range(count):
        field = sweep(field, rhs, coef, diag, inside)
    return field


def crop_all(arrs, h_from, h_to):
    return tuple(crop(a, h_from, h_to) for a in arrs)


def body_wide(viscosity, adjoint_source, forward_velocity, friction, ice_mask, grounded_mask):
    layers = viscosity.shape[0]
    own_rows = viscosity.shape[1]
    mid_rows = own_rows // 2
    cols_own = viscosity.shape[2]
    half_cols = cols_own // 2
    gz = lax.axis_index("gz")
    gy = lax.axis_index("gy")
    total_layers = layers * lax.axis_size("gz")
    layer = (gz * layers + jnp.arange(layers)).astype(jnp.float32)
    profile = (jnp.float32(total_layers) - layer) / jnp.float32(total_layers)
    wsq = profile * profile
    icef = ice_mask.astype(jnp.float32)
    groundf = grounded_mask.astype(jnp.float32)
    base = 0.05 + 2.0 * (1.0 - icef)
    ground_fric = groundf * friction
    stacked = jnp.concatenate([viscosity, adjoint_source, base[None], ground_fric[None]], axis=0)
    gathered = gather_blocks(stacked, "gx")
    gathered = jnp.concatenate([gathered[i] for i in range(gathered.shape[0])], axis=2)
    hv = FINE_HALO + 1
    ext = extend_rows(gathered, hv)
    visc_e = ext[:layers]
    src_e = crop(ext[layers : 2 * layers], hv, FINE_HALO)
    base_e = crop(ext[2 * layers : 2 * layers + 1], hv, FINE_HALO)[0]
    gfr_e = crop(ext[2 * layers + 1 : 2 * layers + 2], hv, FINE_HALO)[0]
    extra = base_e[None, :, :] + gfr_e[None, :, :] * wsq[:, None, None]
    fine = crop_all(face_set(visc_e), hv, FINE_HALO) + (extra,)
    dfine = diagonal(fine)
    middle = coarsen(fine)
    dmid = diagonal(middle)
    coarse_own = coarsen(crop_all(middle, FINE_HALO // 2, 0))
    coarse_all = gather_blocks(jnp.concatenate(coarse_own, axis=0), "gy")
    coarse_all = jnp.concatenate([coarse_all[i] for i in range(coarse_all.shape[0])], axis=1)
    coarse = tuple(coarse_all[i * layers : (i + 1) * layers] for i in range(7))
    dcoarse = diagonal(coarse)
    in_fine = row_mask(own_rows, FINE_HALO)
    in_mid = row_mask(mid_rows, FINE_HALO // 2)

    lam = jnp.where(in_fine, OMEGA * src_e / dfine, 0.0)
    lam = smooth(lam, src_e, fine, dfine, in_fine, S0 - 1)
    b_mid = mean_four(src_e - operate(lam, fine))
    e_mid = jnp.where(in_mid, OMEGA * b_mid / dmid, 0.0)
    e_mid = smooth(e_mid, b_mid, middle, dmid, in_mid, S1 - 1)
    hm = FINE_HALO // 2
    res_mid = crop(b_mid - operate(e_mid, middle), hm, 0)
    b_low = gather_blocks(mean_four(res_mid), "gy")
    b_low = jnp.concatenate([b_low[i] for i in range(b_low.shape[0])], axis=1)
    e_low = OMEGA * b_low / dcoarse
    ones = jnp.ones((1, b_low.shape[1], 1), dtype=bool)
    e_low = smooth(e_low, b_low, coarse, dcoarse, ones, S2 - 1)

    pair = jnp.concatenate([crop(e_mid, hm, 0), crop(b_mid, hm, 0)], axis=0)
    pair = extend_rows(pair, MID_HALO)
    e_mid = pair[:layers]
    b_mid = pair[layers:]
    low_rows = own_rows // 4
    ch = MID_HALO // 2
    padded = jnp.pad(e_low, ((0, 0), (ch, ch), (0, 0)))
    e_near = lax.dynamic_slice_in_dim(padded, gy * low_rows, low_rows + 2 * ch, 1)
    e_mid = e_mid + prolong(e_near)
    middle_p = crop_all(middle, hm, MID_HALO)
    dmid_p = crop(dmid, hm, MID_HALO)
    in_mid_p = row_mask(mid_rows, MID_HALO)
    e_mid = smooth(e_mid, b_mid, middle_p, dmid_p, in_mid_p, S1)

    lam = crop(lam, FINE_HALO, POST_HALO) + prolong(crop(e_mid, MID_HALO, POST_HALO // 2))
    fine_p = crop_all(fine, FINE_HALO, POST_HALO)
    dfine_p = crop(dfine, FINE_HALO, POST_HALO)
    src_p = crop(src_e, FINE_HALO, POST_HALO)
    in_fine_p = row_mask(own_rows, POST_HALO)
    lam = smooth(lam, src_p, fine_p, dfine_p, in_fine_p, S0)
    lam = crop(lam, POST_HALO, 0)

    own = lax.dynamic_slice_in_dim(lam, lax.axis_index("gx") * cols_own, cols_own, 2)
    column = jnp.sum(wsq[:, None, None] * forward_velocity * own, axis=0)
    summed = lax.psum(column, "gz")
    terms = -ground_fric * summed
    gradient = lax.dynamic_slice_in_dim(terms, gz * half_cols, half_cols, 1)
    return (own, gradient)


def n_layer_halos(u):
    count = lax.axis_size("gz")
    head = u[:1]
    tail = u[-1:]
    if count == 2:
        first = lax.axis_index("gz") == 0
        got = lax.ppermute(jnp.where(first, tail, head), "gz", [(0, 1), (1, 0)])
        zero = jnp.zeros_like(got)
        return jnp.where(first, zero, got), jnp.where(first, got, zero)
    lo = lax.ppermute(tail, "gz", [(i, i + 1) for i in range(count - 1)])
    hi = lax.ppermute(head, "gz", [(i + 1, i) for i in range(count - 1)])
    return lo, hi


def n_row_halos(u):
    count = lax.axis_size("gy")
    lo = lax.ppermute(u[:, -1:], "gy", [(i, i + 1) for i in range(count - 1)])
    hi = lax.ppermute(u[:, :1], "gy", [(i + 1, i) for i in range(count - 1)])
    return lo, hi


def n_neighbours(u):
    zlo, zhi = n_layer_halos(u)
    ylo, yhi = n_row_halos(u)
    zero = jnp.zeros_like(u[:, :, :1])
    zm = jnp.concatenate([zlo, u[:-1]], axis=0)
    zp = jnp.concatenate([u[1:], zhi], axis=0)
    ym = jnp.concatenate([ylo, u[:, :-1]], axis=1)
    yp = jnp.concatenate([u[:, 1:], yhi], axis=1)
    xm = jnp.concatenate([zero, u[:, :, :-1]], axis=2)
    xp = jnp.concatenate([u[:, :, 1:], zero], axis=2)
    return zm, zp, ym, yp, xm, xp


def n_face_set(eta):
    zm, zp, ym, yp, xm, xp = n_neighbours(eta)
    zlo = VERT * (0.5 * (eta + zm))
    zhi = VERT * (0.5 * (eta + zp))
    ylo = 0.5 * (eta + ym)
    yhi = 0.5 * (eta + yp)
    xlo = 0.5 * (eta + xm)
    xhi = 0.5 * (eta + xp)
    return (zlo, zhi, ylo, yhi, xlo, xhi)


def n_operate(u, coef):
    zlo, zhi, ylo, yhi, xlo, xhi, extra = coef
    zm, zp, ym, yp, xm, xp = n_neighbours(u)
    out = zlo * (u - zm) + zhi * (u - zp)
    out = out + ylo * (u - ym) + yhi * (u - yp)
    out = out + xlo * (u - xm) + xhi * (u - xp)
    return out + extra * u


def n_diagonal(coef):
    zlo, zhi, ylo, yhi, xlo, xhi, extra = coef
    return zlo + zhi + ylo + yhi + xlo + xhi + extra


def n_pick_matrix(cols):
    half = cols // 2
    src = lax.broadcasted_iota(jnp.int32, (cols, cols), 0)
    dst = lax.broadcasted_iota(jnp.int32, (cols, cols), 1)
    want = jnp.where(dst < half, 2 * dst, 2 * (dst - half) + 1)
    return (src == want).astype(jnp.float32)


def n_split_x(a):
    cols = a.shape[-1]
    both = jnp.dot(a, n_pick_matrix(cols), precision=HI)
    return both[..., : cols // 2], both[..., cols // 2 :]


def n_mean_four(a):
    e0, o0 = n_split_x(a[:, 0::2])
    e1, o1 = n_split_x(a[:, 1::2])
    return 0.25 * (e0 + e1 + o0 + o1)


def n_coarsen(coef):
    zlo, zhi, ylo, yhi, xlo, xhi, extra = coef
    xlo_e, _ = n_split_x(xlo[:, 0::2] + xlo[:, 1::2])
    _, xhi_o = n_split_x(xhi[:, 0::2] + xhi[:, 1::2])
    ylo_e, ylo_o = n_split_x(ylo[:, 0::2])
    yhi_e, yhi_o = n_split_x(yhi[:, 1::2])
    cxlo = 0.125 * xlo_e
    cxhi = 0.125 * xhi_o
    cylo = 0.125 * (ylo_e + ylo_o)
    cyhi = 0.125 * (yhi_e + yhi_o)
    return (n_mean_four(zlo), n_mean_four(zhi), cylo, cyhi, cxlo, cxhi, n_mean_four(extra))


def n_prolong(field):
    cols = field.shape[-1]
    src = lax.broadcasted_iota(jnp.int32, (cols, 2 * cols), 0)
    dst = lax.broadcasted_iota(jnp.int32, (cols, 2 * cols), 1)
    spread = (src == dst // 2).astype(jnp.float32)
    wide = jnp.dot(field, spread, precision=HI)
    return jnp.repeat(wide, 2, axis=1)


def n_sweep(field, rhs, coef, diag):
    return field + OMEGA * (rhs - n_operate(field, coef)) / diag


def n_body(viscosity, adjoint_source, forward_velocity, friction, ice_mask, grounded_mask):
    layers = viscosity.shape[0]
    cols = viscosity.shape[2]
    half_cols = cols // 2
    gz = lax.axis_index("gz")
    total_layers = layers * lax.axis_size("gz")
    layer = (gz * layers + jnp.arange(layers)).astype(jnp.float32)
    profile = (jnp.float32(total_layers) - layer) / jnp.float32(total_layers)
    wsq = profile * profile
    icef = ice_mask.astype(jnp.float32)
    groundf = grounded_mask.astype(jnp.float32)
    base = 0.05 + 2.0 * (1.0 - icef)
    ground_fric = groundf * friction
    stacked = jnp.concatenate([viscosity, adjoint_source, base[None], ground_fric[None]], axis=0)
    gathered = lax.all_gather(stacked, "gx", axis=0, tiled=False)
    count_x = gathered.shape[0]
    gathered = jnp.concatenate([gathered[i] for i in range(count_x)], axis=2)
    visc_all = gathered[:layers]
    source_all = gathered[layers : 2 * layers]
    base_all = gathered[2 * layers]
    gfr_all = gathered[2 * layers + 1]
    extra = base_all[None, :, :] + gfr_all[None, :, :] * wsq[:, None, None]
    fine = n_face_set(visc_all) + (extra,)
    dfine = n_diagonal(fine)
    middle = n_coarsen(fine)
    dmid = n_diagonal(middle)
    coarse = n_coarsen(middle)
    dcoarse = n_diagonal(coarse)
    lam = OMEGA * source_all / dfine
    for i in range(S0 - 1):
        lam = n_sweep(lam, source_all, fine, dfine)
    b_mid = n_mean_four(source_all - n_operate(lam, fine))
    e_mid = OMEGA * b_mid / dmid
    for i in range(S1 - 1):
        e_mid = n_sweep(e_mid, b_mid, middle, dmid)
    b_low = n_mean_four(b_mid - n_operate(e_mid, middle))
    e_low = OMEGA * b_low / dcoarse
    for i in range(S2 - 1):
        e_low = n_sweep(e_low, b_low, coarse, dcoarse)
    e_mid = e_mid + n_prolong(e_low)
    for i in range(S1):
        e_mid = n_sweep(e_mid, b_mid, middle, dmid)
    lam = lam + n_prolong(e_mid)
    for i in range(S0):
        lam = n_sweep(lam, source_all, fine, dfine)
    own = lax.dynamic_slice_in_dim(lam, lax.axis_index("gx") * cols, cols, 2)
    column = jnp.sum(wsq[:, None, None] * forward_velocity * own, axis=0)
    summed = lax.psum(column, "gz")
    terms = -ground_fric * summed
    gradient = lax.dynamic_slice_in_dim(terms, gz * half_cols, half_cols, 1)
    return (own, gradient)


def body(viscosity, *rest):
    layers, own_rows, cols_own = viscosity.shape
    cols_all = cols_own * lax.axis_size("gx")
    wide_bytes = 4 * layers * (own_rows + 2 * FINE_HALO + 2) * cols_all
    if FINE_HALO + 1 <= own_rows and MID_HALO <= own_rows // 2 and 20 * wide_bytes <= 40 * 2**20 and lax.axis_size("gy") <= 8:
        return body_wide(viscosity, *rest)
    return n_body(viscosity, *rest)


def solution(mesh):
    placed = (
        P("gz", "gy", "gx"),
        P("gz", "gy", "gx"),
        P("gz", "gy", "gx"),
        P("gy", "gx"),
        P("gy", "gx"),
        P("gy", "gx"),
    )
    return jax.shard_map(
        body,
        mesh=mesh,
        in_specs=placed,
        out_specs=(P("gz", "gy", "gx"), P("gy", ("gx", "gz"))),
        check_vma=False,
    )
```

```python
import jax
import jax.numpy as jnp
from jax import lax
from jax.sharding import PartitionSpec as P

S0 = 4
S1 = 4
S2 = 8


OMEGA = 0.8
VERT = 4.0
HI = lax.Precision.HIGHEST
FINE_HALO = 12
MID_HALO = 6
POST_HALO = 4


def layer_halos(u):
    count = lax.axis_size("gz")
    head = u[:1]
    tail = u[-1:]
    if count == 2:
        first = lax.axis_index("gz") == 0
        got = lax.ppermute(jnp.where(first, tail, head), "gz", [(0, 1), (1, 0)])
        zero = jnp.zeros_like(got)
        return jnp.where(first, zero, got), jnp.where(first, got, zero)
    lo = lax.ppermute(tail, "gz", [(i, i + 1) for i in range(count - 1)])
    hi = lax.ppermute(head, "gz", [(i + 1, i) for i in range(count - 1)])
    return lo, hi


def extend_rows(a, h):
    count = lax.axis_size("gy")
    lo = lax.ppermute(a[:, -h:], "gy", [(i, i + 1) for i in range(count - 1)])
    hi = lax.ppermute(a[:, :h], "gy", [(i + 1, i) for i in range(count - 1)])
    return jnp.concatenate([lo, a, hi], axis=1)


def gather_blocks(a, axis):
    count = lax.axis_size(axis)
    got = [a]
    for s in range(1, count):
        got.append(lax.ppermute(a, axis, [(i, (i + s) % count) for i in range(count)]))
    rev = jnp.stack(got[::-1], axis=0)
    return jnp.roll(rev, lax.axis_index(axis) + 1, axis=0)


def crop(a, h_from, h_to):
    cut = h_from - h_to
    return a[:, cut : a.shape[1] - cut]


def row_mask(own_rows, h):
    g = lax.axis_index("gy") * own_rows - h + lax.broadcasted_iota(jnp.int32, (1, own_rows + 2 * h, 1), 1)
    return (g >= 0) & (g < own_rows * lax.axis_size("gy"))


def neighbours(u, whole_z=False):
    if whole_z:
        zlo = zhi = jnp.zeros_like(u[:1])
    else:
        zlo, zhi = layer_halos(u)
    zero_row = jnp.zeros_like(u[:, :1])
    zero_col = jnp.zeros_like(u[:, :, :1])
    zm = jnp.concatenate([zlo, u[:-1]], axis=0)
    zp = jnp.concatenate([u[1:], zhi], axis=0)
    ym = jnp.concatenate([zero_row, u[:, :-1]], axis=1)
    yp = jnp.concatenate([u[:, 1:], zero_row], axis=1)
    xm = jnp.concatenate([zero_col, u[:, :, :-1]], axis=2)
    xp = jnp.concatenate([u[:, :, 1:], zero_col], axis=2)
    return zm, zp, ym, yp, xm, xp


def face_set(eta):
    zm, zp, ym, yp, xm, xp = neighbours(eta)
    zlo = VERT * (0.5 * (eta + zm))
    zhi = VERT * (0.5 * (eta + zp))
    ylo = 0.5 * (eta + ym)
    yhi = 0.5 * (eta + yp)
    xlo = 0.5 * (eta + xm)
    xhi = 0.5 * (eta + xp)
    return (zlo, zhi, ylo, yhi, xlo, xhi)


def operate(u, coef, whole_z=False):
    zlo, zhi, ylo, yhi, xlo, xhi, extra = coef
    zm, zp, ym, yp, xm, xp = neighbours(u, whole_z)
    out = zlo * (u - zm) + zhi * (u - zp)
    out = out + ylo * (u - ym) + yhi * (u - yp)
    out = out + xlo * (u - xm) + xhi * (u - xp)
    return out + extra * u


def diagonal(coef):
    zlo, zhi, ylo, yhi, xlo, xhi, extra = coef
    return zlo + zhi + ylo + yhi + xlo + xhi + extra


def pick(n, parity):
    src = lax.broadcasted_iota(jnp.int32, (n, n // 2), 0)
    dst = lax.broadcasted_iota(jnp.int32, (n, n // 2), 1)
    return (src == 2 * dst + parity).astype(jnp.float32)


def cols(a, parity):
    return jnp.dot(a, pick(a.shape[-1], parity), precision=HI)


def rows(a, parity):
    return jnp.einsum("yr,zyx->zrx", pick(a.shape[1], parity), a, precision=HI)


def mean_four(a):
    r0 = rows(a, 0)
    r1 = rows(a, 1)
    return 0.25 * (cols(r0, 0) + cols(r1, 0) + cols(r0, 1) + cols(r1, 1))


def coarsen(coef):
    zlo, zhi, ylo, yhi, xlo, xhi, extra = coef
    cxlo = 0.125 * cols(rows(xlo, 0) + rows(xlo, 1), 0)
    cxhi = 0.125 * cols(rows(xhi, 0) + rows(xhi, 1), 1)
    ylo0 = rows(ylo, 0)
    yhi1 = rows(yhi, 1)
    cylo = 0.125 * (cols(ylo0, 0) + cols(ylo0, 1))
    cyhi = 0.125 * (cols(yhi1, 0) + cols(yhi1, 1))
    return (mean_four(zlo), mean_four(zhi), cylo, cyhi, cxlo, cxhi, mean_four(extra))


def spread(n):
    src = lax.broadcasted_iota(jnp.int32, (n, 2 * n), 0)
    dst = lax.broadcasted_iota(jnp.int32, (n, 2 * n), 1)
    return (src == dst // 2).astype(jnp.float32)


def prolong(field):
    wide = jnp.dot(field, spread(field.shape[-1]), precision=HI)
    return jnp.einsum("ry,zrx->zyx", spread(field.shape[1]), wide, precision=HI)


def sweep(field, rhs, coef, diag, inside, whole_z=False):
    new = field + OMEGA * (rhs - operate(field, coef, whole_z)) / diag
    return jnp.where(inside, new, 0.0)


def smooth(field, rhs, coef, diag, inside, count, whole_z=False):
    for i in range(count):
        field = sweep(field, rhs, coef, diag, inside, whole_z)
    return field


def crop_all(arrs, h_from, h_to):
    return tuple(crop(a, h_from, h_to) for a in arrs)


def body_wide(viscosity, adjoint_source, forward_velocity, friction, ice_mask, grounded_mask):
    layers = viscosity.shape[0]
    own_rows = viscosity.shape[1]
    mid_rows = own_rows // 2
    cols_own = viscosity.shape[2]
    half_cols = cols_own // 2
    gz = lax.axis_index("gz")
    gy = lax.axis_index("gy")
    total_layers = layers * lax.axis_size("gz")
    layer = (gz * layers + jnp.arange(layers)).astype(jnp.float32)
    profile = (jnp.float32(total_layers) - layer) / jnp.float32(total_layers)
    wsq = profile * profile
    icef = ice_mask.astype(jnp.float32)
    groundf = grounded_mask.astype(jnp.float32)
    base = 0.05 + 2.0 * (1.0 - icef)
    ground_fric = groundf * friction
    stacked = jnp.concatenate([viscosity, adjoint_source, base[None], ground_fric[None]], axis=0)
    gathered = gather_blocks(stacked, "gx")
    gathered = jnp.concatenate([gathered[i] for i in range(gathered.shape[0])], axis=2)
    hv = FINE_HALO + 1
    ext = extend_rows(gathered, hv)
    visc_e = ext[:layers]
    src_e = crop(ext[layers : 2 * layers], hv, FINE_HALO)
    base_e = crop(ext[2 * layers : 2 * layers + 1], hv, FINE_HALO)[0]
    gfr_e = crop(ext[2 * layers + 1 : 2 * layers + 2], hv, FINE_HALO)[0]
    extra = base_e[None, :, :] + gfr_e[None, :, :] * wsq[:, None, None]
    fine = crop_all(face_set(visc_e), hv, FINE_HALO) + (extra,)
    dfine = diagonal(fine)
    middle = coarsen(fine)
    dmid = diagonal(middle)
    coarse_own = coarsen(crop_all(middle, FINE_HALO // 2, 0))
    coarse_all = gather_blocks(jnp.concatenate(coarse_own, axis=0), "gy")
    coarse_all = jnp.concatenate([coarse_all[i] for i in range(coarse_all.shape[0])], axis=1)
    coarse_all = gather_blocks(coarse_all, "gz")
    coarse = tuple(
        jnp.concatenate([coarse_all[k, i * layers : (i + 1) * layers] for k in range(coarse_all.shape[0])], axis=0)
        for i in range(7)
    )
    dcoarse = diagonal(coarse)
    in_fine = row_mask(own_rows, FINE_HALO)
    in_mid = row_mask(mid_rows, FINE_HALO // 2)

    lam = jnp.where(in_fine, OMEGA * src_e / dfine, 0.0)
    lam = smooth(lam, src_e, fine, dfine, in_fine, S0 - 1)
    b_mid = mean_four(src_e - operate(lam, fine))
    e_mid = jnp.where(in_mid, OMEGA * b_mid / dmid, 0.0)
    e_mid = smooth(e_mid, b_mid, middle, dmid, in_mid, S1 - 1)
    hm = FINE_HALO // 2
    res_mid = crop(b_mid - operate(e_mid, middle), hm, 0)
    b_low = gather_blocks(mean_four(res_mid), "gy")
    b_low = jnp.concatenate([b_low[i] for i in range(b_low.shape[0])], axis=1)
    b_low = gather_blocks(b_low, "gz")
    b_low = jnp.concatenate([b_low[k] for k in range(b_low.shape[0])], axis=0)
    e_low = OMEGA * b_low / dcoarse
    ones = jnp.ones((1, b_low.shape[1], 1), dtype=bool)
    e_low = smooth(e_low, b_low, coarse, dcoarse, ones, S2 - 1, whole_z=True)
    e_low = lax.dynamic_slice_in_dim(e_low, gz * layers, layers, 0)

    pair = jnp.concatenate([crop(e_mid, hm, 0), crop(b_mid, hm, 0)], axis=0)
    pair = extend_rows(pair, MID_HALO)
    e_mid = pair[:layers]
    b_mid = pair[layers:]
    low_rows = own_rows // 4
    ch = MID_HALO // 2
    padded = jnp.pad(e_low, ((0, 0), (ch, ch), (0, 0)))
    e_near = lax.dynamic_slice_in_dim(padded, gy * low_rows, low_rows + 2 * ch, 1)
    e_mid = e_mid + prolong(e_near)
    middle_p = crop_all(middle, hm, MID_HALO)
    dmid_p = crop(dmid, hm, MID_HALO)
    in_mid_p = row_mask(mid_rows, MID_HALO)
    e_mid = smooth(e_mid, b_mid, middle_p, dmid_p, in_mid_p, S1)

    lam = crop(lam, FINE_HALO, POST_HALO) + prolong(crop(e_mid, MID_HALO, POST_HALO // 2))
    fine_p = crop_all(fine, FINE_HALO, POST_HALO)
    dfine_p = crop(dfine, FINE_HALO, POST_HALO)
    src_p = crop(src_e, FINE_HALO, POST_HALO)
    in_fine_p = row_mask(own_rows, POST_HALO)
    lam = smooth(lam, src_p, fine_p, dfine_p, in_fine_p, S0)
    lam = crop(lam, POST_HALO, 0)

    own = lax.dynamic_slice_in_dim(lam, lax.axis_index("gx") * cols_own, cols_own, 2)
    column = jnp.sum(wsq[:, None, None] * forward_velocity * own, axis=0)
    parts = gather_blocks(column, "gz")
    summed = parts[0]
    for k in range(1, parts.shape[0]):
        summed = summed + parts[k]
    terms = -ground_fric * summed
    gradient = lax.dynamic_slice_in_dim(terms, gz * half_cols, half_cols, 1)
    return (own, gradient)


def n_layer_halos(u):
    count = lax.axis_size("gz")
    head = u[:1]
    tail = u[-1:]
    if count == 2:
        first = lax.axis_index("gz") == 0
        got = lax.ppermute(jnp.where(first, tail, head), "gz", [(0, 1), (1, 0)])
        zero = jnp.zeros_like(got)
        return jnp.where(first, zero, got), jnp.where(first, got, zero)
    lo = lax.ppermute(tail, "gz", [(i, i + 1) for i in range(count - 1)])
    hi = lax.ppermute(head, "gz", [(i + 1, i) for i in range(count - 1)])
    return lo, hi


def n_row_halos(u):
    count = lax.axis_size("gy")
    lo = lax.ppermute(u[:, -1:], "gy", [(i, i + 1) for i in range(count - 1)])
    hi = lax.ppermute(u[:, :1], "gy", [(i + 1, i) for i in range(count - 1)])
    return lo, hi


def n_neighbours(u):
    zlo, zhi = n_layer_halos(u)
    ylo, yhi = n_row_halos(u)
    zero = jnp.zeros_like(u[:, :, :1])
    zm = jnp.concatenate([zlo, u[:-1]], axis=0)
    zp = jnp.concatenate([u[1:], zhi], axis=0)
    ym = jnp.concatenate([ylo, u[:, :-1]], axis=1)
    yp = jnp.concatenate([u[:, 1:], yhi], axis=1)
    xm = jnp.concatenate([zero, u[:, :, :-1]], axis=2)
    xp = jnp.concatenate([u[:, :, 1:], zero], axis=2)
    return zm, zp, ym, yp, xm, xp


def n_face_set(eta):
    zm, zp, ym, yp, xm, xp = n_neighbours(eta)
    zlo = VERT * (0.5 * (eta + zm))
    zhi = VERT * (0.5 * (eta + zp))
    ylo = 0.5 * (eta + ym)
    yhi = 0.5 * (eta + yp)
    xlo = 0.5 * (eta + xm)
    xhi = 0.5 * (eta + xp)
    return (zlo, zhi, ylo, yhi, xlo, xhi)


def n_operate(u, coef):
    zlo, zhi, ylo, yhi, xlo, xhi, extra = coef
    zm, zp, ym, yp, xm, xp = n_neighbours(u)
    out = zlo * (u - zm) + zhi * (u - zp)
    out = out + ylo * (u - ym) + yhi * (u - yp)
    out = out + xlo * (u - xm) + xhi * (u - xp)
    return out + extra * u


def n_diagonal(coef):
    zlo, zhi, ylo, yhi, xlo, xhi, extra = coef
    return zlo + zhi + ylo + yhi + xlo + xhi + extra


def n_pick_matrix(cols):
    half = cols // 2
    src = lax.broadcasted_iota(jnp.int32, (cols, cols), 0)
    dst = lax.broadcasted_iota(jnp.int32, (cols, cols), 1)
    want = jnp.where(dst < half, 2 * dst, 2 * (dst - half) + 1)
    return (src == want).astype(jnp.float32)


def n_split_x(a):
    cols = a.shape[-1]
    both = jnp.dot(a, n_pick_matrix(cols), precision=HI)
    return both[..., : cols // 2], both[..., cols // 2 :]


def n_mean_four(a):
    e0, o0 = n_split_x(a[:, 0::2])
    e1, o1 = n_split_x(a[:, 1::2])
    return 0.25 * (e0 + e1 + o0 + o1)


def n_coarsen(coef):
    zlo, zhi, ylo, yhi, xlo, xhi, extra = coef
    xlo_e, _ = n_split_x(xlo[:, 0::2] + xlo[:, 1::2])
    _, xhi_o = n_split_x(xhi[:, 0::2] + xhi[:, 1::2])
    ylo_e, ylo_o = n_split_x(ylo[:, 0::2])
    yhi_e, yhi_o = n_split_x(yhi[:, 1::2])
    cxlo = 0.125 * xlo_e
    cxhi = 0.125 * xhi_o
    cylo = 0.125 * (ylo_e + ylo_o)
    cyhi = 0.125 * (yhi_e + yhi_o)
    return (n_mean_four(zlo), n_mean_four(zhi), cylo, cyhi, cxlo, cxhi, n_mean_four(extra))


def n_prolong(field):
    cols = field.shape[-1]
    src = lax.broadcasted_iota(jnp.int32, (cols, 2 * cols), 0)
    dst = lax.broadcasted_iota(jnp.int32, (cols, 2 * cols), 1)
    spread = (src == dst // 2).astype(jnp.float32)
    wide = jnp.dot(field, spread, precision=HI)
    return jnp.repeat(wide, 2, axis=1)


def n_sweep(field, rhs, coef, diag):
    return field + OMEGA * (rhs - n_operate(field, coef)) / diag


def n_body(viscosity, adjoint_source, forward_velocity, friction, ice_mask, grounded_mask):
    layers = viscosity.shape[0]
    cols = viscosity.shape[2]
    half_cols = cols // 2
    gz = lax.axis_index("gz")
    total_layers = layers * lax.axis_size("gz")
    layer = (gz * layers + jnp.arange(layers)).astype(jnp.float32)
    profile = (jnp.float32(total_layers) - layer) / jnp.float32(total_layers)
    wsq = profile * profile
    icef = ice_mask.astype(jnp.float32)
    groundf = grounded_mask.astype(jnp.float32)
    base = 0.05 + 2.0 * (1.0 - icef)
    ground_fric = groundf * friction
    stacked = jnp.concatenate([viscosity, adjoint_source, base[None], ground_fric[None]], axis=0)
    gathered = lax.all_gather(stacked, "gx", axis=0, tiled=False)
    count_x = gathered.shape[0]
    gathered = jnp.concatenate([gathered[i] for i in range(count_x)], axis=2)
    visc_all = gathered[:layers]
    source_all = gathered[layers : 2 * layers]
    base_all = gathered[2 * layers]
    gfr_all = gathered[2 * layers + 1]
    extra = base_all[None, :, :] + gfr_all[None, :, :] * wsq[:, None, None]
    fine = n_face_set(visc_all) + (extra,)
    dfine = n_diagonal(fine)
    middle = n_coarsen(fine)
    dmid = n_diagonal(middle)
    coarse = n_coarsen(middle)
    dcoarse = n_diagonal(coarse)
    lam = OMEGA * source_all / dfine
    for i in range(S0 - 1):
        lam = n_sweep(lam, source_all, fine, dfine)
    b_mid = n_mean_four(source_all - n_operate(lam, fine))
    e_mid = OMEGA * b_mid / dmid
    for i in range(S1 - 1):
        e_mid = n_sweep(e_mid, b_mid, middle, dmid)
    b_low = n_mean_four(b_mid - n_operate(e_mid, middle))
    e_low = OMEGA * b_low / dcoarse
    for i in range(S2 - 1):
        e_low = n_sweep(e_low, b_low, coarse, dcoarse)
    e_mid = e_mid + n_prolong(e_low)
    for i in range(S1):
        e_mid = n_sweep(e_mid, b_mid, middle, dmid)
    lam = lam + n_prolong(e_mid)
    for i in range(S0):
        lam = n_sweep(lam, source_all, fine, dfine)
    own = lax.dynamic_slice_in_dim(lam, lax.axis_index("gx") * cols, cols, 2)
    column = jnp.sum(wsq[:, None, None] * forward_velocity * own, axis=0)
    summed = lax.psum(column, "gz")
    terms = -ground_fric * summed
    gradient = lax.dynamic_slice_in_dim(terms, gz * half_cols, half_cols, 1)
    return (own, gradient)


def body(viscosity, *rest):
    layers, own_rows, cols_own = viscosity.shape
    cols_all = cols_own * lax.axis_size("gx")
    wide_bytes = 4 * layers * (own_rows + 2 * FINE_HALO + 2) * cols_all
    if FINE_HALO + 1 <= own_rows and MID_HALO <= own_rows // 2 and 20 * wide_bytes <= 40 * 2**20 and lax.axis_size("gy") <= 8:
        return body_wide(viscosity, *rest)
    return n_body(viscosity, *rest)


def solution(mesh):
    placed = (
        P("gz", "gy", "gx"),
        P("gz", "gy", "gx"),
        P("gz", "gy", "gx"),
        P("gy", "gx"),
        P("gy", "gx"),
        P("gy", "gx"),
    )
    return jax.shard_map(
        body,
        mesh=mesh,
        in_specs=placed,
        out_specs=(P("gz", "gy", "gx"), P("gy", ("gx", "gz"))),
        check_vma=False,
    )
```

```python
import jax
import jax.numpy as jnp
from jax import lax
from jax.sharding import PartitionSpec as P

S0 = 4
S1 = 4
S2 = 8


OMEGA = 0.8
VERT = 4.0
HI = lax.Precision.HIGHEST
FINE_HALO = 12
MID_HALO = 6
POST_HALO = 4


def layer_halos(u):
    count = lax.axis_size("gz")
    head = u[:1]
    tail = u[-1:]
    if count == 2:
        first = lax.axis_index("gz") == 0
        got = lax.ppermute(jnp.where(first, tail, head), "gz", [(0, 1), (1, 0)])
        zero = jnp.zeros_like(got)
        return jnp.where(first, zero, got), jnp.where(first, got, zero)
    lo = lax.ppermute(tail, "gz", [(i, i + 1) for i in range(count - 1)])
    hi = lax.ppermute(head, "gz", [(i + 1, i) for i in range(count - 1)])
    return lo, hi


def extend_rows(a, h):
    count = lax.axis_size("gy")
    lo = lax.ppermute(a[:, -h:], "gy", [(i, i + 1) for i in range(count - 1)])
    hi = lax.ppermute(a[:, :h], "gy", [(i + 1, i) for i in range(count - 1)])
    return jnp.concatenate([lo, a, hi], axis=1)


def gather_blocks(a, axis):
    count = lax.axis_size(axis)
    got = [a]
    for s in range(1, count):
        got.append(lax.ppermute(a, axis, [(i, (i + s) % count) for i in range(count)]))
    rev = jnp.stack(got[::-1], axis=0)
    return jnp.roll(rev, lax.axis_index(axis) + 1, axis=0)


def crop(a, h_from, h_to):
    cut = h_from - h_to
    return a[:, cut : a.shape[1] - cut]


def row_mask(own_rows, h):
    g = lax.axis_index("gy") * own_rows - h + lax.broadcasted_iota(jnp.int32, (1, own_rows + 2 * h, 1), 1)
    return (g >= 0) & (g < own_rows * lax.axis_size("gy"))


def neighbours(u, whole_z=False):
    if whole_z:
        zlo = zhi = jnp.zeros_like(u[:1])
    else:
        zlo, zhi = layer_halos(u)
    zero_row = jnp.zeros_like(u[:, :1])
    zero_col = jnp.zeros_like(u[:, :, :1])
    zm = jnp.concatenate([zlo, u[:-1]], axis=0)
    zp = jnp.concatenate([u[1:], zhi], axis=0)
    ym = jnp.concatenate([zero_row, u[:, :-1]], axis=1)
    yp = jnp.concatenate([u[:, 1:], zero_row], axis=1)
    xm = jnp.concatenate([zero_col, u[:, :, :-1]], axis=2)
    xp = jnp.concatenate([u[:, :, 1:], zero_col], axis=2)
    return zm, zp, ym, yp, xm, xp


def face_set(eta):
    zm, zp, ym, yp, xm, xp = neighbours(eta)
    zlo = VERT * (0.5 * (eta + zm))
    zhi = VERT * (0.5 * (eta + zp))
    ylo = 0.5 * (eta + ym)
    yhi = 0.5 * (eta + yp)
    xlo = 0.5 * (eta + xm)
    xhi = 0.5 * (eta + xp)
    return (zlo, zhi, ylo, yhi, xlo, xhi)


def operate(u, coef, whole_z=False):
    zlo, zhi, ylo, yhi, xlo, xhi, extra = coef
    zm, zp, ym, yp, xm, xp = neighbours(u, whole_z)
    out = zlo * (u - zm) + zhi * (u - zp)
    out = out + ylo * (u - ym) + yhi * (u - yp)
    out = out + xlo * (u - xm) + xhi * (u - xp)
    return out + extra * u


def diagonal(coef):
    zlo, zhi, ylo, yhi, xlo, xhi, extra = coef
    return zlo + zhi + ylo + yhi + xlo + xhi + extra


def pick(n, parity):
    src = lax.broadcasted_iota(jnp.int32, (n, n // 2), 0)
    dst = lax.broadcasted_iota(jnp.int32, (n, n // 2), 1)
    return (src == 2 * dst + parity).astype(jnp.float32)


def cols(a, parity):
    return jnp.dot(a, pick(a.shape[-1], parity), precision=HI)


def rows(a, parity):
    return jnp.einsum("yr,zyx->zrx", pick(a.shape[1], parity), a, precision=HI)


def mean_four(a):
    r0 = rows(a, 0)
    r1 = rows(a, 1)
    return 0.25 * (cols(r0, 0) + cols(r1, 0) + cols(r0, 1) + cols(r1, 1))


def coarsen(coef):
    zlo, zhi, ylo, yhi, xlo, xhi, extra = coef
    cxlo = 0.125 * cols(rows(xlo, 0) + rows(xlo, 1), 0)
    cxhi = 0.125 * cols(rows(xhi, 0) + rows(xhi, 1), 1)
    ylo0 = rows(ylo, 0)
    yhi1 = rows(yhi, 1)
    cylo = 0.125 * (cols(ylo0, 0) + cols(ylo0, 1))
    cyhi = 0.125 * (cols(yhi1, 0) + cols(yhi1, 1))
    return (mean_four(zlo), mean_four(zhi), cylo, cyhi, cxlo, cxhi, mean_four(extra))


def spread(n):
    src = lax.broadcasted_iota(jnp.int32, (n, 2 * n), 0)
    dst = lax.broadcasted_iota(jnp.int32, (n, 2 * n), 1)
    return (src == dst // 2).astype(jnp.float32)


def prolong(field):
    wide = jnp.dot(field, spread(field.shape[-1]), precision=HI)
    return jnp.einsum("ry,zrx->zyx", spread(field.shape[1]), wide, precision=HI)


def sweep(field, rhs, coef, diag, inside, whole_z=False):
    new = field + OMEGA * (rhs - operate(field, coef, whole_z)) / diag
    return jnp.where(inside, new, 0.0)


def smooth(field, rhs, coef, diag, inside, count, whole_z=False):
    for i in range(count):
        field = sweep(field, rhs, coef, diag, inside, whole_z)
    return field


def crop_all(arrs, h_from, h_to):
    return tuple(crop(a, h_from, h_to) for a in arrs)


def body_wide(viscosity, adjoint_source, forward_velocity, friction, ice_mask, grounded_mask):
    layers = viscosity.shape[0]
    own_rows = viscosity.shape[1]
    mid_rows = own_rows // 2
    cols_own = viscosity.shape[2]
    half_cols = cols_own // 2
    gz = lax.axis_index("gz")
    gy = lax.axis_index("gy")
    total_layers = layers * lax.axis_size("gz")
    layer = (gz * layers + jnp.arange(layers)).astype(jnp.float32)
    profile = (jnp.float32(total_layers) - layer) / jnp.float32(total_layers)
    wsq = profile * profile
    icef = ice_mask.astype(jnp.float32)
    groundf = grounded_mask.astype(jnp.float32)
    base = 0.05 + 2.0 * (1.0 - icef)
    ground_fric = groundf * friction
    stacked = jnp.concatenate([viscosity, adjoint_source, base[None], ground_fric[None]], axis=0)
    hv = FINE_HALO + 1
    ext = gather_blocks(extend_rows(stacked, hv), "gx")
    ext = jnp.concatenate([ext[i] for i in range(ext.shape[0])], axis=2)
    visc_e = ext[:layers]
    src_e = crop(ext[layers : 2 * layers], hv, FINE_HALO)
    base_e = crop(ext[2 * layers : 2 * layers + 1], hv, FINE_HALO)[0]
    gfr_e = crop(ext[2 * layers + 1 : 2 * layers + 2], hv, FINE_HALO)[0]
    extra = base_e[None, :, :] + gfr_e[None, :, :] * wsq[:, None, None]
    fine = crop_all(face_set(visc_e), hv, FINE_HALO) + (extra,)
    dfine = diagonal(fine)
    middle = coarsen(fine)
    dmid = diagonal(middle)
    coarse_own = coarsen(crop_all(middle, FINE_HALO // 2, 0))
    coarse_all = gather_blocks(jnp.concatenate(coarse_own, axis=0), "gy")
    coarse_all = jnp.concatenate([coarse_all[i] for i in range(coarse_all.shape[0])], axis=1)
    coarse_all = gather_blocks(coarse_all, "gz")
    coarse = tuple(
        jnp.concatenate([coarse_all[k, i * layers : (i + 1) * layers] for k in range(coarse_all.shape[0])], axis=0)
        for i in range(7)
    )
    dcoarse = diagonal(coarse)
    in_fine = row_mask(own_rows, FINE_HALO)
    in_mid = row_mask(mid_rows, FINE_HALO // 2)

    lam = jnp.where(in_fine, OMEGA * src_e / dfine, 0.0)
    lam = smooth(lam, src_e, fine, dfine, in_fine, S0 - 1)
    b_mid = mean_four(src_e - operate(lam, fine))
    e_mid = jnp.where(in_mid, OMEGA * b_mid / dmid, 0.0)
    e_mid = smooth(e_mid, b_mid, middle, dmid, in_mid, S1 - 1)
    hm = FINE_HALO // 2
    res_mid = crop(b_mid - operate(e_mid, middle), hm, 0)
    b_low = gather_blocks(mean_four(res_mid), "gy")
    b_low = jnp.concatenate([b_low[i] for i in range(b_low.shape[0])], axis=1)
    b_low = gather_blocks(b_low, "gz")
    b_low = jnp.concatenate([b_low[k] for k in range(b_low.shape[0])], axis=0)
    e_low = OMEGA * b_low / dcoarse
    ones = jnp.ones((1, b_low.shape[1], 1), dtype=bool)
    e_low = smooth(e_low, b_low, coarse, dcoarse, ones, S2 - 1, whole_z=True)
    e_low = lax.dynamic_slice_in_dim(e_low, gz * layers, layers, 0)

    pair = jnp.concatenate([crop(e_mid, hm, 0), crop(b_mid, hm, 0)], axis=0)
    pair = extend_rows(pair, MID_HALO)
    e_mid = pair[:layers]
    b_mid = pair[layers:]
    low_rows = own_rows // 4
    ch = MID_HALO // 2
    padded = jnp.pad(e_low, ((0, 0), (ch, ch), (0, 0)))
    e_near = lax.dynamic_slice_in_dim(padded, gy * low_rows, low_rows + 2 * ch, 1)
    e_mid = e_mid + prolong(e_near)
    middle_p = crop_all(middle, hm, MID_HALO)
    dmid_p = crop(dmid, hm, MID_HALO)
    in_mid_p = row_mask(mid_rows, MID_HALO)
    e_mid = smooth(e_mid, b_mid, middle_p, dmid_p, in_mid_p, S1)

    lam = crop(lam, FINE_HALO, POST_HALO) + prolong(crop(e_mid, MID_HALO, POST_HALO // 2))
    fine_p = crop_all(fine, FINE_HALO, POST_HALO)
    dfine_p = crop(dfine, FINE_HALO, POST_HALO)
    src_p = crop(src_e, FINE_HALO, POST_HALO)
    in_fine_p = row_mask(own_rows, POST_HALO)
    lam = smooth(lam, src_p, fine_p, dfine_p, in_fine_p, S0)
    lam = crop(lam, POST_HALO, 0)

    own = lax.dynamic_slice_in_dim(lam, lax.axis_index("gx") * cols_own, cols_own, 2)
    column = jnp.sum(wsq[:, None, None] * forward_velocity * own, axis=0)
    parts = gather_blocks(column, "gz")
    summed = parts[0]
    for k in range(1, parts.shape[0]):
        summed = summed + parts[k]
    terms = -ground_fric * summed
    gradient = lax.dynamic_slice_in_dim(terms, gz * half_cols, half_cols, 1)
    return (own, gradient)


def n_layer_halos(u):
    count = lax.axis_size("gz")
    head = u[:1]
    tail = u[-1:]
    if count == 2:
        first = lax.axis_index("gz") == 0
        got = lax.ppermute(jnp.where(first, tail, head), "gz", [(0, 1), (1, 0)])
        zero = jnp.zeros_like(got)
        return jnp.where(first, zero, got), jnp.where(first, got, zero)
    lo = lax.ppermute(tail, "gz", [(i, i + 1) for i in range(count - 1)])
    hi = lax.ppermute(head, "gz", [(i + 1, i) for i in range(count - 1)])
    return lo, hi


def n_row_halos(u):
    count = lax.axis_size("gy")
    lo = lax.ppermute(u[:, -1:], "gy", [(i, i + 1) for i in range(count - 1)])
    hi = lax.ppermute(u[:, :1], "gy", [(i + 1, i) for i in range(count - 1)])
    return lo, hi


def n_neighbours(u):
    zlo, zhi = n_layer_halos(u)
    ylo, yhi = n_row_halos(u)
    zero = jnp.zeros_like(u[:, :, :1])
    zm = jnp.concatenate([zlo, u[:-1]], axis=0)
    zp = jnp.concatenate([u[1:], zhi], axis=0)
    ym = jnp.concatenate([ylo, u[:, :-1]], axis=1)
    yp = jnp.concatenate([u[:, 1:], yhi], axis=1)
    xm = jnp.concatenate([zero, u[:, :, :-1]], axis=2)
    xp = jnp.concatenate([u[:, :, 1:], zero], axis=2)
    return zm, zp, ym, yp, xm, xp


def n_face_set(eta):
    zm, zp, ym, yp, xm, xp = n_neighbours(eta)
    zlo = VERT * (0.5 * (eta + zm))
    zhi = VERT * (0.5 * (eta + zp))
    ylo = 0.5 * (eta + ym)
    yhi = 0.5 * (eta + yp)
    xlo = 0.5 * (eta + xm)
    xhi = 0.5 * (eta + xp)
    return (zlo, zhi, ylo, yhi, xlo, xhi)


def n_operate(u, coef):
    zlo, zhi, ylo, yhi, xlo, xhi, extra = coef
    zm, zp, ym, yp, xm, xp = n_neighbours(u)
    out = zlo * (u - zm) + zhi * (u - zp)
    out = out + ylo * (u - ym) + yhi * (u - yp)
    out = out + xlo * (u - xm) + xhi * (u - xp)
    return out + extra * u


def n_diagonal(coef):
    zlo, zhi, ylo, yhi, xlo, xhi, extra = coef
    return zlo + zhi + ylo + yhi + xlo + xhi + extra


def n_pick_matrix(cols):
    half = cols // 2
    src = lax.broadcasted_iota(jnp.int32, (cols, cols), 0)
    dst = lax.broadcasted_iota(jnp.int32, (cols, cols), 1)
    want = jnp.where(dst < half, 2 * dst, 2 * (dst - half) + 1)
    return (src == want).astype(jnp.float32)


def n_split_x(a):
    cols = a.shape[-1]
    both = jnp.dot(a, n_pick_matrix(cols), precision=HI)
    return both[..., : cols // 2], both[..., cols // 2 :]


def n_mean_four(a):
    e0, o0 = n_split_x(a[:, 0::2])
    e1, o1 = n_split_x(a[:, 1::2])
    return 0.25 * (e0 + e1 + o0 + o1)


def n_coarsen(coef):
    zlo, zhi, ylo, yhi, xlo, xhi, extra = coef
    xlo_e, _ = n_split_x(xlo[:, 0::2] + xlo[:, 1::2])
    _, xhi_o = n_split_x(xhi[:, 0::2] + xhi[:, 1::2])
    ylo_e, ylo_o = n_split_x(ylo[:, 0::2])
    yhi_e, yhi_o = n_split_x(yhi[:, 1::2])
    cxlo = 0.125 * xlo_e
    cxhi = 0.125 * xhi_o
    cylo = 0.125 * (ylo_e + ylo_o)
    cyhi = 0.125 * (yhi_e + yhi_o)
    return (n_mean_four(zlo), n_mean_four(zhi), cylo, cyhi, cxlo, cxhi, n_mean_four(extra))


def n_prolong(field):
    cols = field.shape[-1]
    src = lax.broadcasted_iota(jnp.int32, (cols, 2 * cols), 0)
    dst = lax.broadcasted_iota(jnp.int32, (cols, 2 * cols), 1)
    spread = (src == dst // 2).astype(jnp.float32)
    wide = jnp.dot(field, spread, precision=HI)
    return jnp.repeat(wide, 2, axis=1)


def n_sweep(field, rhs, coef, diag):
    return field + OMEGA * (rhs - n_operate(field, coef)) / diag


def n_body(viscosity, adjoint_source, forward_velocity, friction, ice_mask, grounded_mask):
    layers = viscosity.shape[0]
    cols = viscosity.shape[2]
    half_cols = cols // 2
    gz = lax.axis_index("gz")
    total_layers = layers * lax.axis_size("gz")
    layer = (gz * layers + jnp.arange(layers)).astype(jnp.float32)
    profile = (jnp.float32(total_layers) - layer) / jnp.float32(total_layers)
    wsq = profile * profile
    icef = ice_mask.astype(jnp.float32)
    groundf = grounded_mask.astype(jnp.float32)
    base = 0.05 + 2.0 * (1.0 - icef)
    ground_fric = groundf * friction
    stacked = jnp.concatenate([viscosity, adjoint_source, base[None], ground_fric[None]], axis=0)
    gathered = lax.all_gather(stacked, "gx", axis=0, tiled=False)
    count_x = gathered.shape[0]
    gathered = jnp.concatenate([gathered[i] for i in range(count_x)], axis=2)
    visc_all = gathered[:layers]
    source_all = gathered[layers : 2 * layers]
    base_all = gathered[2 * layers]
    gfr_all = gathered[2 * layers + 1]
    extra = base_all[None, :, :] + gfr_all[None, :, :] * wsq[:, None, None]
    fine = n_face_set(visc_all) + (extra,)
    dfine = n_diagonal(fine)
    middle = n_coarsen(fine)
    dmid = n_diagonal(middle)
    coarse = n_coarsen(middle)
    dcoarse = n_diagonal(coarse)
    lam = OMEGA * source_all / dfine
    for i in range(S0 - 1):
        lam = n_sweep(lam, source_all, fine, dfine)
    b_mid = n_mean_four(source_all - n_operate(lam, fine))
    e_mid = OMEGA * b_mid / dmid
    for i in range(S1 - 1):
        e_mid = n_sweep(e_mid, b_mid, middle, dmid)
    b_low = n_mean_four(b_mid - n_operate(e_mid, middle))
    e_low = OMEGA * b_low / dcoarse
    for i in range(S2 - 1):
        e_low = n_sweep(e_low, b_low, coarse, dcoarse)
    e_mid = e_mid + n_prolong(e_low)
    for i in range(S1):
        e_mid = n_sweep(e_mid, b_mid, middle, dmid)
    lam = lam + n_prolong(e_mid)
    for i in range(S0):
        lam = n_sweep(lam, source_all, fine, dfine)
    own = lax.dynamic_slice_in_dim(lam, lax.axis_index("gx") * cols, cols, 2)
    column = jnp.sum(wsq[:, None, None] * forward_velocity * own, axis=0)
    summed = lax.psum(column, "gz")
    terms = -ground_fric * summed
    gradient = lax.dynamic_slice_in_dim(terms, gz * half_cols, half_cols, 1)
    return (own, gradient)


def body(viscosity, *rest):
    layers, own_rows, cols_own = viscosity.shape
    cols_all = cols_own * lax.axis_size("gx")
    wide_bytes = 4 * layers * (own_rows + 2 * FINE_HALO + 2) * cols_all
    if FINE_HALO + 1 <= own_rows and MID_HALO <= own_rows // 2 and 20 * wide_bytes <= 40 * 2**20 and lax.axis_size("gy") <= 8:
        return body_wide(viscosity, *rest)
    return n_body(viscosity, *rest)


def solution(mesh):
    placed = (
        P("gz", "gy", "gx"),
        P("gz", "gy", "gx"),
        P("gz", "gy", "gx"),
        P("gy", "gx"),
        P("gy", "gx"),
        P("gy", "gx"),
    )
    return jax.shard_map(
        body,
        mesh=mesh,
        in_specs=placed,
        out_specs=(P("gz", "gy", "gx"), P("gy", ("gx", "gz"))),
        check_vma=False,
    )
```

```python
import jax
import jax.numpy as jnp
from jax import lax
from jax.sharding import PartitionSpec as P

S0 = 4
S1 = 4
S2 = 8


OMEGA = 0.8
VERT = 4.0
HI = lax.Precision.HIGHEST
FINE_HALO = 12
MID_HALO = 6
POST_HALO = 4


def layer_halos(u):
    count = lax.axis_size("gz")
    head = u[:1]
    tail = u[-1:]
    if count == 2:
        first = lax.axis_index("gz") == 0
        got = lax.ppermute(jnp.where(first, tail, head), "gz", [(0, 1), (1, 0)])
        zero = jnp.zeros_like(got)
        return jnp.where(first, zero, got), jnp.where(first, got, zero)
    lo = lax.ppermute(tail, "gz", [(i, i + 1) for i in range(count - 1)])
    hi = lax.ppermute(head, "gz", [(i + 1, i) for i in range(count - 1)])
    return lo, hi


def extend_rows(a, h):
    count = lax.axis_size("gy")
    lo = lax.ppermute(a[:, -h:], "gy", [(i, i + 1) for i in range(count - 1)])
    hi = lax.ppermute(a[:, :h], "gy", [(i + 1, i) for i in range(count - 1)])
    return jnp.concatenate([lo, a, hi], axis=1)


def gather_blocks(a, axis):
    count = lax.axis_size(axis)
    got = [a]
    for s in range(1, count):
        got.append(lax.ppermute(a, axis, [(i, (i + s) % count) for i in range(count)]))
    rev = jnp.stack(got[::-1], axis=0)
    return jnp.roll(rev, lax.axis_index(axis) + 1, axis=0)


def crop(a, h_from, h_to):
    cut = h_from - h_to
    return a[:, cut : a.shape[1] - cut]


def row_mask(own_rows, h):
    g = lax.axis_index("gy") * own_rows - h + lax.broadcasted_iota(jnp.int32, (1, own_rows + 2 * h, 1), 1)
    return (g >= 0) & (g < own_rows * lax.axis_size("gy"))


def neighbours(u, whole_z=False):
    if whole_z:
        zlo = zhi = jnp.zeros_like(u[:1])
    else:
        zlo, zhi = layer_halos(u)
    zero_row = jnp.zeros_like(u[:, :1])
    zero_col = jnp.zeros_like(u[:, :, :1])
    zm = jnp.concatenate([zlo, u[:-1]], axis=0)
    zp = jnp.concatenate([u[1:], zhi], axis=0)
    ym = jnp.concatenate([zero_row, u[:, :-1]], axis=1)
    yp = jnp.concatenate([u[:, 1:], zero_row], axis=1)
    xm = jnp.concatenate([zero_col, u[:, :, :-1]], axis=2)
    xp = jnp.concatenate([u[:, :, 1:], zero_col], axis=2)
    return zm, zp, ym, yp, xm, xp


def face_set(eta):
    zm, zp, ym, yp, xm, xp = neighbours(eta)
    zlo = VERT * (0.5 * (eta + zm))
    zhi = VERT * (0.5 * (eta + zp))
    ylo = 0.5 * (eta + ym)
    yhi = 0.5 * (eta + yp)
    xlo = 0.5 * (eta + xm)
    xhi = 0.5 * (eta + xp)
    return (zlo, zhi, ylo, yhi, xlo, xhi)


def operate(u, coef, whole_z=False):
    zlo, zhi, ylo, yhi, xlo, xhi, extra = coef
    zm, zp, ym, yp, xm, xp = neighbours(u, whole_z)
    out = zlo * (u - zm) + zhi * (u - zp)
    out = out + ylo * (u - ym) + yhi * (u - yp)
    out = out + xlo * (u - xm) + xhi * (u - xp)
    return out + extra * u


def diagonal(coef):
    zlo, zhi, ylo, yhi, xlo, xhi, extra = coef
    return zlo + zhi + ylo + yhi + xlo + xhi + extra


def pick(n, parity):
    src = lax.broadcasted_iota(jnp.int32, (n, n // 2), 0)
    dst = lax.broadcasted_iota(jnp.int32, (n, n // 2), 1)
    return (src == 2 * dst + parity).astype(jnp.float32)


def cols(a, parity):
    return jnp.dot(a, pick(a.shape[-1], parity), precision=HI)


def rows(a, parity):
    return jnp.einsum("yr,zyx->zrx", pick(a.shape[1], parity), a, precision=HI)


def mean_four(a):
    r0 = rows(a, 0)
    r1 = rows(a, 1)
    return 0.25 * (cols(r0, 0) + cols(r1, 0) + cols(r0, 1) + cols(r1, 1))


def coarsen(coef):
    zlo, zhi, ylo, yhi, xlo, xhi, extra = coef
    cxlo = 0.125 * cols(rows(xlo, 0) + rows(xlo, 1), 0)
    cxhi = 0.125 * cols(rows(xhi, 0) + rows(xhi, 1), 1)
    ylo0 = rows(ylo, 0)
    yhi1 = rows(yhi, 1)
    cylo = 0.125 * (cols(ylo0, 0) + cols(ylo0, 1))
    cyhi = 0.125 * (cols(yhi1, 0) + cols(yhi1, 1))
    return (mean_four(zlo), mean_four(zhi), cylo, cyhi, cxlo, cxhi, mean_four(extra))


def spread(n):
    src = lax.broadcasted_iota(jnp.int32, (n, 2 * n), 0)
    dst = lax.broadcasted_iota(jnp.int32, (n, 2 * n), 1)
    return (src == dst // 2).astype(jnp.float32)


def prolong(field):
    wide = jnp.dot(field, spread(field.shape[-1]), precision=HI)
    return jnp.einsum("ry,zrx->zyx", spread(field.shape[1]), wide, precision=HI)


def sweep(field, rhs, coef, diag, inside, whole_z=False):
    new = field + OMEGA * (rhs - operate(field, coef, whole_z)) / diag
    return jnp.where(inside, new, 0.0)


def smooth(field, rhs, coef, diag, inside, count, whole_z=False):
    for i in range(count):
        field = sweep(field, rhs, coef, diag, inside, whole_z)
    return field


def crop_all(arrs, h_from, h_to):
    return tuple(crop(a, h_from, h_to) for a in arrs)


def body_wide(viscosity, adjoint_source, forward_velocity, friction, ice_mask, grounded_mask):
    layers = viscosity.shape[0]
    own_rows = viscosity.shape[1]
    mid_rows = own_rows // 2
    cols_own = viscosity.shape[2]
    half_cols = cols_own // 2
    gz = lax.axis_index("gz")
    gy = lax.axis_index("gy")
    total_layers = layers * lax.axis_size("gz")
    layer = (gz * layers + jnp.arange(layers)).astype(jnp.float32)
    profile = (jnp.float32(total_layers) - layer) / jnp.float32(total_layers)
    wsq = profile * profile
    icef = ice_mask.astype(jnp.float32)
    groundf = grounded_mask.astype(jnp.float32)
    base = 0.05 + 2.0 * (1.0 - icef)
    ground_fric = groundf * friction
    stacked = jnp.concatenate([viscosity, adjoint_source, base[None], ground_fric[None]], axis=0)
    gathered = gather_blocks(stacked, "gx")
    gathered = jnp.concatenate([gathered[i] for i in range(gathered.shape[0])], axis=2)
    hv = FINE_HALO + 1
    ext = extend_rows(gathered, hv)
    visc_e = ext[:layers]
    src_e = crop(ext[layers : 2 * layers], hv, FINE_HALO)
    base_e = crop(ext[2 * layers : 2 * layers + 1], hv, FINE_HALO)[0]
    gfr_e = crop(ext[2 * layers + 1 : 2 * layers + 2], hv, FINE_HALO)[0]
    extra = base_e[None, :, :] + gfr_e[None, :, :] * wsq[:, None, None]
    fine = crop_all(face_set(visc_e), hv, FINE_HALO) + (extra,)
    dfine = diagonal(fine)
    middle = coarsen(fine)
    dmid = diagonal(middle)
    coarse_own = coarsen(crop_all(middle, FINE_HALO // 2, 0))
    in_fine = row_mask(own_rows, FINE_HALO)
    in_mid = row_mask(mid_rows, FINE_HALO // 2)

    lam = jnp.where(in_fine, OMEGA * src_e / dfine, 0.0)
    lam = smooth(lam, src_e, fine, dfine, in_fine, S0 - 1)
    b_mid = mean_four(src_e - operate(lam, fine))
    e_mid = jnp.where(in_mid, OMEGA * b_mid / dmid, 0.0)
    e_mid = smooth(e_mid, b_mid, middle, dmid, in_mid, S1 - 1)
    hm = FINE_HALO // 2
    res_mid = crop(b_mid - operate(e_mid, middle), hm, 0)
    low_all = gather_blocks(jnp.concatenate(coarse_own + (mean_four(res_mid),), axis=0), "gy")
    low_all = jnp.concatenate([low_all[i] for i in range(low_all.shape[0])], axis=1)
    low_all = gather_blocks(low_all, "gz")
    low_all = tuple(
        jnp.concatenate([low_all[k, i * layers : (i + 1) * layers] for k in range(low_all.shape[0])], axis=0)
        for i in range(8)
    )
    coarse = low_all[:7]
    b_low = low_all[7]
    dcoarse = diagonal(coarse)
    e_low = OMEGA * b_low / dcoarse
    ones = jnp.ones((1, b_low.shape[1], 1), dtype=bool)
    e_low = smooth(e_low, b_low, coarse, dcoarse, ones, S2 - 1, whole_z=True)
    e_low = lax.dynamic_slice_in_dim(e_low, gz * layers, layers, 0)

    pair = jnp.concatenate([crop(e_mid, hm, 0), crop(b_mid, hm, 0)], axis=0)
    pair = extend_rows(pair, MID_HALO)
    e_mid = pair[:layers]
    b_mid = pair[layers:]
    low_rows = own_rows // 4
    ch = MID_HALO // 2
    padded = jnp.pad(e_low, ((0, 0), (ch, ch), (0, 0)))
    e_near = lax.dynamic_slice_in_dim(padded, gy * low_rows, low_rows + 2 * ch, 1)
    e_mid = e_mid + prolong(e_near)
    middle_p = crop_all(middle, hm, MID_HALO)
    dmid_p = crop(dmid, hm, MID_HALO)
    in_mid_p = row_mask(mid_rows, MID_HALO)
    e_mid = smooth(e_mid, b_mid, middle_p, dmid_p, in_mid_p, S1)

    lam = crop(lam, FINE_HALO, POST_HALO) + prolong(crop(e_mid, MID_HALO, POST_HALO // 2))
    fine_p = crop_all(fine, FINE_HALO, POST_HALO)
    dfine_p = crop(dfine, FINE_HALO, POST_HALO)
    src_p = crop(src_e, FINE_HALO, POST_HALO)
    in_fine_p = row_mask(own_rows, POST_HALO)
    lam = smooth(lam, src_p, fine_p, dfine_p, in_fine_p, S0)
    lam = crop(lam, POST_HALO, 0)

    own = lax.dynamic_slice_in_dim(lam, lax.axis_index("gx") * cols_own, cols_own, 2)
    column = jnp.sum(wsq[:, None, None] * forward_velocity * own, axis=0)
    parts = gather_blocks(column, "gz")
    summed = parts[0]
    for k in range(1, parts.shape[0]):
        summed = summed + parts[k]
    terms = -ground_fric * summed
    gradient = lax.dynamic_slice_in_dim(terms, gz * half_cols, half_cols, 1)
    return (own, gradient)


def n_layer_halos(u):
    count = lax.axis_size("gz")
    head = u[:1]
    tail = u[-1:]
    if count == 2:
        first = lax.axis_index("gz") == 0
        got = lax.ppermute(jnp.where(first, tail, head), "gz", [(0, 1), (1, 0)])
        zero = jnp.zeros_like(got)
        return jnp.where(first, zero, got), jnp.where(first, got, zero)
    lo = lax.ppermute(tail, "gz", [(i, i + 1) for i in range(count - 1)])
    hi = lax.ppermute(head, "gz", [(i + 1, i) for i in range(count - 1)])
    return lo, hi


def n_row_halos(u):
    count = lax.axis_size("gy")
    lo = lax.ppermute(u[:, -1:], "gy", [(i, i + 1) for i in range(count - 1)])
    hi = lax.ppermute(u[:, :1], "gy", [(i + 1, i) for i in range(count - 1)])
    return lo, hi


def n_neighbours(u):
    zlo, zhi = n_layer_halos(u)
    ylo, yhi = n_row_halos(u)
    zero = jnp.zeros_like(u[:, :, :1])
    zm = jnp.concatenate([zlo, u[:-1]], axis=0)
    zp = jnp.concatenate([u[1:], zhi], axis=0)
    ym = jnp.concatenate([ylo, u[:, :-1]], axis=1)
    yp = jnp.concatenate([u[:, 1:], yhi], axis=1)
    xm = jnp.concatenate([zero, u[:, :, :-1]], axis=2)
    xp = jnp.concatenate([u[:, :, 1:], zero], axis=2)
    return zm, zp, ym, yp, xm, xp


def n_face_set(eta):
    zm, zp, ym, yp, xm, xp = n_neighbours(eta)
    zlo = VERT * (0.5 * (eta + zm))
    zhi = VERT * (0.5 * (eta + zp))
    ylo = 0.5 * (eta + ym)
    yhi = 0.5 * (eta + yp)
    xlo = 0.5 * (eta + xm)
    xhi = 0.5 * (eta + xp)
    return (zlo, zhi, ylo, yhi, xlo, xhi)


def n_operate(u, coef):
    zlo, zhi, ylo, yhi, xlo, xhi, extra = coef
    zm, zp, ym, yp, xm, xp = n_neighbours(u)
    out = zlo * (u - zm) + zhi * (u - zp)
    out = out + ylo * (u - ym) + yhi * (u - yp)
    out = out + xlo * (u - xm) + xhi * (u - xp)
    return out + extra * u


def n_diagonal(coef):
    zlo, zhi, ylo, yhi, xlo, xhi, extra = coef
    return zlo + zhi + ylo + yhi + xlo + xhi + extra


def n_pick_matrix(cols):
    half = cols // 2
    src = lax.broadcasted_iota(jnp.int32, (cols, cols), 0)
    dst = lax.broadcasted_iota(jnp.int32, (cols, cols), 1)
    want = jnp.where(dst < half, 2 * dst, 2 * (dst - half) + 1)
    return (src == want).astype(jnp.float32)


def n_split_x(a):
    cols = a.shape[-1]
    both = jnp.dot(a, n_pick_matrix(cols), precision=HI)
    return both[..., : cols // 2], both[..., cols // 2 :]


def n_mean_four(a):
    e0, o0 = n_split_x(a[:, 0::2])
    e1, o1 = n_split_x(a[:, 1::2])
    return 0.25 * (e0 + e1 + o0 + o1)


def n_coarsen(coef):
    zlo, zhi, ylo, yhi, xlo, xhi, extra = coef
    xlo_e, _ = n_split_x(xlo[:, 0::2] + xlo[:, 1::2])
    _, xhi_o = n_split_x(xhi[:, 0::2] + xhi[:, 1::2])
    ylo_e, ylo_o = n_split_x(ylo[:, 0::2])
    yhi_e, yhi_o = n_split_x(yhi[:, 1::2])
    cxlo = 0.125 * xlo_e
    cxhi = 0.125 * xhi_o
    cylo = 0.125 * (ylo_e + ylo_o)
    cyhi = 0.125 * (yhi_e + yhi_o)
    return (n_mean_four(zlo), n_mean_four(zhi), cylo, cyhi, cxlo, cxhi, n_mean_four(extra))


def n_prolong(field):
    cols = field.shape[-1]
    src = lax.broadcasted_iota(jnp.int32, (cols, 2 * cols), 0)
    dst = lax.broadcasted_iota(jnp.int32, (cols, 2 * cols), 1)
    spread = (src == dst // 2).astype(jnp.float32)
    wide = jnp.dot(field, spread, precision=HI)
    return jnp.repeat(wide, 2, axis=1)


def n_sweep(field, rhs, coef, diag):
    return field + OMEGA * (rhs - n_operate(field, coef)) / diag


def n_body(viscosity, adjoint_source, forward_velocity, friction, ice_mask, grounded_mask):
    layers = viscosity.shape[0]
    cols = viscosity.shape[2]
    half_cols = cols // 2
    gz = lax.axis_index("gz")
    total_layers = layers * lax.axis_size("gz")
    layer = (gz * layers + jnp.arange(layers)).astype(jnp.float32)
    profile = (jnp.float32(total_layers) - layer) / jnp.float32(total_layers)
    wsq = profile * profile
    icef = ice_mask.astype(jnp.float32)
    groundf = grounded_mask.astype(jnp.float32)
    base = 0.05 + 2.0 * (1.0 - icef)
    ground_fric = groundf * friction
    stacked = jnp.concatenate([viscosity, adjoint_source, base[None], ground_fric[None]], axis=0)
    gathered = lax.all_gather(stacked, "gx", axis=0, tiled=False)
    count_x = gathered.shape[0]
    gathered = jnp.concatenate([gathered[i] for i in range(count_x)], axis=2)
    visc_all = gathered[:layers]
    source_all = gathered[layers : 2 * layers]
    base_all = gathered[2 * layers]
    gfr_all = gathered[2 * layers + 1]
    extra = base_all[None, :, :] + gfr_all[None, :, :] * wsq[:, None, None]
    fine = n_face_set(visc_all) + (extra,)
    dfine = n_diagonal(fine)
    middle = n_coarsen(fine)
    dmid = n_diagonal(middle)
    coarse = n_coarsen(middle)
    dcoarse = n_diagonal(coarse)
    lam = OMEGA * source_all / dfine
    for i in range(S0 - 1):
        lam = n_sweep(lam, source_all, fine, dfine)
    b_mid = n_mean_four(source_all - n_operate(lam, fine))
    e_mid = OMEGA * b_mid / dmid
    for i in range(S1 - 1):
        e_mid = n_sweep(e_mid, b_mid, middle, dmid)
    b_low = n_mean_four(b_mid - n_operate(e_mid, middle))
    e_low = OMEGA * b_low / dcoarse
    for i in range(S2 - 1):
        e_low = n_sweep(e_low, b_low, coarse, dcoarse)
    e_mid = e_mid + n_prolong(e_low)
    for i in range(S1):
        e_mid = n_sweep(e_mid, b_mid, middle, dmid)
    lam = lam + n_prolong(e_mid)
    for i in range(S0):
        lam = n_sweep(lam, source_all, fine, dfine)
    own = lax.dynamic_slice_in_dim(lam, lax.axis_index("gx") * cols, cols, 2)
    column = jnp.sum(wsq[:, None, None] * forward_velocity * own, axis=0)
    summed = lax.psum(column, "gz")
    terms = -ground_fric * summed
    gradient = lax.dynamic_slice_in_dim(terms, gz * half_cols, half_cols, 1)
    return (own, gradient)


def body(viscosity, *rest):
    layers, own_rows, cols_own = viscosity.shape
    cols_all = cols_own * lax.axis_size("gx")
    wide_bytes = 4 * layers * (own_rows + 2 * FINE_HALO + 2) * cols_all
    if FINE_HALO + 1 <= own_rows and MID_HALO <= own_rows // 2 and 20 * wide_bytes <= 40 * 2**20 and lax.axis_size("gy") <= 8:
        return body_wide(viscosity, *rest)
    return n_body(viscosity, *rest)


def solution(mesh):
    placed = (
        P("gz", "gy", "gx"),
        P("gz", "gy", "gx"),
        P("gz", "gy", "gx"),
        P("gy", "gx"),
        P("gy", "gx"),
        P("gy", "gx"),
    )
    return jax.shard_map(
        body,
        mesh=mesh,
        in_specs=placed,
        out_specs=(P("gz", "gy", "gx"), P("gy", ("gx", "gz"))),
        check_vma=False,
    )
```

```python
import jax
import jax.numpy as jnp
from jax import lax
from jax.sharding import PartitionSpec as P

S0 = 4
S1 = 4
S2 = 8


OMEGA = 0.8
VERT = 4.0
HI = lax.Precision.HIGHEST
FINE_HALO = 12
MID_HALO = 6
POST_HALO = 4
COL_HALO = 64


def layer_halos(u):
    count = lax.axis_size("gz")
    head = u[:1]
    tail = u[-1:]
    if count == 2:
        first = lax.axis_index("gz") == 0
        got = lax.ppermute(jnp.where(first, tail, head), "gz", [(0, 1), (1, 0)])
        zero = jnp.zeros_like(got)
        return jnp.where(first, zero, got), jnp.where(first, got, zero)
    lo = lax.ppermute(tail, "gz", [(i, i + 1) for i in range(count - 1)])
    hi = lax.ppermute(head, "gz", [(i + 1, i) for i in range(count - 1)])
    return lo, hi


def extend_rows(a, h):
    count = lax.axis_size("gy")
    lo = lax.ppermute(a[:, -h:], "gy", [(i, i + 1) for i in range(count - 1)])
    hi = lax.ppermute(a[:, :h], "gy", [(i + 1, i) for i in range(count - 1)])
    return jnp.concatenate([lo, a, hi], axis=1)


def gather_blocks(a, axis):
    count = lax.axis_size(axis)
    got = [a]
    for s in range(1, count):
        got.append(lax.ppermute(a, axis, [(i, (i + s) % count) for i in range(count)]))
    rev = jnp.stack(got[::-1], axis=0)
    return jnp.roll(rev, lax.axis_index(axis) + 1, axis=0)


def extend_cols(a, h):
    count = lax.axis_size("gx")
    lo = lax.ppermute(a[:, :, -h:], "gx", [(i, i + 1) for i in range(count - 1)])
    hi = lax.ppermute(a[:, :, :h], "gx", [(i + 1, i) for i in range(count - 1)])
    return jnp.concatenate([lo, a, hi], axis=2)


def col_mask(own_cols, h):
    g = lax.axis_index("gx") * own_cols - h + lax.broadcasted_iota(jnp.int32, (1, 1, own_cols + 2 * h), 2)
    return (g >= 0) & (g < own_cols * lax.axis_size("gx"))


def crop(a, h_from, h_to):
    cut = h_from - h_to
    return a[:, cut : a.shape[1] - cut]


def row_mask(own_rows, h):
    g = lax.axis_index("gy") * own_rows - h + lax.broadcasted_iota(jnp.int32, (1, own_rows + 2 * h, 1), 1)
    return (g >= 0) & (g < own_rows * lax.axis_size("gy"))


def neighbours(u):
    zlo, zhi = layer_halos(u)
    zero_row = jnp.zeros_like(u[:, :1])
    zero_col = jnp.zeros_like(u[:, :, :1])
    zm = jnp.concatenate([zlo, u[:-1]], axis=0)
    zp = jnp.concatenate([u[1:], zhi], axis=0)
    ym = jnp.concatenate([zero_row, u[:, :-1]], axis=1)
    yp = jnp.concatenate([u[:, 1:], zero_row], axis=1)
    xm = jnp.concatenate([zero_col, u[:, :, :-1]], axis=2)
    xp = jnp.concatenate([u[:, :, 1:], zero_col], axis=2)
    return zm, zp, ym, yp, xm, xp


def face_set(eta):
    zm, zp, ym, yp, xm, xp = neighbours(eta)
    zlo = VERT * (0.5 * (eta + zm))
    zhi = VERT * (0.5 * (eta + zp))
    ylo = 0.5 * (eta + ym)
    yhi = 0.5 * (eta + yp)
    xlo = 0.5 * (eta + xm)
    xhi = 0.5 * (eta + xp)
    return (zlo, zhi, ylo, yhi, xlo, xhi)


def operate(u, coef):
    zlo, zhi, ylo, yhi, xlo, xhi, extra = coef
    zm, zp, ym, yp, xm, xp = neighbours(u)
    out = zlo * (u - zm) + zhi * (u - zp)
    out = out + ylo * (u - ym) + yhi * (u - yp)
    out = out + xlo * (u - xm) + xhi * (u - xp)
    return out + extra * u


def diagonal(coef):
    zlo, zhi, ylo, yhi, xlo, xhi, extra = coef
    return zlo + zhi + ylo + yhi + xlo + xhi + extra


def pick(n, parity):
    src = lax.broadcasted_iota(jnp.int32, (n, n // 2), 0)
    dst = lax.broadcasted_iota(jnp.int32, (n, n // 2), 1)
    return (src == 2 * dst + parity).astype(jnp.float32)


def cols(a, parity):
    return jnp.dot(a, pick(a.shape[-1], parity), precision=HI)


def rows(a, parity):
    return jnp.einsum("yr,zyx->zrx", pick(a.shape[1], parity), a, precision=HI)


def mean_four(a):
    r0 = rows(a, 0)
    r1 = rows(a, 1)
    return 0.25 * (cols(r0, 0) + cols(r1, 0) + cols(r0, 1) + cols(r1, 1))


def coarsen(coef):
    zlo, zhi, ylo, yhi, xlo, xhi, extra = coef
    cxlo = 0.125 * cols(rows(xlo, 0) + rows(xlo, 1), 0)
    cxhi = 0.125 * cols(rows(xhi, 0) + rows(xhi, 1), 1)
    ylo0 = rows(ylo, 0)
    yhi1 = rows(yhi, 1)
    cylo = 0.125 * (cols(ylo0, 0) + cols(ylo0, 1))
    cyhi = 0.125 * (cols(yhi1, 0) + cols(yhi1, 1))
    return (mean_four(zlo), mean_four(zhi), cylo, cyhi, cxlo, cxhi, mean_four(extra))


def spread(n):
    src = lax.broadcasted_iota(jnp.int32, (n, 2 * n), 0)
    dst = lax.broadcasted_iota(jnp.int32, (n, 2 * n), 1)
    return (src == dst // 2).astype(jnp.float32)


def prolong(field):
    wide = jnp.dot(field, spread(field.shape[-1]), precision=HI)
    return jnp.einsum("ry,zrx->zyx", spread(field.shape[1]), wide, precision=HI)


def sweep(field, rhs, coef, diag, inside):
    new = field + OMEGA * (rhs - operate(field, coef)) / diag
    return jnp.where(inside, new, 0.0)


def smooth(field, rhs, coef, diag, inside, count):
    for i in range(count):
        field = sweep(field, rhs, coef, diag, inside)
    return field


def crop_all(arrs, h_from, h_to):
    return tuple(crop(a, h_from, h_to) for a in arrs)


def body_wide(viscosity, adjoint_source, forward_velocity, friction, ice_mask, grounded_mask):
    layers = viscosity.shape[0]
    own_rows = viscosity.shape[1]
    mid_rows = own_rows // 2
    cols_own = viscosity.shape[2]
    half_cols = cols_own // 2
    gz = lax.axis_index("gz")
    gy = lax.axis_index("gy")
    total_layers = layers * lax.axis_size("gz")
    layer = (gz * layers + jnp.arange(layers)).astype(jnp.float32)
    profile = (jnp.float32(total_layers) - layer) / jnp.float32(total_layers)
    wsq = profile * profile
    icef = ice_mask.astype(jnp.float32)
    groundf = grounded_mask.astype(jnp.float32)
    base = 0.05 + 2.0 * (1.0 - icef)
    ground_fric = groundf * friction
    stacked = jnp.concatenate([viscosity, adjoint_source, base[None], ground_fric[None]], axis=0)
    hv = FINE_HALO + 1
    ext = extend_rows(extend_cols(stacked, COL_HALO), hv)
    visc_e = ext[:layers]
    src_e = crop(ext[layers : 2 * layers], hv, FINE_HALO)
    base_e = crop(ext[2 * layers : 2 * layers + 1], hv, FINE_HALO)[0]
    gfr_e = crop(ext[2 * layers + 1 : 2 * layers + 2], hv, FINE_HALO)[0]
    extra = base_e[None, :, :] + gfr_e[None, :, :] * wsq[:, None, None]
    fine = crop_all(face_set(visc_e), hv, FINE_HALO) + (extra,)
    dfine = diagonal(fine)
    middle = coarsen(fine)
    dmid = diagonal(middle)
    coarse_own = coarsen(crop_all(middle, FINE_HALO // 2, 0))
    coarse_all = gather_blocks(jnp.concatenate(coarse_own, axis=0), "gy")
    coarse_all = jnp.concatenate([coarse_all[i] for i in range(coarse_all.shape[0])], axis=1)
    coarse = tuple(coarse_all[i * layers : (i + 1) * layers] for i in range(7))
    dcoarse = diagonal(coarse)
    in_fine = row_mask(own_rows, FINE_HALO) & col_mask(cols_own, COL_HALO)
    in_mid = row_mask(mid_rows, FINE_HALO // 2) & col_mask(cols_own // 2, COL_HALO // 2)

    lam = jnp.where(in_fine, OMEGA * src_e / dfine, 0.0)
    lam = smooth(lam, src_e, fine, dfine, in_fine, S0 - 1)
    b_mid = mean_four(src_e - operate(lam, fine))
    e_mid = jnp.where(in_mid, OMEGA * b_mid / dmid, 0.0)
    e_mid = smooth(e_mid, b_mid, middle, dmid, in_mid, S1 - 1)
    hm = FINE_HALO // 2
    res_mid = crop(b_mid - operate(e_mid, middle), hm, 0)
    b_low = gather_blocks(mean_four(res_mid), "gy")
    b_low = jnp.concatenate([b_low[i] for i in range(b_low.shape[0])], axis=1)
    ones = col_mask(cols_own // 4, COL_HALO // 4)
    e_low = jnp.where(ones, OMEGA * b_low / dcoarse, 0.0)
    e_low = smooth(e_low, b_low, coarse, dcoarse, ones, S2 - 1)

    pair = jnp.concatenate([crop(e_mid, hm, 0), crop(b_mid, hm, 0)], axis=0)
    pair = extend_rows(pair, MID_HALO)
    e_mid = pair[:layers]
    b_mid = pair[layers:]
    low_rows = own_rows // 4
    ch = MID_HALO // 2
    padded = jnp.pad(e_low, ((0, 0), (ch, ch), (0, 0)))
    e_near = lax.dynamic_slice_in_dim(padded, gy * low_rows, low_rows + 2 * ch, 1)
    e_mid = e_mid + prolong(e_near)
    middle_p = crop_all(middle, hm, MID_HALO)
    dmid_p = crop(dmid, hm, MID_HALO)
    in_mid_p = row_mask(mid_rows, MID_HALO) & col_mask(cols_own // 2, COL_HALO // 2)
    e_mid = smooth(e_mid, b_mid, middle_p, dmid_p, in_mid_p, S1)

    lam = crop(lam, FINE_HALO, POST_HALO) + prolong(crop(e_mid, MID_HALO, POST_HALO // 2))
    fine_p = crop_all(fine, FINE_HALO, POST_HALO)
    dfine_p = crop(dfine, FINE_HALO, POST_HALO)
    src_p = crop(src_e, FINE_HALO, POST_HALO)
    in_fine_p = row_mask(own_rows, POST_HALO) & col_mask(cols_own, COL_HALO)
    lam = smooth(lam, src_p, fine_p, dfine_p, in_fine_p, S0)
    lam = crop(lam, POST_HALO, 0)

    own = lam[:, :, COL_HALO : COL_HALO + cols_own]
    column = jnp.sum(wsq[:, None, None] * forward_velocity * own, axis=0)
    summed = lax.psum(column, "gz")
    terms = -ground_fric * summed
    gradient = lax.dynamic_slice_in_dim(terms, gz * half_cols, half_cols, 1)
    return (own, gradient)


def n_layer_halos(u):
    count = lax.axis_size("gz")
    head = u[:1]
    tail = u[-1:]
    if count == 2:
        first = lax.axis_index("gz") == 0
        got = lax.ppermute(jnp.where(first, tail, head), "gz", [(0, 1), (1, 0)])
        zero = jnp.zeros_like(got)
        return jnp.where(first, zero, got), jnp.where(first, got, zero)
    lo = lax.ppermute(tail, "gz", [(i, i + 1) for i in range(count - 1)])
    hi = lax.ppermute(head, "gz", [(i + 1, i) for i in range(count - 1)])
    return lo, hi


def n_row_halos(u):
    count = lax.axis_size("gy")
    lo = lax.ppermute(u[:, -1:], "gy", [(i, i + 1) for i in range(count - 1)])
    hi = lax.ppermute(u[:, :1], "gy", [(i + 1, i) for i in range(count - 1)])
    return lo, hi


def n_neighbours(u):
    zlo, zhi = n_layer_halos(u)
    ylo, yhi = n_row_halos(u)
    zero = jnp.zeros_like(u[:, :, :1])
    zm = jnp.concatenate([zlo, u[:-1]], axis=0)
    zp = jnp.concatenate([u[1:], zhi], axis=0)
    ym = jnp.concatenate([ylo, u[:, :-1]], axis=1)
    yp = jnp.concatenate([u[:, 1:], yhi], axis=1)
    xm = jnp.concatenate([zero, u[:, :, :-1]], axis=2)
    xp = jnp.concatenate([u[:, :, 1:], zero], axis=2)
    return zm, zp, ym, yp, xm, xp


def n_face_set(eta):
    zm, zp, ym, yp, xm, xp = n_neighbours(eta)
    zlo = VERT * (0.5 * (eta + zm))
    zhi = VERT * (0.5 * (eta + zp))
    ylo = 0.5 * (eta + ym)
    yhi = 0.5 * (eta + yp)
    xlo = 0.5 * (eta + xm)
    xhi = 0.5 * (eta + xp)
    return (zlo, zhi, ylo, yhi, xlo, xhi)


def n_operate(u, coef):
    zlo, zhi, ylo, yhi, xlo, xhi, extra = coef
    zm, zp, ym, yp, xm, xp = n_neighbours(u)
    out = zlo * (u - zm) + zhi * (u - zp)
    out = out + ylo * (u - ym) + yhi * (u - yp)
    out = out + xlo * (u - xm) + xhi * (u - xp)
    return out + extra * u


def n_diagonal(coef):
    zlo, zhi, ylo, yhi, xlo, xhi, extra = coef
    return zlo + zhi + ylo + yhi + xlo + xhi + extra


def n_pick_matrix(cols):
    half = cols // 2
    src = lax.broadcasted_iota(jnp.int32, (cols, cols), 0)
    dst = lax.broadcasted_iota(jnp.int32, (cols, cols), 1)
    want = jnp.where(dst < half, 2 * dst, 2 * (dst - half) + 1)
    return (src == want).astype(jnp.float32)


def n_split_x(a):
    cols = a.shape[-1]
    both = jnp.dot(a, n_pick_matrix(cols), precision=HI)
    return both[..., : cols // 2], both[..., cols // 2 :]


def n_mean_four(a):
    e0, o0 = n_split_x(a[:, 0::2])
    e1, o1 = n_split_x(a[:, 1::2])
    return 0.25 * (e0 + e1 + o0 + o1)


def n_coarsen(coef):
    zlo, zhi, ylo, yhi, xlo, xhi, extra = coef
    xlo_e, _ = n_split_x(xlo[:, 0::2] + xlo[:, 1::2])
    _, xhi_o = n_split_x(xhi[:, 0::2] + xhi[:, 1::2])
    ylo_e, ylo_o = n_split_x(ylo[:, 0::2])
    yhi_e, yhi_o = n_split_x(yhi[:, 1::2])
    cxlo = 0.125 * xlo_e
    cxhi = 0.125 * xhi_o
    cylo = 0.125 * (ylo_e + ylo_o)
    cyhi = 0.125 * (yhi_e + yhi_o)
    return (n_mean_four(zlo), n_mean_four(zhi), cylo, cyhi, cxlo, cxhi, n_mean_four(extra))


def n_prolong(field):
    cols = field.shape[-1]
    src = lax.broadcasted_iota(jnp.int32, (cols, 2 * cols), 0)
    dst = lax.broadcasted_iota(jnp.int32, (cols, 2 * cols), 1)
    spread = (src == dst // 2).astype(jnp.float32)
    wide = jnp.dot(field, spread, precision=HI)
    return jnp.repeat(wide, 2, axis=1)


def n_sweep(field, rhs, coef, diag):
    return field + OMEGA * (rhs - n_operate(field, coef)) / diag


def n_body(viscosity, adjoint_source, forward_velocity, friction, ice_mask, grounded_mask):
    layers = viscosity.shape[0]
    cols = viscosity.shape[2]
    half_cols = cols // 2
    gz = lax.axis_index("gz")
    total_layers = layers * lax.axis_size("gz")
    layer = (gz * layers + jnp.arange(layers)).astype(jnp.float32)
    profile = (jnp.float32(total_layers) - layer) / jnp.float32(total_layers)
    wsq = profile * profile
    icef = ice_mask.astype(jnp.float32)
    groundf = grounded_mask.astype(jnp.float32)
    base = 0.05 + 2.0 * (1.0 - icef)
    ground_fric = groundf * friction
    stacked = jnp.concatenate([viscosity, adjoint_source, base[None], ground_fric[None]], axis=0)
    gathered = lax.all_gather(stacked, "gx", axis=0, tiled=False)
    count_x = gathered.shape[0]
    gathered = jnp.concatenate([gathered[i] for i in range(count_x)], axis=2)
    visc_all = gathered[:layers]
    source_all = gathered[layers : 2 * layers]
    base_all = gathered[2 * layers]
    gfr_all = gathered[2 * layers + 1]
    extra = base_all[None, :, :] + gfr_all[None, :, :] * wsq[:, None, None]
    fine = n_face_set(visc_all) + (extra,)
    dfine = n_diagonal(fine)
    middle = n_coarsen(fine)
    dmid = n_diagonal(middle)
    coarse = n_coarsen(middle)
    dcoarse = n_diagonal(coarse)
    lam = OMEGA * source_all / dfine
    for i in range(S0 - 1):
        lam = n_sweep(lam, source_all, fine, dfine)
    b_mid = n_mean_four(source_all - n_operate(lam, fine))
    e_mid = OMEGA * b_mid / dmid
    for i in range(S1 - 1):
        e_mid = n_sweep(e_mid, b_mid, middle, dmid)
    b_low = n_mean_four(b_mid - n_operate(e_mid, middle))
    e_low = OMEGA * b_low / dcoarse
    for i in range(S2 - 1):
        e_low = n_sweep(e_low, b_low, coarse, dcoarse)
    e_mid = e_mid + n_prolong(e_low)
    for i in range(S1):
        e_mid = n_sweep(e_mid, b_mid, middle, dmid)
    lam = lam + n_prolong(e_mid)
    for i in range(S0):
        lam = n_sweep(lam, source_all, fine, dfine)
    own = lax.dynamic_slice_in_dim(lam, lax.axis_index("gx") * cols, cols, 2)
    column = jnp.sum(wsq[:, None, None] * forward_velocity * own, axis=0)
    summed = lax.psum(column, "gz")
    terms = -ground_fric * summed
    gradient = lax.dynamic_slice_in_dim(terms, gz * half_cols, half_cols, 1)
    return (own, gradient)


def body(viscosity, *rest):
    layers, own_rows, cols_own = viscosity.shape
    cols_all = cols_own + 2 * COL_HALO
    wide_bytes = 4 * layers * (own_rows + 2 * FINE_HALO + 2) * cols_all
    if COL_HALO <= cols_own and FINE_HALO + 1 <= own_rows and MID_HALO <= own_rows // 2 and 20 * wide_bytes <= 40 * 2**20 and lax.axis_size("gy") <= 8:
        return body_wide(viscosity, *rest)
    return n_body(viscosity, *rest)


def solution(mesh):
    placed = (
        P("gz", "gy", "gx"),
        P("gz", "gy", "gx"),
        P("gz", "gy", "gx"),
        P("gy", "gx"),
        P("gy", "gx"),
        P("gy", "gx"),
    )
    return jax.shard_map(
        body,
        mesh=mesh,
        in_specs=placed,
        out_specs=(P("gz", "gy", "gx"), P("gy", ("gx", "gz"))),
        check_vma=False,
    )
```

```python
import jax
import jax.numpy as jnp
from jax import lax
from jax.sharding import PartitionSpec as P

S0 = 4
S1 = 4
S2 = 8


OMEGA = 0.8
VERT = 4.0
HI = lax.Precision.HIGHEST
FINE_HALO = 12
MID_HALO = 6
POST_HALO = 4
COL_HALO = 64


def layer_halos(u):
    count = lax.axis_size("gz")
    head = u[:1]
    tail = u[-1:]
    if count == 2:
        first = lax.axis_index("gz") == 0
        got = lax.ppermute(jnp.where(first, tail, head), "gz", [(0, 1), (1, 0)])
        zero = jnp.zeros_like(got)
        return jnp.where(first, zero, got), jnp.where(first, got, zero)
    lo = lax.ppermute(tail, "gz", [(i, i + 1) for i in range(count - 1)])
    hi = lax.ppermute(head, "gz", [(i + 1, i) for i in range(count - 1)])
    return lo, hi


def extend_rows(a, h):
    count = lax.axis_size("gy")
    lo = lax.ppermute(a[:, -h:], "gy", [(i, i + 1) for i in range(count - 1)])
    hi = lax.ppermute(a[:, :h], "gy", [(i + 1, i) for i in range(count - 1)])
    return jnp.concatenate([lo, a, hi], axis=1)


def gather_blocks(a, axis):
    count = lax.axis_size(axis)
    got = [a]
    for s in range(1, count):
        got.append(lax.ppermute(a, axis, [(i, (i + s) % count) for i in range(count)]))
    rev = jnp.stack(got[::-1], axis=0)
    return jnp.roll(rev, lax.axis_index(axis) + 1, axis=0)


def extend_cols(a, h):
    count = lax.axis_size("gx")
    lo = lax.ppermute(a[:, :, -h:], "gx", [(i, i + 1) for i in range(count - 1)])
    hi = lax.ppermute(a[:, :, :h], "gx", [(i + 1, i) for i in range(count - 1)])
    return jnp.concatenate([lo, a, hi], axis=2)


def extend_both(a, hr, hc):
    nx = lax.axis_size("gx")
    ny = lax.axis_size("gy")

    def shift(block, dx, dy):
        pairs = []
        for i in range(nx):
            for j in range(ny):
                if 0 <= i + dx < nx and 0 <= j + dy < ny:
                    pairs.append((i * ny + j, (i + dx) * ny + j + dy))
        return lax.ppermute(block, ("gx", "gy"), pairs)

    top, bottom = a[:, :hr], a[:, -hr:]
    left, right = a[:, :, :hc], a[:, :, -hc:]
    lo_rows = shift(bottom, 0, 1)
    hi_rows = shift(top, 0, -1)
    lo_cols = shift(right, 1, 0)
    hi_cols = shift(left, -1, 0)
    c_mm = shift(bottom[:, :, -hc:], 1, 1)
    c_pm = shift(bottom[:, :, :hc], -1, 1)
    c_mp = shift(top[:, :, -hc:], 1, -1)
    c_pp = shift(top[:, :, :hc], -1, -1)
    rows_lo = jnp.concatenate([c_mm, lo_rows, c_pm], axis=2)
    middle = jnp.concatenate([lo_cols, a, hi_cols], axis=2)
    rows_hi = jnp.concatenate([c_mp, hi_rows, c_pp], axis=2)
    return jnp.concatenate([rows_lo, middle, rows_hi], axis=1)


def col_mask(own_cols, h):
    g = lax.axis_index("gx") * own_cols - h + lax.broadcasted_iota(jnp.int32, (1, 1, own_cols + 2 * h), 2)
    return (g >= 0) & (g < own_cols * lax.axis_size("gx"))


def crop(a, h_from, h_to):
    cut = h_from - h_to
    return a[:, cut : a.shape[1] - cut]


def row_mask(own_rows, h):
    g = lax.axis_index("gy") * own_rows - h + lax.broadcasted_iota(jnp.int32, (1, own_rows + 2 * h, 1), 1)
    return (g >= 0) & (g < own_rows * lax.axis_size("gy"))


def neighbours(u):
    zlo, zhi = layer_halos(u)
    zero_row = jnp.zeros_like(u[:, :1])
    zero_col = jnp.zeros_like(u[:, :, :1])
    zm = jnp.concatenate([zlo, u[:-1]], axis=0)
    zp = jnp.concatenate([u[1:], zhi], axis=0)
    ym = jnp.concatenate([zero_row, u[:, :-1]], axis=1)
    yp = jnp.concatenate([u[:, 1:], zero_row], axis=1)
    xm = jnp.concatenate([zero_col, u[:, :, :-1]], axis=2)
    xp = jnp.concatenate([u[:, :, 1:], zero_col], axis=2)
    return zm, zp, ym, yp, xm, xp


def face_set(eta):
    zm, zp, ym, yp, xm, xp = neighbours(eta)
    zlo = VERT * (0.5 * (eta + zm))
    zhi = VERT * (0.5 * (eta + zp))
    ylo = 0.5 * (eta + ym)
    yhi = 0.5 * (eta + yp)
    xlo = 0.5 * (eta + xm)
    xhi = 0.5 * (eta + xp)
    return (zlo, zhi, ylo, yhi, xlo, xhi)


def operate(u, coef):
    zlo, zhi, ylo, yhi, xlo, xhi, extra = coef
    zm, zp, ym, yp, xm, xp = neighbours(u)
    out = zlo * (u - zm) + zhi * (u - zp)
    out = out + ylo * (u - ym) + yhi * (u - yp)
    out = out + xlo * (u - xm) + xhi * (u - xp)
    return out + extra * u


def diagonal(coef):
    zlo, zhi, ylo, yhi, xlo, xhi, extra = coef
    return zlo + zhi + ylo + yhi + xlo + xhi + extra


def pick(n, parity):
    src = lax.broadcasted_iota(jnp.int32, (n, n // 2), 0)
    dst = lax.broadcasted_iota(jnp.int32, (n, n // 2), 1)
    return (src == 2 * dst + parity).astype(jnp.float32)


def cols(a, parity):
    return jnp.dot(a, pick(a.shape[-1], parity), precision=HI)


def rows(a, parity):
    return jnp.einsum("yr,zyx->zrx", pick(a.shape[1], parity), a, precision=HI)


def mean_four(a):
    r0 = rows(a, 0)
    r1 = rows(a, 1)
    return 0.25 * (cols(r0, 0) + cols(r1, 0) + cols(r0, 1) + cols(r1, 1))


def coarsen(coef):
    zlo, zhi, ylo, yhi, xlo, xhi, extra = coef
    cxlo = 0.125 * cols(rows(xlo, 0) + rows(xlo, 1), 0)
    cxhi = 0.125 * cols(rows(xhi, 0) + rows(xhi, 1), 1)
    ylo0 = rows(ylo, 0)
    yhi1 = rows(yhi, 1)
    cylo = 0.125 * (cols(ylo0, 0) + cols(ylo0, 1))
    cyhi = 0.125 * (cols(yhi1, 0) + cols(yhi1, 1))
    return (mean_four(zlo), mean_four(zhi), cylo, cyhi, cxlo, cxhi, mean_four(extra))


def spread(n):
    src = lax.broadcasted_iota(jnp.int32, (n, 2 * n), 0)
    dst = lax.broadcasted_iota(jnp.int32, (n, 2 * n), 1)
    return (src == dst // 2).astype(jnp.float32)


def prolong(field):
    wide = jnp.dot(field, spread(field.shape[-1]), precision=HI)
    return jnp.einsum("ry,zrx->zyx", spread(field.shape[1]), wide, precision=HI)


def sweep(field, rhs, coef, diag, inside):
    new = field + OMEGA * (rhs - operate(field, coef)) / diag
    return jnp.where(inside, new, 0.0)


def smooth(field, rhs, coef, diag, inside, count):
    for i in range(count):
        field = sweep(field, rhs, coef, diag, inside)
    return field


def crop_all(arrs, h_from, h_to):
    return tuple(crop(a, h_from, h_to) for a in arrs)


def body_wide(viscosity, adjoint_source, forward_velocity, friction, ice_mask, grounded_mask):
    layers = viscosity.shape[0]
    own_rows = viscosity.shape[1]
    mid_rows = own_rows // 2
    cols_own = viscosity.shape[2]
    half_cols = cols_own // 2
    gz = lax.axis_index("gz")
    gy = lax.axis_index("gy")
    total_layers = layers * lax.axis_size("gz")
    layer = (gz * layers + jnp.arange(layers)).astype(jnp.float32)
    profile = (jnp.float32(total_layers) - layer) / jnp.float32(total_layers)
    wsq = profile * profile
    icef = ice_mask.astype(jnp.float32)
    groundf = grounded_mask.astype(jnp.float32)
    base = 0.05 + 2.0 * (1.0 - icef)
    ground_fric = groundf * friction
    stacked = jnp.concatenate([viscosity, adjoint_source, base[None], ground_fric[None]], axis=0)
    hv = FINE_HALO + 1
    ext = extend_both(stacked, hv, COL_HALO)
    visc_e = ext[:layers]
    src_e = crop(ext[layers : 2 * layers], hv, FINE_HALO)
    base_e = crop(ext[2 * layers : 2 * layers + 1], hv, FINE_HALO)[0]
    gfr_e = crop(ext[2 * layers + 1 : 2 * layers + 2], hv, FINE_HALO)[0]
    extra = base_e[None, :, :] + gfr_e[None, :, :] * wsq[:, None, None]
    fine = crop_all(face_set(visc_e), hv, FINE_HALO) + (extra,)
    dfine = diagonal(fine)
    middle = coarsen(fine)
    dmid = diagonal(middle)
    coarse_own = coarsen(crop_all(middle, FINE_HALO // 2, 0))
    coarse_all = gather_blocks(jnp.concatenate(coarse_own, axis=0), "gy")
    coarse_all = jnp.concatenate([coarse_all[i] for i in range(coarse_all.shape[0])], axis=1)
    coarse = tuple(coarse_all[i * layers : (i + 1) * layers] for i in range(7))
    dcoarse = diagonal(coarse)
    in_fine = row_mask(own_rows, FINE_HALO) & col_mask(cols_own, COL_HALO)
    in_mid = row_mask(mid_rows, FINE_HALO // 2) & col_mask(cols_own // 2, COL_HALO // 2)

    lam = jnp.where(in_fine, OMEGA * src_e / dfine, 0.0)
    lam = smooth(lam, src_e, fine, dfine, in_fine, S0 - 1)
    b_mid = mean_four(src_e - operate(lam, fine))
    e_mid = jnp.where(in_mid, OMEGA * b_mid / dmid, 0.0)
    e_mid = smooth(e_mid, b_mid, middle, dmid, in_mid, S1 - 1)
    hm = FINE_HALO // 2
    res_mid = crop(b_mid - operate(e_mid, middle), hm, 0)
    b_low = gather_blocks(mean_four(res_mid), "gy")
    b_low = jnp.concatenate([b_low[i] for i in range(b_low.shape[0])], axis=1)
    ones = col_mask(cols_own // 4, COL_HALO // 4)
    e_low = jnp.where(ones, OMEGA * b_low / dcoarse, 0.0)
    e_low = smooth(e_low, b_low, coarse, dcoarse, ones, S2 - 1)

    pair = jnp.concatenate([crop(e_mid, hm, 0), crop(b_mid, hm, 0)], axis=0)
    pair = extend_rows(pair, MID_HALO)
    e_mid = pair[:layers]
    b_mid = pair[layers:]
    low_rows = own_rows // 4
    ch = MID_HALO // 2
    padded = jnp.pad(e_low, ((0, 0), (ch, ch), (0, 0)))
    e_near = lax.dynamic_slice_in_dim(padded, gy * low_rows, low_rows + 2 * ch, 1)
    e_mid = e_mid + prolong(e_near)
    middle_p = crop_all(middle, hm, MID_HALO)
    dmid_p = crop(dmid, hm, MID_HALO)
    in_mid_p = row_mask(mid_rows, MID_HALO) & col_mask(cols_own // 2, COL_HALO // 2)
    e_mid = smooth(e_mid, b_mid, middle_p, dmid_p, in_mid_p, S1)

    lam = crop(lam, FINE_HALO, POST_HALO) + prolong(crop(e_mid, MID_HALO, POST_HALO // 2))
    fine_p = crop_all(fine, FINE_HALO, POST_HALO)
    dfine_p = crop(dfine, FINE_HALO, POST_HALO)
    src_p = crop(src_e, FINE_HALO, POST_HALO)
    in_fine_p = row_mask(own_rows, POST_HALO) & col_mask(cols_own, COL_HALO)
    lam = smooth(lam, src_p, fine_p, dfine_p, in_fine_p, S0)
    lam = crop(lam, POST_HALO, 0)

    own = lam[:, :, COL_HALO : COL_HALO + cols_own]
    column = jnp.sum(wsq[:, None, None] * forward_velocity * own, axis=0)
    parts = gather_blocks(column, "gz")
    summed = parts[0]
    for k in range(1, parts.shape[0]):
        summed = summed + parts[k]
    terms = -ground_fric * summed
    gradient = lax.dynamic_slice_in_dim(terms, gz * half_cols, half_cols, 1)
    return (own, gradient)


def n_layer_halos(u):
    count = lax.axis_size("gz")
    head = u[:1]
    tail = u[-1:]
    if count == 2:
        first = lax.axis_index("gz") == 0
        got = lax.ppermute(jnp.where(first, tail, head), "gz", [(0, 1), (1, 0)])
        zero = jnp.zeros_like(got)
        return jnp.where(first, zero, got), jnp.where(first, got, zero)
    lo = lax.ppermute(tail, "gz", [(i, i + 1) for i in range(count - 1)])
    hi = lax.ppermute(head, "gz", [(i + 1, i) for i in range(count - 1)])
    return lo, hi


def n_row_halos(u):
    count = lax.axis_size("gy")
    lo = lax.ppermute(u[:, -1:], "gy", [(i, i + 1) for i in range(count - 1)])
    hi = lax.ppermute(u[:, :1], "gy", [(i + 1, i) for i in range(count - 1)])
    return lo, hi


def n_neighbours(u):
    zlo, zhi = n_layer_halos(u)
    ylo, yhi = n_row_halos(u)
    zero = jnp.zeros_like(u[:, :, :1])
    zm = jnp.concatenate([zlo, u[:-1]], axis=0)
    zp = jnp.concatenate([u[1:], zhi], axis=0)
    ym = jnp.concatenate([ylo, u[:, :-1]], axis=1)
    yp = jnp.concatenate([u[:, 1:], yhi], axis=1)
    xm = jnp.concatenate([zero, u[:, :, :-1]], axis=2)
    xp = jnp.concatenate([u[:, :, 1:], zero], axis=2)
    return zm, zp, ym, yp, xm, xp


def n_face_set(eta):
    zm, zp, ym, yp, xm, xp = n_neighbours(eta)
    zlo = VERT * (0.5 * (eta + zm))
    zhi = VERT * (0.5 * (eta + zp))
    ylo = 0.5 * (eta + ym)
    yhi = 0.5 * (eta + yp)
    xlo = 0.5 * (eta + xm)
    xhi = 0.5 * (eta + xp)
    return (zlo, zhi, ylo, yhi, xlo, xhi)


def n_operate(u, coef):
    zlo, zhi, ylo, yhi, xlo, xhi, extra = coef
    zm, zp, ym, yp, xm, xp = n_neighbours(u)
    out = zlo * (u - zm) + zhi * (u - zp)
    out = out + ylo * (u - ym) + yhi * (u - yp)
    out = out + xlo * (u - xm) + xhi * (u - xp)
    return out + extra * u


def n_diagonal(coef):
    zlo, zhi, ylo, yhi, xlo, xhi, extra = coef
    return zlo + zhi + ylo + yhi + xlo + xhi + extra


def n_pick_matrix(cols):
    half = cols // 2
    src = lax.broadcasted_iota(jnp.int32, (cols, cols), 0)
    dst = lax.broadcasted_iota(jnp.int32, (cols, cols), 1)
    want = jnp.where(dst < half, 2 * dst, 2 * (dst - half) + 1)
    return (src == want).astype(jnp.float32)


def n_split_x(a):
    cols = a.shape[-1]
    both = jnp.dot(a, n_pick_matrix(cols), precision=HI)
    return both[..., : cols // 2], both[..., cols // 2 :]


def n_mean_four(a):
    e0, o0 = n_split_x(a[:, 0::2])
    e1, o1 = n_split_x(a[:, 1::2])
    return 0.25 * (e0 + e1 + o0 + o1)


def n_coarsen(coef):
    zlo, zhi, ylo, yhi, xlo, xhi, extra = coef
    xlo_e, _ = n_split_x(xlo[:, 0::2] + xlo[:, 1::2])
    _, xhi_o = n_split_x(xhi[:, 0::2] + xhi[:, 1::2])
    ylo_e, ylo_o = n_split_x(ylo[:, 0::2])
    yhi_e, yhi_o = n_split_x(yhi[:, 1::2])
    cxlo = 0.125 * xlo_e
    cxhi = 0.125 * xhi_o
    cylo = 0.125 * (ylo_e + ylo_o)
    cyhi = 0.125 * (yhi_e + yhi_o)
    return (n_mean_four(zlo), n_mean_four(zhi), cylo, cyhi, cxlo, cxhi, n_mean_four(extra))


def n_prolong(field):
    cols = field.shape[-1]
    src = lax.broadcasted_iota(jnp.int32, (cols, 2 * cols), 0)
    dst = lax.broadcasted_iota(jnp.int32, (cols, 2 * cols), 1)
    spread = (src == dst // 2).astype(jnp.float32)
    wide = jnp.dot(field, spread, precision=HI)
    return jnp.repeat(wide, 2, axis=1)


def n_sweep(field, rhs, coef, diag):
    return field + OMEGA * (rhs - n_operate(field, coef)) / diag


def n_body(viscosity, adjoint_source, forward_velocity, friction, ice_mask, grounded_mask):
    layers = viscosity.shape[0]
    cols = viscosity.shape[2]
    half_cols = cols // 2
    gz = lax.axis_index("gz")
    total_layers = layers * lax.axis_size("gz")
    layer = (gz * layers + jnp.arange(layers)).astype(jnp.float32)
    profile = (jnp.float32(total_layers) - layer) / jnp.float32(total_layers)
    wsq = profile * profile
    icef = ice_mask.astype(jnp.float32)
    groundf = grounded_mask.astype(jnp.float32)
    base = 0.05 + 2.0 * (1.0 - icef)
    ground_fric = groundf * friction
    stacked = jnp.concatenate([viscosity, adjoint_source, base[None], ground_fric[None]], axis=0)
    gathered = lax.all_gather(stacked, "gx", axis=0, tiled=False)
    count_x = gathered.shape[0]
    gathered = jnp.concatenate([gathered[i] for i in range(count_x)], axis=2)
    visc_all = gathered[:layers]
    source_all = gathered[layers : 2 * layers]
    base_all = gathered[2 * layers]
    gfr_all = gathered[2 * layers + 1]
    extra = base_all[None, :, :] + gfr_all[None, :, :] * wsq[:, None, None]
    fine = n_face_set(visc_all) + (extra,)
    dfine = n_diagonal(fine)
    middle = n_coarsen(fine)
    dmid = n_diagonal(middle)
    coarse = n_coarsen(middle)
    dcoarse = n_diagonal(coarse)
    lam = OMEGA * source_all / dfine
    for i in range(S0 - 1):
        lam = n_sweep(lam, source_all, fine, dfine)
    b_mid = n_mean_four(source_all - n_operate(lam, fine))
    e_mid = OMEGA * b_mid / dmid
    for i in range(S1 - 1):
        e_mid = n_sweep(e_mid, b_mid, middle, dmid)
    b_low = n_mean_four(b_mid - n_operate(e_mid, middle))
    e_low = OMEGA * b_low / dcoarse
    for i in range(S2 - 1):
        e_low = n_sweep(e_low, b_low, coarse, dcoarse)
    e_mid = e_mid + n_prolong(e_low)
    for i in range(S1):
        e_mid = n_sweep(e_mid, b_mid, middle, dmid)
    lam = lam + n_prolong(e_mid)
    for i in range(S0):
        lam = n_sweep(lam, source_all, fine, dfine)
    own = lax.dynamic_slice_in_dim(lam, lax.axis_index("gx") * cols, cols, 2)
    column = jnp.sum(wsq[:, None, None] * forward_velocity * own, axis=0)
    summed = lax.psum(column, "gz")
    terms = -ground_fric * summed
    gradient = lax.dynamic_slice_in_dim(terms, gz * half_cols, half_cols, 1)
    return (own, gradient)


def body(viscosity, *rest):
    layers, own_rows, cols_own = viscosity.shape
    cols_all = cols_own + 2 * COL_HALO
    wide_bytes = 4 * layers * (own_rows + 2 * FINE_HALO + 2) * cols_all
    if COL_HALO <= cols_own and FINE_HALO + 1 <= own_rows and MID_HALO <= own_rows // 2 and 20 * wide_bytes <= 40 * 2**20 and lax.axis_size("gy") <= 8:
        return body_wide(viscosity, *rest)
    return n_body(viscosity, *rest)


def solution(mesh):
    placed = (
        P("gz", "gy", "gx"),
        P("gz", "gy", "gx"),
        P("gz", "gy", "gx"),
        P("gy", "gx"),
        P("gy", "gx"),
        P("gy", "gx"),
    )
    return jax.shard_map(
        body,
        mesh=mesh,
        in_specs=placed,
        out_specs=(P("gz", "gy", "gx"), P("gy", ("gx", "gz"))),
        check_vma=False,
    )
```

```python
import jax
import jax.numpy as jnp
from jax import lax
from jax.sharding import PartitionSpec as P

S0 = 4
S1 = 4
S2 = 8


OMEGA = 0.8
VERT = 4.0
HI = lax.Precision.HIGHEST
FINE_HALO = 12
MID_HALO = 6
POST_HALO = 4
COL_HALO = 64


def layer_halos(u):
    count = lax.axis_size("gz")
    head = u[:1]
    tail = u[-1:]
    if count == 2:
        first = lax.axis_index("gz") == 0
        got = lax.ppermute(jnp.where(first, tail, head), "gz", [(0, 1), (1, 0)])
        zero = jnp.zeros_like(got)
        return jnp.where(first, zero, got), jnp.where(first, got, zero)
    lo = lax.ppermute(tail, "gz", [(i, i + 1) for i in range(count - 1)])
    hi = lax.ppermute(head, "gz", [(i + 1, i) for i in range(count - 1)])
    return lo, hi


def extend_rows(a, h):
    count = lax.axis_size("gy")
    lo = lax.ppermute(a[:, -h:], "gy", [(i, i + 1) for i in range(count - 1)])
    hi = lax.ppermute(a[:, :h], "gy", [(i + 1, i) for i in range(count - 1)])
    return jnp.concatenate([lo, a, hi], axis=1)


def gather_blocks(a, axis):
    count = lax.axis_size(axis)
    got = [a]
    for s in range(1, count):
        got.append(lax.ppermute(a, axis, [(i, (i + s) % count) for i in range(count)]))
    rev = jnp.stack(got[::-1], axis=0)
    return jnp.roll(rev, lax.axis_index(axis) + 1, axis=0)


def extend_cols(a, h):
    count = lax.axis_size("gx")
    lo = lax.ppermute(a[:, :, -h:], "gx", [(i, i + 1) for i in range(count - 1)])
    hi = lax.ppermute(a[:, :, :h], "gx", [(i + 1, i) for i in range(count - 1)])
    return jnp.concatenate([lo, a, hi], axis=2)


def col_mask(own_cols, h):
    g = lax.axis_index("gx") * own_cols - h + lax.broadcasted_iota(jnp.int32, (1, 1, own_cols + 2 * h), 2)
    return (g >= 0) & (g < own_cols * lax.axis_size("gx"))


def crop(a, h_from, h_to):
    cut = h_from - h_to
    return a[:, cut : a.shape[1] - cut]


def row_mask(own_rows, h):
    g = lax.axis_index("gy") * own_rows - h + lax.broadcasted_iota(jnp.int32, (1, own_rows + 2 * h, 1), 1)
    return (g >= 0) & (g < own_rows * lax.axis_size("gy"))


def neighbours(u):
    zlo, zhi = layer_halos(u)
    zero_row = jnp.zeros_like(u[:, :1])
    zero_col = jnp.zeros_like(u[:, :, :1])
    zm = jnp.concatenate([zlo, u[:-1]], axis=0)
    zp = jnp.concatenate([u[1:], zhi], axis=0)
    ym = jnp.concatenate([zero_row, u[:, :-1]], axis=1)
    yp = jnp.concatenate([u[:, 1:], zero_row], axis=1)
    xm = jnp.concatenate([zero_col, u[:, :, :-1]], axis=2)
    xp = jnp.concatenate([u[:, :, 1:], zero_col], axis=2)
    return zm, zp, ym, yp, xm, xp


def face_set(eta):
    zm, zp, ym, yp, xm, xp = neighbours(eta)
    zlo = VERT * (0.5 * (eta + zm))
    zhi = VERT * (0.5 * (eta + zp))
    ylo = 0.5 * (eta + ym)
    yhi = 0.5 * (eta + yp)
    xlo = 0.5 * (eta + xm)
    xhi = 0.5 * (eta + xp)
    return (zlo, zhi, ylo, yhi, xlo, xhi)


def operate(u, coef):
    zlo, zhi, ylo, yhi, xlo, xhi, extra = coef
    zm, zp, ym, yp, xm, xp = neighbours(u)
    out = zlo * (u - zm) + zhi * (u - zp)
    out = out + ylo * (u - ym) + yhi * (u - yp)
    out = out + xlo * (u - xm) + xhi * (u - xp)
    return out + extra * u


def diagonal(coef):
    zlo, zhi, ylo, yhi, xlo, xhi, extra = coef
    return zlo + zhi + ylo + yhi + xlo + xhi + extra


def pick(n, parity):
    src = lax.broadcasted_iota(jnp.int32, (n, n // 2), 0)
    dst = lax.broadcasted_iota(jnp.int32, (n, n // 2), 1)
    return (src == 2 * dst + parity).astype(jnp.float32)


def cols(a, parity):
    return jnp.dot(a, pick(a.shape[-1], parity), precision=HI)


def rows(a, parity):
    return jnp.einsum("yr,zyx->zrx", pick(a.shape[1], parity), a, precision=HI)


def mean_four(a):
    r0 = rows(a, 0)
    r1 = rows(a, 1)
    return 0.25 * (cols(r0, 0) + cols(r1, 0) + cols(r0, 1) + cols(r1, 1))


def coarsen(coef):
    zlo, zhi, ylo, yhi, xlo, xhi, extra = coef
    cxlo = 0.125 * cols(rows(xlo, 0) + rows(xlo, 1), 0)
    cxhi = 0.125 * cols(rows(xhi, 0) + rows(xhi, 1), 1)
    ylo0 = rows(ylo, 0)
    yhi1 = rows(yhi, 1)
    cylo = 0.125 * (cols(ylo0, 0) + cols(ylo0, 1))
    cyhi = 0.125 * (cols(yhi1, 0) + cols(yhi1, 1))
    return (mean_four(zlo), mean_four(zhi), cylo, cyhi, cxlo, cxhi, mean_four(extra))


def spread(n):
    src = lax.broadcasted_iota(jnp.int32, (n, 2 * n), 0)
    dst = lax.broadcasted_iota(jnp.int32, (n, 2 * n), 1)
    return (src == dst // 2).astype(jnp.float32)


def prolong(field):
    wide = jnp.dot(field, spread(field.shape[-1]), precision=HI)
    return jnp.einsum("ry,zrx->zyx", spread(field.shape[1]), wide, precision=HI)


def sweep(field, rhs, coef, diag, inside):
    new = field + OMEGA * (rhs - operate(field, coef)) / diag
    return jnp.where(inside, new, 0.0)


def smooth(field, rhs, coef, diag, inside, count):
    return lax.fori_loop(0, count, lambda i, u: sweep(u, rhs, coef, diag, inside), field)


def crop_all(arrs, h_from, h_to):
    return tuple(crop(a, h_from, h_to) for a in arrs)


def body_wide(viscosity, adjoint_source, forward_velocity, friction, ice_mask, grounded_mask):
    layers = viscosity.shape[0]
    own_rows = viscosity.shape[1]
    mid_rows = own_rows // 2
    cols_own = viscosity.shape[2]
    half_cols = cols_own // 2
    gz = lax.axis_index("gz")
    gy = lax.axis_index("gy")
    total_layers = layers * lax.axis_size("gz")
    layer = (gz * layers + jnp.arange(layers)).astype(jnp.float32)
    profile = (jnp.float32(total_layers) - layer) / jnp.float32(total_layers)
    wsq = profile * profile
    icef = ice_mask.astype(jnp.float32)
    groundf = grounded_mask.astype(jnp.float32)
    base = 0.05 + 2.0 * (1.0 - icef)
    ground_fric = groundf * friction
    stacked = jnp.concatenate([viscosity, adjoint_source, base[None], ground_fric[None]], axis=0)
    hv = FINE_HALO + 1
    ext = extend_rows(extend_cols(stacked, COL_HALO), hv)
    visc_e = ext[:layers]
    src_e = crop(ext[layers : 2 * layers], hv, FINE_HALO)
    base_e = crop(ext[2 * layers : 2 * layers + 1], hv, FINE_HALO)[0]
    gfr_e = crop(ext[2 * layers + 1 : 2 * layers + 2], hv, FINE_HALO)[0]
    extra = base_e[None, :, :] + gfr_e[None, :, :] * wsq[:, None, None]
    fine = crop_all(face_set(visc_e), hv, FINE_HALO) + (extra,)
    dfine = diagonal(fine)
    middle = coarsen(fine)
    dmid = diagonal(middle)
    coarse_own = coarsen(crop_all(middle, FINE_HALO // 2, 0))
    coarse_all = gather_blocks(jnp.concatenate(coarse_own, axis=0), "gy")
    coarse_all = jnp.concatenate([coarse_all[i] for i in range(coarse_all.shape[0])], axis=1)
    coarse = tuple(coarse_all[i * layers : (i + 1) * layers] for i in range(7))
    dcoarse = diagonal(coarse)
    in_fine = row_mask(own_rows, FINE_HALO) & col_mask(cols_own, COL_HALO)
    in_mid = row_mask(mid_rows, FINE_HALO // 2) & col_mask(cols_own // 2, COL_HALO // 2)

    lam = jnp.where(in_fine, OMEGA * src_e / dfine, 0.0)
    lam = smooth(lam, src_e, fine, dfine, in_fine, S0 - 1)
    b_mid = mean_four(src_e - operate(lam, fine))
    e_mid = jnp.where(in_mid, OMEGA * b_mid / dmid, 0.0)
    e_mid = smooth(e_mid, b_mid, middle, dmid, in_mid, S1 - 1)
    hm = FINE_HALO // 2
    res_mid = crop(b_mid - operate(e_mid, middle), hm, 0)
    b_low = gather_blocks(mean_four(res_mid), "gy")
    b_low = jnp.concatenate([b_low[i] for i in range(b_low.shape[0])], axis=1)
    ones = col_mask(cols_own // 4, COL_HALO // 4)
    e_low = jnp.where(ones, OMEGA * b_low / dcoarse, 0.0)
    e_low = smooth(e_low, b_low, coarse, dcoarse, ones, S2 - 1)

    pair = jnp.concatenate([crop(e_mid, hm, 0), crop(b_mid, hm, 0)], axis=0)
    pair = extend_rows(pair, MID_HALO)
    e_mid = pair[:layers]
    b_mid = pair[layers:]
    low_rows = own_rows // 4
    ch = MID_HALO // 2
    padded = jnp.pad(e_low, ((0, 0), (ch, ch), (0, 0)))
    e_near = lax.dynamic_slice_in_dim(padded, gy * low_rows, low_rows + 2 * ch, 1)
    e_mid = e_mid + prolong(e_near)
    middle_p = crop_all(middle, hm, MID_HALO)
    dmid_p = crop(dmid, hm, MID_HALO)
    in_mid_p = row_mask(mid_rows, MID_HALO) & col_mask(cols_own // 2, COL_HALO // 2)
    e_mid = smooth(e_mid, b_mid, middle_p, dmid_p, in_mid_p, S1)

    lam = crop(lam, FINE_HALO, POST_HALO) + prolong(crop(e_mid, MID_HALO, POST_HALO // 2))
    fine_p = crop_all(fine, FINE_HALO, POST_HALO)
    dfine_p = crop(dfine, FINE_HALO, POST_HALO)
    src_p = crop(src_e, FINE_HALO, POST_HALO)
    in_fine_p = row_mask(own_rows, POST_HALO) & col_mask(cols_own, COL_HALO)
    lam = smooth(lam, src_p, fine_p, dfine_p, in_fine_p, S0)
    lam = crop(lam, POST_HALO, 0)

    own = lam[:, :, COL_HALO : COL_HALO + cols_own]
    column = jnp.sum(wsq[:, None, None] * forward_velocity * own, axis=0)
    parts = gather_blocks(column, "gz")
    summed = parts[0]
    for k in range(1, parts.shape[0]):
        summed = summed + parts[k]
    terms = -ground_fric * summed
    gradient = lax.dynamic_slice_in_dim(terms, gz * half_cols, half_cols, 1)
    return (own, gradient)


def n_layer_halos(u):
    count = lax.axis_size("gz")
    head = u[:1]
    tail = u[-1:]
    if count == 2:
        first = lax.axis_index("gz") == 0
        got = lax.ppermute(jnp.where(first, tail, head), "gz", [(0, 1), (1, 0)])
        zero = jnp.zeros_like(got)
        return jnp.where(first, zero, got), jnp.where(first, got, zero)
    lo = lax.ppermute(tail, "gz", [(i, i + 1) for i in range(count - 1)])
    hi = lax.ppermute(head, "gz", [(i + 1, i) for i in range(count - 1)])
    return lo, hi


def n_row_halos(u):
    count = lax.axis_size("gy")
    lo = lax.ppermute(u[:, -1:], "gy", [(i, i + 1) for i in range(count - 1)])
    hi = lax.ppermute(u[:, :1], "gy", [(i + 1, i) for i in range(count - 1)])
    return lo, hi


def n_neighbours(u):
    zlo, zhi = n_layer_halos(u)
    ylo, yhi = n_row_halos(u)
    zero = jnp.zeros_like(u[:, :, :1])
    zm = jnp.concatenate([zlo, u[:-1]], axis=0)
    zp = jnp.concatenate([u[1:], zhi], axis=0)
    ym = jnp.concatenate([ylo, u[:, :-1]], axis=1)
    yp = jnp.concatenate([u[:, 1:], yhi], axis=1)
    xm = jnp.concatenate([zero, u[:, :, :-1]], axis=2)
    xp = jnp.concatenate([u[:, :, 1:], zero], axis=2)
    return zm, zp, ym, yp, xm, xp


def n_face_set(eta):
    zm, zp, ym, yp, xm, xp = n_neighbours(eta)
    zlo = VERT * (0.5 * (eta + zm))
    zhi = VERT * (0.5 * (eta + zp))
    ylo = 0.5 * (eta + ym)
    yhi = 0.5 * (eta + yp)
    xlo = 0.5 * (eta + xm)
    xhi = 0.5 * (eta + xp)
    return (zlo, zhi, ylo, yhi, xlo, xhi)


def n_operate(u, coef):
    zlo, zhi, ylo, yhi, xlo, xhi, extra = coef
    zm, zp, ym, yp, xm, xp = n_neighbours(u)
    out = zlo * (u - zm) + zhi * (u - zp)
    out = out + ylo * (u - ym) + yhi * (u - yp)
    out = out + xlo * (u - xm) + xhi * (u - xp)
    return out + extra * u


def n_diagonal(coef):
    zlo, zhi, ylo, yhi, xlo, xhi, extra = coef
    return zlo + zhi + ylo + yhi + xlo + xhi + extra


def n_pick_matrix(cols):
    half = cols // 2
    src = lax.broadcasted_iota(jnp.int32, (cols, cols), 0)
    dst = lax.broadcasted_iota(jnp.int32, (cols, cols), 1)
    want = jnp.where(dst < half, 2 * dst, 2 * (dst - half) + 1)
    return (src == want).astype(jnp.float32)


def n_split_x(a):
    cols = a.shape[-1]
    both = jnp.dot(a, n_pick_matrix(cols), precision=HI)
    return both[..., : cols // 2], both[..., cols // 2 :]


def n_mean_four(a):
    e0, o0 = n_split_x(a[:, 0::2])
    e1, o1 = n_split_x(a[:, 1::2])
    return 0.25 * (e0 + e1 + o0 + o1)


def n_coarsen(coef):
    zlo, zhi, ylo, yhi, xlo, xhi, extra = coef
    xlo_e, _ = n_split_x(xlo[:, 0::2] + xlo[:, 1::2])
    _, xhi_o = n_split_x(xhi[:, 0::2] + xhi[:, 1::2])
    ylo_e, ylo_o = n_split_x(ylo[:, 0::2])
    yhi_e, yhi_o = n_split_x(yhi[:, 1::2])
    cxlo = 0.125 * xlo_e
    cxhi = 0.125 * xhi_o
    cylo = 0.125 * (ylo_e + ylo_o)
    cyhi = 0.125 * (yhi_e + yhi_o)
    return (n_mean_four(zlo), n_mean_four(zhi), cylo, cyhi, cxlo, cxhi, n_mean_four(extra))


def n_prolong(field):
    cols = field.shape[-1]
    src = lax.broadcasted_iota(jnp.int32, (cols, 2 * cols), 0)
    dst = lax.broadcasted_iota(jnp.int32, (cols, 2 * cols), 1)
    spread = (src == dst // 2).astype(jnp.float32)
    wide = jnp.dot(field, spread, precision=HI)
    return jnp.repeat(wide, 2, axis=1)


def n_sweep(field, rhs, coef, diag):
    return field + OMEGA * (rhs - n_operate(field, coef)) / diag


def n_body(viscosity, adjoint_source, forward_velocity, friction, ice_mask, grounded_mask):
    layers = viscosity.shape[0]
    cols = viscosity.shape[2]
    half_cols = cols // 2
    gz = lax.axis_index("gz")
    total_layers = layers * lax.axis_size("gz")
    layer = (gz * layers + jnp.arange(layers)).astype(jnp.float32)
    profile = (jnp.float32(total_layers) - layer) / jnp.float32(total_layers)
    wsq = profile * profile
    icef = ice_mask.astype(jnp.float32)
    groundf = grounded_mask.astype(jnp.float32)
    base = 0.05 + 2.0 * (1.0 - icef)
    ground_fric = groundf * friction
    stacked = jnp.concatenate([viscosity, adjoint_source, base[None], ground_fric[None]], axis=0)
    gathered = lax.all_gather(stacked, "gx", axis=0, tiled=False)
    count_x = gathered.shape[0]
    gathered = jnp.concatenate([gathered[i] for i in range(count_x)], axis=2)
    visc_all = gathered[:layers]
    source_all = gathered[layers : 2 * layers]
    base_all = gathered[2 * layers]
    gfr_all = gathered[2 * layers + 1]
    extra = base_all[None, :, :] + gfr_all[None, :, :] * wsq[:, None, None]
    fine = n_face_set(visc_all) + (extra,)
    dfine = n_diagonal(fine)
    middle = n_coarsen(fine)
    dmid = n_diagonal(middle)
    coarse = n_coarsen(middle)
    dcoarse = n_diagonal(coarse)
    lam = OMEGA * source_all / dfine
    for i in range(S0 - 1):
        lam = n_sweep(lam, source_all, fine, dfine)
    b_mid = n_mean_four(source_all - n_operate(lam, fine))
    e_mid = OMEGA * b_mid / dmid
    for i in range(S1 - 1):
        e_mid = n_sweep(e_mid, b_mid, middle, dmid)
    b_low = n_mean_four(b_mid - n_operate(e_mid, middle))
    e_low = OMEGA * b_low / dcoarse
    for i in range(S2 - 1):
        e_low = n_sweep(e_low, b_low, coarse, dcoarse)
    e_mid = e_mid + n_prolong(e_low)
    for i in range(S1):
        e_mid = n_sweep(e_mid, b_mid, middle, dmid)
    lam = lam + n_prolong(e_mid)
    for i in range(S0):
        lam = n_sweep(lam, source_all, fine, dfine)
    own = lax.dynamic_slice_in_dim(lam, lax.axis_index("gx") * cols, cols, 2)
    column = jnp.sum(wsq[:, None, None] * forward_velocity * own, axis=0)
    summed = lax.psum(column, "gz")
    terms = -ground_fric * summed
    gradient = lax.dynamic_slice_in_dim(terms, gz * half_cols, half_cols, 1)
    return (own, gradient)


def body(viscosity, *rest):
    layers, own_rows, cols_own = viscosity.shape
    cols_all = cols_own + 2 * COL_HALO
    wide_bytes = 4 * layers * (own_rows + 2 * FINE_HALO + 2) * cols_all
    if COL_HALO <= cols_own and FINE_HALO + 1 <= own_rows and MID_HALO <= own_rows // 2 and 20 * wide_bytes <= 40 * 2**20 and lax.axis_size("gy") <= 8:
        return body_wide(viscosity, *rest)
    return n_body(viscosity, *rest)


def solution(mesh):
    placed = (
        P("gz", "gy", "gx"),
        P("gz", "gy", "gx"),
        P("gz", "gy", "gx"),
        P("gy", "gx"),
        P("gy", "gx"),
        P("gy", "gx"),
    )
    return jax.shard_map(
        body,
        mesh=mesh,
        in_specs=placed,
        out_specs=(P("gz", "gy", "gx"), P("gy", ("gx", "gz"))),
        check_vma=False,
    )
```

```python
import jax
import jax.numpy as jnp
from jax import lax
from jax.sharding import PartitionSpec as P

S0 = 4
S1 = 4
S2 = 8


OMEGA = 0.8
VERT = 4.0
HI = lax.Precision.HIGHEST
FINE_HALO = 12
MID_HALO = 6
POST_HALO = 4
COL_HALO = 64


def layer_halos(u):
    count = lax.axis_size("gz")
    head = u[:1]
    tail = u[-1:]
    if count == 2:
        first = lax.axis_index("gz") == 0
        got = lax.ppermute(jnp.where(first, tail, head), "gz", [(0, 1), (1, 0)])
        zero = jnp.zeros_like(got)
        return jnp.where(first, zero, got), jnp.where(first, got, zero)
    lo = lax.ppermute(tail, "gz", [(i, i + 1) for i in range(count - 1)])
    hi = lax.ppermute(head, "gz", [(i + 1, i) for i in range(count - 1)])
    return lo, hi


def extend_rows(a, h):
    count = lax.axis_size("gy")
    lo = lax.ppermute(a[:, -h:], "gy", [(i, i + 1) for i in range(count - 1)])
    hi = lax.ppermute(a[:, :h], "gy", [(i + 1, i) for i in range(count - 1)])
    return jnp.concatenate([lo, a, hi], axis=1)


def gather_blocks(a, axis):
    count = lax.axis_size(axis)
    got = [a]
    for s in range(1, count):
        got.append(lax.ppermute(a, axis, [(i, (i + s) % count) for i in range(count)]))
    rev = jnp.stack(got[::-1], axis=0)
    return jnp.roll(rev, lax.axis_index(axis) + 1, axis=0)


def extend_cols(a, h):
    count = lax.axis_size("gx")
    lo = lax.ppermute(a[:, :, -h:], "gx", [(i, i + 1) for i in range(count - 1)])
    hi = lax.ppermute(a[:, :, :h], "gx", [(i + 1, i) for i in range(count - 1)])
    return jnp.concatenate([lo, a, hi], axis=2)


def col_mask(own_cols, h):
    g = lax.axis_index("gx") * own_cols - h + lax.broadcasted_iota(jnp.int32, (1, 1, own_cols + 2 * h), 2)
    return (g >= 0) & (g < own_cols * lax.axis_size("gx"))


def crop(a, h_from, h_to):
    cut = h_from - h_to
    return a[:, cut : a.shape[1] - cut]


def row_mask(own_rows, h):
    g = lax.axis_index("gy") * own_rows - h + lax.broadcasted_iota(jnp.int32, (1, own_rows + 2 * h, 1), 1)
    return (g >= 0) & (g < own_rows * lax.axis_size("gy"))


def neighbours(u):
    zlo, zhi = layer_halos(u)
    zero_row = jnp.zeros_like(u[:, :1])
    zero_col = jnp.zeros_like(u[:, :, :1])
    zm = jnp.concatenate([zlo, u[:-1]], axis=0)
    zp = jnp.concatenate([u[1:], zhi], axis=0)
    ym = jnp.concatenate([zero_row, u[:, :-1]], axis=1)
    yp = jnp.concatenate([u[:, 1:], zero_row], axis=1)
    xm = jnp.concatenate([zero_col, u[:, :, :-1]], axis=2)
    xp = jnp.concatenate([u[:, :, 1:], zero_col], axis=2)
    return zm, zp, ym, yp, xm, xp


def face_set(eta):
    zm, zp, ym, yp, xm, xp = neighbours(eta)
    zlo = VERT * (0.5 * (eta + zm))
    zhi = VERT * (0.5 * (eta + zp))
    ylo = 0.5 * (eta + ym)
    yhi = 0.5 * (eta + yp)
    xlo = 0.5 * (eta + xm)
    xhi = 0.5 * (eta + xp)
    return (zlo, zhi, ylo, yhi, xlo, xhi)


def operate(u, coef):
    zlo, zhi, ylo, yhi, xlo, xhi, extra = coef
    zm, zp, ym, yp, xm, xp = neighbours(u)
    out = zlo * (u - zm) + zhi * (u - zp)
    out = out + ylo * (u - ym) + yhi * (u - yp)
    out = out + xlo * (u - xm) + xhi * (u - xp)
    return out + extra * u


def diagonal(coef):
    zlo, zhi, ylo, yhi, xlo, xhi, extra = coef
    return zlo + zhi + ylo + yhi + xlo + xhi + extra


def pick(n, parity):
    src = lax.broadcasted_iota(jnp.int32, (n, n // 2), 0)
    dst = lax.broadcasted_iota(jnp.int32, (n, n // 2), 1)
    return (src == 2 * dst + parity).astype(jnp.float32)


def cols(a, parity):
    return jnp.dot(a, pick(a.shape[-1], parity), precision=HI)


def rows(a, parity):
    return jnp.einsum("yr,zyx->zrx", pick(a.shape[1], parity), a, precision=HI)


def mean_four(a):
    r0 = rows(a, 0)
    r1 = rows(a, 1)
    return 0.25 * (cols(r0, 0) + cols(r1, 0) + cols(r0, 1) + cols(r1, 1))


def coarsen(coef):
    zlo, zhi, ylo, yhi, xlo, xhi, extra = coef
    cxlo = 0.125 * cols(rows(xlo, 0) + rows(xlo, 1), 0)
    cxhi = 0.125 * cols(rows(xhi, 0) + rows(xhi, 1), 1)
    ylo0 = rows(ylo, 0)
    yhi1 = rows(yhi, 1)
    cylo = 0.125 * (cols(ylo0, 0) + cols(ylo0, 1))
    cyhi = 0.125 * (cols(yhi1, 0) + cols(yhi1, 1))
    return (mean_four(zlo), mean_four(zhi), cylo, cyhi, cxlo, cxhi, mean_four(extra))


def spread(n):
    src = lax.broadcasted_iota(jnp.int32, (n, 2 * n), 0)
    dst = lax.broadcasted_iota(jnp.int32, (n, 2 * n), 1)
    return (src == dst // 2).astype(jnp.float32)


def prolong(field):
    wide = jnp.dot(field, spread(field.shape[-1]), precision=HI)
    return jnp.einsum("ry,zrx->zyx", spread(field.shape[1]), wide, precision=HI)


def local_sweep(u, zm, zp, rhs, coef, diag, inside):
    zlo, zhi, ylo, yhi, xlo, xhi, extra = coef
    zero_row = jnp.zeros_like(u[:, :1])
    zero_col = jnp.zeros_like(u[:, :, :1])
    ym = jnp.concatenate([zero_row, u[:, :-1]], axis=1)
    yp = jnp.concatenate([u[:, 1:], zero_row], axis=1)
    xm = jnp.concatenate([zero_col, u[:, :, :-1]], axis=2)
    xp = jnp.concatenate([u[:, :, 1:], zero_col], axis=2)
    out = zlo * (u - zm) + zhi * (u - zp)
    out = out + ylo * (u - ym) + yhi * (u - yp)
    out = out + xlo * (u - xm) + xhi * (u - xp)
    out = out + extra * u
    return jnp.where(inside, u + OMEGA * (rhs - out) / diag, 0.0)


def sweep(field, rhs, coef, diag, inside):
    n = field.shape[0]
    zlo_h, zhi_h = layer_halos(field)

    def part(lo, hi, zm, zp):
        return local_sweep(field[lo:hi], zm, zp, rhs[lo:hi], tuple(c[lo:hi] for c in coef), diag[lo:hi], inside)

    inner = part(1, n - 1, field[: n - 2], field[2:])
    first = part(0, 1, zlo_h, field[1:2])
    last = part(n - 1, n, field[n - 2 : n - 1], zhi_h)
    return jnp.concatenate([first, inner, last], axis=0)


def smooth(field, rhs, coef, diag, inside, count):
    for i in range(count):
        field = sweep(field, rhs, coef, diag, inside)
    return field


def crop_all(arrs, h_from, h_to):
    return tuple(crop(a, h_from, h_to) for a in arrs)


def body_wide(viscosity, adjoint_source, forward_velocity, friction, ice_mask, grounded_mask):
    layers = viscosity.shape[0]
    own_rows = viscosity.shape[1]
    mid_rows = own_rows // 2
    cols_own = viscosity.shape[2]
    half_cols = cols_own // 2
    gz = lax.axis_index("gz")
    gy = lax.axis_index("gy")
    total_layers = layers * lax.axis_size("gz")
    layer = (gz * layers + jnp.arange(layers)).astype(jnp.float32)
    profile = (jnp.float32(total_layers) - layer) / jnp.float32(total_layers)
    wsq = profile * profile
    icef = ice_mask.astype(jnp.float32)
    groundf = grounded_mask.astype(jnp.float32)
    base = 0.05 + 2.0 * (1.0 - icef)
    ground_fric = groundf * friction
    stacked = jnp.concatenate([viscosity, adjoint_source, base[None], ground_fric[None]], axis=0)
    hv = FINE_HALO + 1
    ext = extend_rows(extend_cols(stacked, COL_HALO), hv)
    visc_e = ext[:layers]
    src_e = crop(ext[layers : 2 * layers], hv, FINE_HALO)
    base_e = crop(ext[2 * layers : 2 * layers + 1], hv, FINE_HALO)[0]
    gfr_e = crop(ext[2 * layers + 1 : 2 * layers + 2], hv, FINE_HALO)[0]
    extra = base_e[None, :, :] + gfr_e[None, :, :] * wsq[:, None, None]
    fine = crop_all(face_set(visc_e), hv, FINE_HALO) + (extra,)
    dfine = diagonal(fine)
    middle = coarsen(fine)
    dmid = diagonal(middle)
    coarse_own = coarsen(crop_all(middle, FINE_HALO // 2, 0))
    coarse_all = gather_blocks(jnp.concatenate(coarse_own, axis=0), "gy")
    coarse_all = jnp.concatenate([coarse_all[i] for i in range(coarse_all.shape[0])], axis=1)
    coarse = tuple(coarse_all[i * layers : (i + 1) * layers] for i in range(7))
    dcoarse = diagonal(coarse)
    in_fine = row_mask(own_rows, FINE_HALO) & col_mask(cols_own, COL_HALO)
    in_mid = row_mask(mid_rows, FINE_HALO // 2) & col_mask(cols_own // 2, COL_HALO // 2)

    lam = jnp.where(in_fine, OMEGA * src_e / dfine, 0.0)
    lam = smooth(lam, src_e, fine, dfine, in_fine, S0 - 1)
    b_mid = mean_four(src_e - operate(lam, fine))
    e_mid = jnp.where(in_mid, OMEGA * b_mid / dmid, 0.0)
    e_mid = smooth(e_mid, b_mid, middle, dmid, in_mid, S1 - 1)
    hm = FINE_HALO // 2
    res_mid = crop(b_mid - operate(e_mid, middle), hm, 0)
    b_low = gather_blocks(mean_four(res_mid), "gy")
    b_low = jnp.concatenate([b_low[i] for i in range(b_low.shape[0])], axis=1)
    ones = col_mask(cols_own // 4, COL_HALO // 4)
    e_low = jnp.where(ones, OMEGA * b_low / dcoarse, 0.0)
    e_low = smooth(e_low, b_low, coarse, dcoarse, ones, S2 - 1)

    pair = jnp.concatenate([crop(e_mid, hm, 0), crop(b_mid, hm, 0)], axis=0)
    pair = extend_rows(pair, MID_HALO)
    e_mid = pair[:layers]
    b_mid = pair[layers:]
    low_rows = own_rows // 4
    ch = MID_HALO // 2
    padded = jnp.pad(e_low, ((0, 0), (ch, ch), (0, 0)))
    e_near = lax.dynamic_slice_in_dim(padded, gy * low_rows, low_rows + 2 * ch, 1)
    e_mid = e_mid + prolong(e_near)
    middle_p = crop_all(middle, hm, MID_HALO)
    dmid_p = crop(dmid, hm, MID_HALO)
    in_mid_p = row_mask(mid_rows, MID_HALO) & col_mask(cols_own // 2, COL_HALO // 2)
    e_mid = smooth(e_mid, b_mid, middle_p, dmid_p, in_mid_p, S1)

    lam = crop(lam, FINE_HALO, POST_HALO) + prolong(crop(e_mid, MID_HALO, POST_HALO // 2))
    fine_p = crop_all(fine, FINE_HALO, POST_HALO)
    dfine_p = crop(dfine, FINE_HALO, POST_HALO)
    src_p = crop(src_e, FINE_HALO, POST_HALO)
    in_fine_p = row_mask(own_rows, POST_HALO) & col_mask(cols_own, COL_HALO)
    lam = smooth(lam, src_p, fine_p, dfine_p, in_fine_p, S0)
    lam = crop(lam, POST_HALO, 0)

    own = lam[:, :, COL_HALO : COL_HALO + cols_own]
    column = jnp.sum(wsq[:, None, None] * forward_velocity * own, axis=0)
    parts = gather_blocks(column, "gz")
    summed = parts[0]
    for k in range(1, parts.shape[0]):
        summed = summed + parts[k]
    terms = -ground_fric * summed
    gradient = lax.dynamic_slice_in_dim(terms, gz * half_cols, half_cols, 1)
    return (own, gradient)


def n_layer_halos(u):
    count = lax.axis_size("gz")
    head = u[:1]
    tail = u[-1:]
    if count == 2:
        first = lax.axis_index("gz") == 0
        got = lax.ppermute(jnp.where(first, tail, head), "gz", [(0, 1), (1, 0)])
        zero = jnp.zeros_like(got)
        return jnp.where(first, zero, got), jnp.where(first, got, zero)
    lo = lax.ppermute(tail, "gz", [(i, i + 1) for i in range(count - 1)])
    hi = lax.ppermute(head, "gz", [(i + 1, i) for i in range(count - 1)])
    return lo, hi


def n_row_halos(u):
    count = lax.axis_size("gy")
    lo = lax.ppermute(u[:, -1:], "gy", [(i, i + 1) for i in range(count - 1)])
    hi = lax.ppermute(u[:, :1], "gy", [(i + 1, i) for i in range(count - 1)])
    return lo, hi


def n_neighbours(u):
    zlo, zhi = n_layer_halos(u)
    ylo, yhi = n_row_halos(u)
    zero = jnp.zeros_like(u[:, :, :1])
    zm = jnp.concatenate([zlo, u[:-1]], axis=0)
    zp = jnp.concatenate([u[1:], zhi], axis=0)
    ym = jnp.concatenate([ylo, u[:, :-1]], axis=1)
    yp = jnp.concatenate([u[:, 1:], yhi], axis=1)
    xm = jnp.concatenate([zero, u[:, :, :-1]], axis=2)
    xp = jnp.concatenate([u[:, :, 1:], zero], axis=2)
    return zm, zp, ym, yp, xm, xp


def n_face_set(eta):
    zm, zp, ym, yp, xm, xp = n_neighbours(eta)
    zlo = VERT * (0.5 * (eta + zm))
    zhi = VERT * (0.5 * (eta + zp))
    ylo = 0.5 * (eta + ym)
    yhi = 0.5 * (eta + yp)
    xlo = 0.5 * (eta + xm)
    xhi = 0.5 * (eta + xp)
    return (zlo, zhi, ylo, yhi, xlo, xhi)


def n_operate(u, coef):
    zlo, zhi, ylo, yhi, xlo, xhi, extra = coef
    zm, zp, ym, yp, xm, xp = n_neighbours(u)
    out = zlo * (u - zm) + zhi * (u - zp)
    out = out + ylo * (u - ym) + yhi * (u - yp)
    out = out + xlo * (u - xm) + xhi * (u - xp)
    return out + extra * u


def n_diagonal(coef):
    zlo, zhi, ylo, yhi, xlo, xhi, extra = coef
    return zlo + zhi + ylo + yhi + xlo + xhi + extra


def n_pick_matrix(cols):
    half = cols // 2
    src = lax.broadcasted_iota(jnp.int32, (cols, cols), 0)
    dst = lax.broadcasted_iota(jnp.int32, (cols, cols), 1)
    want = jnp.where(dst < half, 2 * dst, 2 * (dst - half) + 1)
    return (src == want).astype(jnp.float32)


def n_split_x(a):
    cols = a.shape[-1]
    both = jnp.dot(a, n_pick_matrix(cols), precision=HI)
    return both[..., : cols // 2], both[..., cols // 2 :]


def n_mean_four(a):
    e0, o0 = n_split_x(a[:, 0::2])
    e1, o1 = n_split_x(a[:, 1::2])
    return 0.25 * (e0 + e1 + o0 + o1)


def n_coarsen(coef):
    zlo, zhi, ylo, yhi, xlo, xhi, extra = coef
    xlo_e, _ = n_split_x(xlo[:, 0::2] + xlo[:, 1::2])
    _, xhi_o = n_split_x(xhi[:, 0::2] + xhi[:, 1::2])
    ylo_e, ylo_o = n_split_x(ylo[:, 0::2])
    yhi_e, yhi_o = n_split_x(yhi[:, 1::2])
    cxlo = 0.125 * xlo_e
    cxhi = 0.125 * xhi_o
    cylo = 0.125 * (ylo_e + ylo_o)
    cyhi = 0.125 * (yhi_e + yhi_o)
    return (n_mean_four(zlo), n_mean_four(zhi), cylo, cyhi, cxlo, cxhi, n_mean_four(extra))


def n_prolong(field):
    cols = field.shape[-1]
    src = lax.broadcasted_iota(jnp.int32, (cols, 2 * cols), 0)
    dst = lax.broadcasted_iota(jnp.int32, (cols, 2 * cols), 1)
    spread = (src == dst // 2).astype(jnp.float32)
    wide = jnp.dot(field, spread, precision=HI)
    return jnp.repeat(wide, 2, axis=1)


def n_sweep(field, rhs, coef, diag):
    return field + OMEGA * (rhs - n_operate(field, coef)) / diag


def n_body(viscosity, adjoint_source, forward_velocity, friction, ice_mask, grounded_mask):
    layers = viscosity.shape[0]
    cols = viscosity.shape[2]
    half_cols = cols // 2
    gz = lax.axis_index("gz")
    total_layers = layers * lax.axis_size("gz")
    layer = (gz * layers + jnp.arange(layers)).astype(jnp.float32)
    profile = (jnp.float32(total_layers) - layer) / jnp.float32(total_layers)
    wsq = profile * profile
    icef = ice_mask.astype(jnp.float32)
    groundf = grounded_mask.astype(jnp.float32)
    base = 0.05 + 2.0 * (1.0 - icef)
    ground_fric = groundf * friction
    stacked = jnp.concatenate([viscosity, adjoint_source, base[None], ground_fric[None]], axis=0)
    gathered = lax.all_gather(stacked, "gx", axis=0, tiled=False)
    count_x = gathered.shape[0]
    gathered = jnp.concatenate([gathered[i] for i in range(count_x)], axis=2)
    visc_all = gathered[:layers]
    source_all = gathered[layers : 2 * layers]
    base_all = gathered[2 * layers]
    gfr_all = gathered[2 * layers + 1]
    extra = base_all[None, :, :] + gfr_all[None, :, :] * wsq[:, None, None]
    fine = n_face_set(visc_all) + (extra,)
    dfine = n_diagonal(fine)
    middle = n_coarsen(fine)
    dmid = n_diagonal(middle)
    coarse = n_coarsen(middle)
    dcoarse = n_diagonal(coarse)
    lam = OMEGA * source_all / dfine
    for i in range(S0 - 1):
        lam = n_sweep(lam, source_all, fine, dfine)
    b_mid = n_mean_four(source_all - n_operate(lam, fine))
    e_mid = OMEGA * b_mid / dmid
    for i in range(S1 - 1):
        e_mid = n_sweep(e_mid, b_mid, middle, dmid)
    b_low = n_mean_four(b_mid - n_operate(e_mid, middle))
    e_low = OMEGA * b_low / dcoarse
    for i in range(S2 - 1):
        e_low = n_sweep(e_low, b_low, coarse, dcoarse)
    e_mid = e_mid + n_prolong(e_low)
    for i in range(S1):
        e_mid = n_sweep(e_mid, b_mid, middle, dmid)
    lam = lam + n_prolong(e_mid)
    for i in range(S0):
        lam = n_sweep(lam, source_all, fine, dfine)
    own = lax.dynamic_slice_in_dim(lam, lax.axis_index("gx") * cols, cols, 2)
    column = jnp.sum(wsq[:, None, None] * forward_velocity * own, axis=0)
    summed = lax.psum(column, "gz")
    terms = -ground_fric * summed
    gradient = lax.dynamic_slice_in_dim(terms, gz * half_cols, half_cols, 1)
    return (own, gradient)


def body(viscosity, *rest):
    layers, own_rows, cols_own = viscosity.shape
    cols_all = cols_own + 2 * COL_HALO
    wide_bytes = 4 * layers * (own_rows + 2 * FINE_HALO + 2) * cols_all
    if COL_HALO <= cols_own and FINE_HALO + 1 <= own_rows and MID_HALO <= own_rows // 2 and 20 * wide_bytes <= 40 * 2**20 and lax.axis_size("gy") <= 8:
        return body_wide(viscosity, *rest)
    return n_body(viscosity, *rest)


def solution(mesh):
    placed = (
        P("gz", "gy", "gx"),
        P("gz", "gy", "gx"),
        P("gz", "gy", "gx"),
        P("gy", "gx"),
        P("gy", "gx"),
        P("gy", "gx"),
    )
    return jax.shard_map(
        body,
        mesh=mesh,
        in_specs=placed,
        out_specs=(P("gz", "gy", "gx"), P("gy", ("gx", "gz"))),
        check_vma=False,
    )
```

```python
import jax
import jax.numpy as jnp
from jax import lax
from jax.sharding import PartitionSpec as P

S0 = 4
S1 = 4
S2 = 8


OMEGA = 0.8
VERT = 4.0
HI = lax.Precision.HIGHEST
FINE_HALO = 12
MID_HALO = 6
POST_HALO = 4
COL_HALO = 64


def layer_halos(u):
    count = lax.axis_size("gz")
    head = u[:1]
    tail = u[-1:]
    if count == 2:
        first = lax.axis_index("gz") == 0
        got = lax.ppermute(jnp.where(first, tail, head), "gz", [(0, 1), (1, 0)])
        zero = jnp.zeros_like(got)
        return jnp.where(first, zero, got), jnp.where(first, got, zero)
    lo = lax.ppermute(tail, "gz", [(i, i + 1) for i in range(count - 1)])
    hi = lax.ppermute(head, "gz", [(i + 1, i) for i in range(count - 1)])
    return lo, hi


def extend_rows(a, h):
    count = lax.axis_size("gy")
    lo = lax.ppermute(a[:, -h:], "gy", [(i, i + 1) for i in range(count - 1)])
    hi = lax.ppermute(a[:, :h], "gy", [(i + 1, i) for i in range(count - 1)])
    return jnp.concatenate([lo, a, hi], axis=1)


def gather_blocks(a, axis):
    count = lax.axis_size(axis)
    got = [a]
    for s in range(1, count):
        got.append(lax.ppermute(a, axis, [(i, (i + s) % count) for i in range(count)]))
    rev = jnp.stack(got[::-1], axis=0)
    return jnp.roll(rev, lax.axis_index(axis) + 1, axis=0)


def extend_cols(a, h):
    count = lax.axis_size("gx")
    lo = lax.ppermute(a[:, :, -h:], "gx", [(i, i + 1) for i in range(count - 1)])
    hi = lax.ppermute(a[:, :, :h], "gx", [(i + 1, i) for i in range(count - 1)])
    return jnp.concatenate([lo, a, hi], axis=2)


def col_mask(own_cols, h):
    g = lax.axis_index("gx") * own_cols - h + lax.broadcasted_iota(jnp.int32, (1, 1, own_cols + 2 * h), 2)
    return (g >= 0) & (g < own_cols * lax.axis_size("gx"))


def crop(a, h_from, h_to):
    cut = h_from - h_to
    return a[:, cut : a.shape[1] - cut]


def row_mask(own_rows, h):
    g = lax.axis_index("gy") * own_rows - h + lax.broadcasted_iota(jnp.int32, (1, own_rows + 2 * h, 1), 1)
    return (g >= 0) & (g < own_rows * lax.axis_size("gy"))


def neighbours(u):
    zlo, zhi = layer_halos(u)
    zero_row = jnp.zeros_like(u[:, :1])
    zero_col = jnp.zeros_like(u[:, :, :1])
    zm = jnp.concatenate([zlo, u[:-1]], axis=0)
    zp = jnp.concatenate([u[1:], zhi], axis=0)
    ym = jnp.concatenate([zero_row, u[:, :-1]], axis=1)
    yp = jnp.concatenate([u[:, 1:], zero_row], axis=1)
    xm = jnp.concatenate([zero_col, u[:, :, :-1]], axis=2)
    xp = jnp.concatenate([u[:, :, 1:], zero_col], axis=2)
    return zm, zp, ym, yp, xm, xp


def face_set(eta):
    zm, zp, ym, yp, xm, xp = neighbours(eta)
    zlo = VERT * (0.5 * (eta + zm))
    zhi = VERT * (0.5 * (eta + zp))
    ylo = 0.5 * (eta + ym)
    yhi = 0.5 * (eta + yp)
    xlo = 0.5 * (eta + xm)
    xhi = 0.5 * (eta + xp)
    return (zlo, zhi, ylo, yhi, xlo, xhi)


def operate(u, coef):
    zlo, zhi, ylo, yhi, xlo, xhi, extra = coef
    zm, zp, ym, yp, xm, xp = neighbours(u)
    out = zlo * (u - zm) + zhi * (u - zp)
    out = out + ylo * (u - ym) + yhi * (u - yp)
    out = out + xlo * (u - xm) + xhi * (u - xp)
    return out + extra * u


def diagonal(coef):
    zlo, zhi, ylo, yhi, xlo, xhi, extra = coef
    return zlo + zhi + ylo + yhi + xlo + xhi + extra


def pick(n, parity):
    src = lax.broadcasted_iota(jnp.int32, (n, n // 2), 0)
    dst = lax.broadcasted_iota(jnp.int32, (n, n // 2), 1)
    return (src == 2 * dst + parity).astype(jnp.float32)


def cols(a, parity):
    return jnp.dot(a, pick(a.shape[-1], parity), precision=HI)


def rows(a, parity):
    return jnp.einsum("yr,zyx->zrx", pick(a.shape[1], parity), a, precision=HI)


def mean_four(a):
    r0 = rows(a, 0)
    r1 = rows(a, 1)
    return 0.25 * (cols(r0, 0) + cols(r1, 0) + cols(r0, 1) + cols(r1, 1))


def coarsen(coef):
    zlo, zhi, ylo, yhi, xlo, xhi, extra = coef
    cxlo = 0.125 * cols(rows(xlo, 0) + rows(xlo, 1), 0)
    cxhi = 0.125 * cols(rows(xhi, 0) + rows(xhi, 1), 1)
    ylo0 = rows(ylo, 0)
    yhi1 = rows(yhi, 1)
    cylo = 0.125 * (cols(ylo0, 0) + cols(ylo0, 1))
    cyhi = 0.125 * (cols(yhi1, 0) + cols(yhi1, 1))
    return (mean_four(zlo), mean_four(zhi), cylo, cyhi, cxlo, cxhi, mean_four(extra))


def coarsen_stacked(coef):
    layers = coef[0].shape[0]
    width = coef[0].shape[2]
    half = width // 2
    stack = jnp.concatenate(coef, axis=0)
    both_rows = jnp.concatenate([rows(stack, 0), rows(stack, 1)], axis=0)
    src = lax.broadcasted_iota(jnp.int32, (width, width), 0)
    dst = lax.broadcasted_iota(jnp.int32, (width, width), 1)
    want = jnp.where(dst < half, 2 * dst, 2 * (dst - half) + 1)
    picked = jnp.dot(both_rows, (src == want).astype(jnp.float32), precision=HI)
    count = len(coef)

    def part(k, odd_row, odd_col):
        at = (odd_row * count + k) * layers
        return picked[at : at + layers, :, odd_col * half : (odd_col + 1) * half]

    def four(k):
        return 0.25 * (part(k, 0, 0) + part(k, 1, 0) + part(k, 0, 1) + part(k, 1, 1))

    cxlo = 0.125 * (part(4, 0, 0) + part(4, 1, 0))
    cxhi = 0.125 * (part(5, 0, 1) + part(5, 1, 1))
    cylo = 0.125 * (part(2, 0, 0) + part(2, 0, 1))
    cyhi = 0.125 * (part(3, 1, 0) + part(3, 1, 1))
    return (four(0), four(1), cylo, cyhi, cxlo, cxhi, four(6))


def spread(n):
    src = lax.broadcasted_iota(jnp.int32, (n, 2 * n), 0)
    dst = lax.broadcasted_iota(jnp.int32, (n, 2 * n), 1)
    return (src == dst // 2).astype(jnp.float32)


def prolong(field):
    wide = jnp.dot(field, spread(field.shape[-1]), precision=HI)
    return jnp.einsum("ry,zrx->zyx", spread(field.shape[1]), wide, precision=HI)


def sweep(field, rhs, coef, diag, inside):
    new = field + OMEGA * (rhs - operate(field, coef)) / diag
    return jnp.where(inside, new, 0.0)


def smooth(field, rhs, coef, diag, inside, count):
    for i in range(count):
        field = sweep(field, rhs, coef, diag, inside)
    return field


def crop_all(arrs, h_from, h_to):
    return tuple(crop(a, h_from, h_to) for a in arrs)


def body_wide(viscosity, adjoint_source, forward_velocity, friction, ice_mask, grounded_mask):
    layers = viscosity.shape[0]
    own_rows = viscosity.shape[1]
    mid_rows = own_rows // 2
    cols_own = viscosity.shape[2]
    half_cols = cols_own // 2
    gz = lax.axis_index("gz")
    gy = lax.axis_index("gy")
    total_layers = layers * lax.axis_size("gz")
    layer = (gz * layers + jnp.arange(layers)).astype(jnp.float32)
    profile = (jnp.float32(total_layers) - layer) / jnp.float32(total_layers)
    wsq = profile * profile
    icef = ice_mask.astype(jnp.float32)
    groundf = grounded_mask.astype(jnp.float32)
    base = 0.05 + 2.0 * (1.0 - icef)
    ground_fric = groundf * friction
    stacked = jnp.concatenate([viscosity, adjoint_source, base[None], ground_fric[None]], axis=0)
    hv = FINE_HALO + 1
    ext = extend_rows(extend_cols(stacked, COL_HALO), hv)
    visc_e = ext[:layers]
    src_e = crop(ext[layers : 2 * layers], hv, FINE_HALO)
    base_e = crop(ext[2 * layers : 2 * layers + 1], hv, FINE_HALO)[0]
    gfr_e = crop(ext[2 * layers + 1 : 2 * layers + 2], hv, FINE_HALO)[0]
    extra = base_e[None, :, :] + gfr_e[None, :, :] * wsq[:, None, None]
    fine = crop_all(face_set(visc_e), hv, FINE_HALO) + (extra,)
    dfine = diagonal(fine)
    middle = coarsen_stacked(fine)
    dmid = diagonal(middle)
    coarse_own = coarsen_stacked(crop_all(middle, FINE_HALO // 2, 0))
    coarse_all = gather_blocks(jnp.concatenate(coarse_own, axis=0), "gy")
    coarse_all = jnp.concatenate([coarse_all[i] for i in range(coarse_all.shape[0])], axis=1)
    coarse = tuple(coarse_all[i * layers : (i + 1) * layers] for i in range(7))
    dcoarse = diagonal(coarse)
    in_fine = row_mask(own_rows, FINE_HALO) & col_mask(cols_own, COL_HALO)
    in_mid = row_mask(mid_rows, FINE_HALO // 2) & col_mask(cols_own // 2, COL_HALO // 2)

    lam = jnp.where(in_fine, OMEGA * src_e / dfine, 0.0)
    lam = smooth(lam, src_e, fine, dfine, in_fine, S0 - 1)
    b_mid = mean_four(src_e - operate(lam, fine))
    e_mid = jnp.where(in_mid, OMEGA * b_mid / dmid, 0.0)
    e_mid = smooth(e_mid, b_mid, middle, dmid, in_mid, S1 - 1)
    hm = FINE_HALO // 2
    res_mid = crop(b_mid - operate(e_mid, middle), hm, 0)
    b_low = gather_blocks(mean_four(res_mid), "gy")
    b_low = jnp.concatenate([b_low[i] for i in range(b_low.shape[0])], axis=1)
    ones = col_mask(cols_own // 4, COL_HALO // 4)
    e_low = jnp.where(ones, OMEGA * b_low / dcoarse, 0.0)
    e_low = smooth(e_low, b_low, coarse, dcoarse, ones, S2 - 1)

    pair = jnp.concatenate([crop(e_mid, hm, 0), crop(b_mid, hm, 0)], axis=0)
    pair = extend_rows(pair, MID_HALO)
    e_mid = pair[:layers]
    b_mid = pair[layers:]
    low_rows = own_rows // 4
    ch = MID_HALO // 2
    padded = jnp.pad(e_low, ((0, 0), (ch, ch), (0, 0)))
    e_near = lax.dynamic_slice_in_dim(padded, gy * low_rows, low_rows + 2 * ch, 1)
    e_mid = e_mid + prolong(e_near)
    middle_p = crop_all(middle, hm, MID_HALO)
    dmid_p = crop(dmid, hm, MID_HALO)
    in_mid_p = row_mask(mid_rows, MID_HALO) & col_mask(cols_own // 2, COL_HALO // 2)
    e_mid = smooth(e_mid, b_mid, middle_p, dmid_p, in_mid_p, S1)

    lam = crop(lam, FINE_HALO, POST_HALO) + prolong(crop(e_mid, MID_HALO, POST_HALO // 2))
    fine_p = crop_all(fine, FINE_HALO, POST_HALO)
    dfine_p = crop(dfine, FINE_HALO, POST_HALO)
    src_p = crop(src_e, FINE_HALO, POST_HALO)
    in_fine_p = row_mask(own_rows, POST_HALO) & col_mask(cols_own, COL_HALO)
    lam = smooth(lam, src_p, fine_p, dfine_p, in_fine_p, S0)
    lam = crop(lam, POST_HALO, 0)

    own = lam[:, :, COL_HALO : COL_HALO + cols_own]
    column = jnp.sum(wsq[:, None, None] * forward_velocity * own, axis=0)
    parts = gather_blocks(column, "gz")
    summed = parts[0]
    for k in range(1, parts.shape[0]):
        summed = summed + parts[k]
    terms = -ground_fric * summed
    gradient = lax.dynamic_slice_in_dim(terms, gz * half_cols, half_cols, 1)
    return (own, gradient)


def n_layer_halos(u):
    count = lax.axis_size("gz")
    head = u[:1]
    tail = u[-1:]
    if count == 2:
        first = lax.axis_index("gz") == 0
        got = lax.ppermute(jnp.where(first, tail, head), "gz", [(0, 1), (1, 0)])
        zero = jnp.zeros_like(got)
        return jnp.where(first, zero, got), jnp.where(first, got, zero)
    lo = lax.ppermute(tail, "gz", [(i, i + 1) for i in range(count - 1)])
    hi = lax.ppermute(head, "gz", [(i + 1, i) for i in range(count - 1)])
    return lo, hi


def n_row_halos(u):
    count = lax.axis_size("gy")
    lo = lax.ppermute(u[:, -1:], "gy", [(i, i + 1) for i in range(count - 1)])
    hi = lax.ppermute(u[:, :1], "gy", [(i + 1, i) for i in range(count - 1)])
    return lo, hi


def n_neighbours(u):
    zlo, zhi = n_layer_halos(u)
    ylo, yhi = n_row_halos(u)
    zero = jnp.zeros_like(u[:, :, :1])
    zm = jnp.concatenate([zlo, u[:-1]], axis=0)
    zp = jnp.concatenate([u[1:], zhi], axis=0)
    ym = jnp.concatenate([ylo, u[:, :-1]], axis=1)
    yp = jnp.concatenate([u[:, 1:], yhi], axis=1)
    xm = jnp.concatenate([zero, u[:, :, :-1]], axis=2)
    xp = jnp.concatenate([u[:, :, 1:], zero], axis=2)
    return zm, zp, ym, yp, xm, xp


def n_face_set(eta):
    zm, zp, ym, yp, xm, xp = n_neighbours(eta)
    zlo = VERT * (0.5 * (eta + zm))
    zhi = VERT * (0.5 * (eta + zp))
    ylo = 0.5 * (eta + ym)
    yhi = 0.5 * (eta + yp)
    xlo = 0.5 * (eta + xm)
    xhi = 0.5 * (eta + xp)
    return (zlo, zhi, ylo, yhi, xlo, xhi)


def n_operate(u, coef):
    zlo, zhi, ylo, yhi, xlo, xhi, extra = coef
    zm, zp, ym, yp, xm, xp = n_neighbours(u)
    out = zlo * (u - zm) + zhi * (u - zp)
    out = out + ylo * (u - ym) + yhi * (u - yp)
    out = out + xlo * (u - xm) + xhi * (u - xp)
    return out + extra * u


def n_diagonal(coef):
    zlo, zhi, ylo, yhi, xlo, xhi, extra = coef
    return zlo + zhi + ylo + yhi + xlo + xhi + extra


def n_pick_matrix(cols):
    half = cols // 2
    src = lax.broadcasted_iota(jnp.int32, (cols, cols), 0)
    dst = lax.broadcasted_iota(jnp.int32, (cols, cols), 1)
    want = jnp.where(dst < half, 2 * dst, 2 * (dst - half) + 1)
    return (src == want).astype(jnp.float32)


def n_split_x(a):
    cols = a.shape[-1]
    both = jnp.dot(a, n_pick_matrix(cols), precision=HI)
    return both[..., : cols // 2], both[..., cols // 2 :]


def n_mean_four(a):
    e0, o0 = n_split_x(a[:, 0::2])
    e1, o1 = n_split_x(a[:, 1::2])
    return 0.25 * (e0 + e1 + o0 + o1)


def n_coarsen(coef):
    zlo, zhi, ylo, yhi, xlo, xhi, extra = coef
    xlo_e, _ = n_split_x(xlo[:, 0::2] + xlo[:, 1::2])
    _, xhi_o = n_split_x(xhi[:, 0::2] + xhi[:, 1::2])
    ylo_e, ylo_o = n_split_x(ylo[:, 0::2])
    yhi_e, yhi_o = n_split_x(yhi[:, 1::2])
    cxlo = 0.125 * xlo_e
    cxhi = 0.125 * xhi_o
    cylo = 0.125 * (ylo_e + ylo_o)
    cyhi = 0.125 * (yhi_e + yhi_o)
    return (n_mean_four(zlo), n_mean_four(zhi), cylo, cyhi, cxlo, cxhi, n_mean_four(extra))


def n_prolong(field):
    cols = field.shape[-1]
    src = lax.broadcasted_iota(jnp.int32, (cols, 2 * cols), 0)
    dst = lax.broadcasted_iota(jnp.int32, (cols, 2 * cols), 1)
    spread = (src == dst // 2).astype(jnp.float32)
    wide = jnp.dot(field, spread, precision=HI)
    return jnp.repeat(wide, 2, axis=1)


def n_sweep(field, rhs, coef, diag):
    return field + OMEGA * (rhs - n_operate(field, coef)) / diag


def n_body(viscosity, adjoint_source, forward_velocity, friction, ice_mask, grounded_mask):
    layers = viscosity.shape[0]
    cols = viscosity.shape[2]
    half_cols = cols // 2
    gz = lax.axis_index("gz")
    total_layers = layers * lax.axis_size("gz")
    layer = (gz * layers + jnp.arange(layers)).astype(jnp.float32)
    profile = (jnp.float32(total_layers) - layer) / jnp.float32(total_layers)
    wsq = profile * profile
    icef = ice_mask.astype(jnp.float32)
    groundf = grounded_mask.astype(jnp.float32)
    base = 0.05 + 2.0 * (1.0 - icef)
    ground_fric = groundf * friction
    stacked = jnp.concatenate([viscosity, adjoint_source, base[None], ground_fric[None]], axis=0)
    gathered = lax.all_gather(stacked, "gx", axis=0, tiled=False)
    count_x = gathered.shape[0]
    gathered = jnp.concatenate([gathered[i] for i in range(count_x)], axis=2)
    visc_all = gathered[:layers]
    source_all = gathered[layers : 2 * layers]
    base_all = gathered[2 * layers]
    gfr_all = gathered[2 * layers + 1]
    extra = base_all[None, :, :] + gfr_all[None, :, :] * wsq[:, None, None]
    fine = n_face_set(visc_all) + (extra,)
    dfine = n_diagonal(fine)
    middle = n_coarsen(fine)
    dmid = n_diagonal(middle)
    coarse = n_coarsen(middle)
    dcoarse = n_diagonal(coarse)
    lam = OMEGA * source_all / dfine
    for i in range(S0 - 1):
        lam = n_sweep(lam, source_all, fine, dfine)
    b_mid = n_mean_four(source_all - n_operate(lam, fine))
    e_mid = OMEGA * b_mid / dmid
    for i in range(S1 - 1):
        e_mid = n_sweep(e_mid, b_mid, middle, dmid)
    b_low = n_mean_four(b_mid - n_operate(e_mid, middle))
    e_low = OMEGA * b_low / dcoarse
    for i in range(S2 - 1):
        e_low = n_sweep(e_low, b_low, coarse, dcoarse)
    e_mid = e_mid + n_prolong(e_low)
    for i in range(S1):
        e_mid = n_sweep(e_mid, b_mid, middle, dmid)
    lam = lam + n_prolong(e_mid)
    for i in range(S0):
        lam = n_sweep(lam, source_all, fine, dfine)
    own = lax.dynamic_slice_in_dim(lam, lax.axis_index("gx") * cols, cols, 2)
    column = jnp.sum(wsq[:, None, None] * forward_velocity * own, axis=0)
    summed = lax.psum(column, "gz")
    terms = -ground_fric * summed
    gradient = lax.dynamic_slice_in_dim(terms, gz * half_cols, half_cols, 1)
    return (own, gradient)


def body(viscosity, *rest):
    layers, own_rows, cols_own = viscosity.shape
    cols_all = cols_own + 2 * COL_HALO
    wide_bytes = 4 * layers * (own_rows + 2 * FINE_HALO + 2) * cols_all
    if COL_HALO <= cols_own and FINE_HALO + 1 <= own_rows and MID_HALO <= own_rows // 2 and 20 * wide_bytes <= 40 * 2**20 and lax.axis_size("gy") <= 8:
        return body_wide(viscosity, *rest)
    return n_body(viscosity, *rest)


def solution(mesh):
    placed = (
        P("gz", "gy", "gx"),
        P("gz", "gy", "gx"),
        P("gz", "gy", "gx"),
        P("gy", "gx"),
        P("gy", "gx"),
        P("gy", "gx"),
    )
    return jax.shard_map(
        body,
        mesh=mesh,
        in_specs=placed,
        out_specs=(P("gz", "gy", "gx"), P("gy", ("gx", "gz"))),
        check_vma=False,
    )
```

```python
import jax
import jax.numpy as jnp
from jax import lax
from jax.sharding import PartitionSpec as P

S0 = 4
S1 = 4
S2 = 8


OMEGA = 0.8
VERT = 4.0
HI = lax.Precision.HIGHEST
FINE_HALO = 12
MID_HALO = 6
POST_HALO = 4
COL_HALO = 64


def layer_halos(u):
    count = lax.axis_size("gz")
    head = u[:1]
    tail = u[-1:]
    if count == 2:
        first = lax.axis_index("gz") == 0
        got = lax.ppermute(jnp.where(first, tail, head), "gz", [(0, 1), (1, 0)])
        zero = jnp.zeros_like(got)
        return jnp.where(first, zero, got), jnp.where(first, got, zero)
    lo = lax.ppermute(tail, "gz", [(i, i + 1) for i in range(count - 1)])
    hi = lax.ppermute(head, "gz", [(i + 1, i) for i in range(count - 1)])
    return lo, hi


def extend_rows(a, h):
    count = lax.axis_size("gy")
    lo = lax.ppermute(a[:, -h:], "gy", [(i, i + 1) for i in range(count - 1)])
    hi = lax.ppermute(a[:, :h], "gy", [(i + 1, i) for i in range(count - 1)])
    return jnp.concatenate([lo, a, hi], axis=1)


def gather_blocks(a, axis):
    count = lax.axis_size(axis)
    got = [a]
    for s in range(1, count):
        got.append(lax.ppermute(a, axis, [(i, (i + s) % count) for i in range(count)]))
    rev = jnp.stack(got[::-1], axis=0)
    return jnp.roll(rev, lax.axis_index(axis) + 1, axis=0)


def extend_cols(a, h):
    count = lax.axis_size("gx")
    lo = lax.ppermute(a[:, :, -h:], "gx", [(i, i + 1) for i in range(count - 1)])
    hi = lax.ppermute(a[:, :, :h], "gx", [(i + 1, i) for i in range(count - 1)])
    return jnp.concatenate([lo, a, hi], axis=2)


def col_mask(own_cols, h):
    g = lax.axis_index("gx") * own_cols - h + lax.broadcasted_iota(jnp.int32, (1, 1, own_cols + 2 * h), 2)
    return (g >= 0) & (g < own_cols * lax.axis_size("gx"))


def crop(a, h_from, h_to):
    cut = h_from - h_to
    return a[:, cut : a.shape[1] - cut]


def row_mask(own_rows, h):
    g = lax.axis_index("gy") * own_rows - h + lax.broadcasted_iota(jnp.int32, (1, own_rows + 2 * h, 1), 1)
    return (g >= 0) & (g < own_rows * lax.axis_size("gy"))


def neighbours(u, whole_z=False):
    if whole_z:
        zlo = zhi = jnp.zeros_like(u[:1])
    else:
        zlo, zhi = layer_halos(u)
    zero_row = jnp.zeros_like(u[:, :1])
    zero_col = jnp.zeros_like(u[:, :, :1])
    zm = jnp.concatenate([zlo, u[:-1]], axis=0)
    zp = jnp.concatenate([u[1:], zhi], axis=0)
    ym = jnp.concatenate([zero_row, u[:, :-1]], axis=1)
    yp = jnp.concatenate([u[:, 1:], zero_row], axis=1)
    xm = jnp.concatenate([zero_col, u[:, :, :-1]], axis=2)
    xp = jnp.concatenate([u[:, :, 1:], zero_col], axis=2)
    return zm, zp, ym, yp, xm, xp


def face_set(eta):
    zm, zp, ym, yp, xm, xp = neighbours(eta)
    zlo = VERT * (0.5 * (eta + zm))
    zhi = VERT * (0.5 * (eta + zp))
    ylo = 0.5 * (eta + ym)
    yhi = 0.5 * (eta + yp)
    xlo = 0.5 * (eta + xm)
    xhi = 0.5 * (eta + xp)
    return (zlo, zhi, ylo, yhi, xlo, xhi)


def operate(u, coef, whole_z=False):
    zlo, zhi, ylo, yhi, xlo, xhi, extra = coef
    zm, zp, ym, yp, xm, xp = neighbours(u, whole_z)
    out = zlo * (u - zm) + zhi * (u - zp)
    out = out + ylo * (u - ym) + yhi * (u - yp)
    out = out + xlo * (u - xm) + xhi * (u - xp)
    return out + extra * u


def diagonal(coef):
    zlo, zhi, ylo, yhi, xlo, xhi, extra = coef
    return zlo + zhi + ylo + yhi + xlo + xhi + extra


def pick(n, parity):
    src = lax.broadcasted_iota(jnp.int32, (n, n // 2), 0)
    dst = lax.broadcasted_iota(jnp.int32, (n, n // 2), 1)
    return (src == 2 * dst + parity).astype(jnp.float32)


def cols(a, parity):
    return jnp.dot(a, pick(a.shape[-1], parity), precision=HI)


def rows(a, parity):
    return jnp.einsum("yr,zyx->zrx", pick(a.shape[1], parity), a, precision=HI)


def mean_four(a):
    r0 = rows(a, 0)
    r1 = rows(a, 1)
    return 0.25 * (cols(r0, 0) + cols(r1, 0) + cols(r0, 1) + cols(r1, 1))


def coarsen(coef):
    zlo, zhi, ylo, yhi, xlo, xhi, extra = coef
    cxlo = 0.125 * cols(rows(xlo, 0) + rows(xlo, 1), 0)
    cxhi = 0.125 * cols(rows(xhi, 0) + rows(xhi, 1), 1)
    ylo0 = rows(ylo, 0)
    yhi1 = rows(yhi, 1)
    cylo = 0.125 * (cols(ylo0, 0) + cols(ylo0, 1))
    cyhi = 0.125 * (cols(yhi1, 0) + cols(yhi1, 1))
    return (mean_four(zlo), mean_four(zhi), cylo, cyhi, cxlo, cxhi, mean_four(extra))


def coarsen_stacked(coef):
    layers = coef[0].shape[0]
    width = coef[0].shape[2]
    half = width // 2
    stack = jnp.concatenate(coef, axis=0)
    both_rows = jnp.concatenate([rows(stack, 0), rows(stack, 1)], axis=0)
    src = lax.broadcasted_iota(jnp.int32, (width, width), 0)
    dst = lax.broadcasted_iota(jnp.int32, (width, width), 1)
    want = jnp.where(dst < half, 2 * dst, 2 * (dst - half) + 1)
    picked = jnp.dot(both_rows, (src == want).astype(jnp.float32), precision=HI)
    count = len(coef)

    def part(k, odd_row, odd_col):
        at = (odd_row * count + k) * layers
        return picked[at : at + layers, :, odd_col * half : (odd_col + 1) * half]

    def four(k):
        return 0.25 * (part(k, 0, 0) + part(k, 1, 0) + part(k, 0, 1) + part(k, 1, 1))

    cxlo = 0.125 * (part(4, 0, 0) + part(4, 1, 0))
    cxhi = 0.125 * (part(5, 0, 1) + part(5, 1, 1))
    cylo = 0.125 * (part(2, 0, 0) + part(2, 0, 1))
    cyhi = 0.125 * (part(3, 1, 0) + part(3, 1, 1))
    return (four(0), four(1), cylo, cyhi, cxlo, cxhi, four(6))


def spread(n):
    src = lax.broadcasted_iota(jnp.int32, (n, 2 * n), 0)
    dst = lax.broadcasted_iota(jnp.int32, (n, 2 * n), 1)
    return (src == dst // 2).astype(jnp.float32)


def prolong(field):
    wide = jnp.dot(field, spread(field.shape[-1]), precision=HI)
    return jnp.einsum("ry,zrx->zyx", spread(field.shape[1]), wide, precision=HI)


def sweep(field, rhs, coef, diag, inside, whole_z=False):
    new = field + OMEGA * (rhs - operate(field, coef, whole_z)) / diag
    return jnp.where(inside, new, 0.0)


def smooth(field, rhs, coef, diag, inside, count, whole_z=False):
    for i in range(count):
        field = sweep(field, rhs, coef, diag, inside, whole_z)
    return field


def crop_all(arrs, h_from, h_to):
    return tuple(crop(a, h_from, h_to) for a in arrs)


def body_wide(viscosity, adjoint_source, forward_velocity, friction, ice_mask, grounded_mask):
    layers = viscosity.shape[0]
    own_rows = viscosity.shape[1]
    mid_rows = own_rows // 2
    cols_own = viscosity.shape[2]
    half_cols = cols_own // 2
    gz = lax.axis_index("gz")
    gy = lax.axis_index("gy")
    total_layers = layers * lax.axis_size("gz")
    layer = (gz * layers + jnp.arange(layers)).astype(jnp.float32)
    profile = (jnp.float32(total_layers) - layer) / jnp.float32(total_layers)
    wsq = profile * profile
    icef = ice_mask.astype(jnp.float32)
    groundf = grounded_mask.astype(jnp.float32)
    base = 0.05 + 2.0 * (1.0 - icef)
    ground_fric = groundf * friction
    stacked = jnp.concatenate([viscosity, adjoint_source, base[None], ground_fric[None]], axis=0)
    hv = FINE_HALO + 1
    ext = extend_rows(extend_cols(stacked, COL_HALO), hv)
    visc_e = ext[:layers]
    src_e = crop(ext[layers : 2 * layers], hv, FINE_HALO)
    base_e = crop(ext[2 * layers : 2 * layers + 1], hv, FINE_HALO)[0]
    gfr_e = crop(ext[2 * layers + 1 : 2 * layers + 2], hv, FINE_HALO)[0]
    extra = base_e[None, :, :] + gfr_e[None, :, :] * wsq[:, None, None]
    fine = crop_all(face_set(visc_e), hv, FINE_HALO) + (extra,)
    dfine = diagonal(fine)
    middle = coarsen_stacked(fine)
    dmid = diagonal(middle)
    coarse_own = coarsen_stacked(crop_all(middle, FINE_HALO // 2, 0))
    coarse_z = gather_blocks(jnp.concatenate(coarse_own, axis=0), "gz")
    count_z = coarse_z.shape[0]
    coarse_z = jnp.concatenate(
        [coarse_z[k, i * layers : (i + 1) * layers] for i in range(7) for k in range(count_z)], axis=0
    )
    coarse_all = gather_blocks(coarse_z, "gy")
    coarse_all = jnp.concatenate([coarse_all[i] for i in range(coarse_all.shape[0])], axis=1)
    all_layers = layers * count_z
    coarse = tuple(coarse_all[i * all_layers : (i + 1) * all_layers] for i in range(7))
    dcoarse = diagonal(coarse)
    in_fine = row_mask(own_rows, FINE_HALO) & col_mask(cols_own, COL_HALO)
    in_mid = row_mask(mid_rows, FINE_HALO // 2) & col_mask(cols_own // 2, COL_HALO // 2)

    lam = jnp.where(in_fine, OMEGA * src_e / dfine, 0.0)
    lam = smooth(lam, src_e, fine, dfine, in_fine, S0 - 1)
    b_mid = mean_four(src_e - operate(lam, fine))
    e_mid = jnp.where(in_mid, OMEGA * b_mid / dmid, 0.0)
    e_mid = smooth(e_mid, b_mid, middle, dmid, in_mid, S1 - 1)
    hm = FINE_HALO // 2
    res_mid = crop(b_mid - operate(e_mid, middle), hm, 0)
    b_low = gather_blocks(mean_four(res_mid), "gz")
    b_low = jnp.concatenate([b_low[k] for k in range(b_low.shape[0])], axis=0)
    b_low = gather_blocks(b_low, "gy")
    b_low = jnp.concatenate([b_low[i] for i in range(b_low.shape[0])], axis=1)
    ones = col_mask(cols_own // 4, COL_HALO // 4)
    e_low = jnp.where(ones, OMEGA * b_low / dcoarse, 0.0)
    e_low = smooth(e_low, b_low, coarse, dcoarse, ones, S2 - 1, whole_z=True)
    e_low = lax.dynamic_slice_in_dim(e_low, gz * layers, layers, 0)

    pair = jnp.concatenate([crop(e_mid, hm, 0), crop(b_mid, hm, 0)], axis=0)
    pair = extend_rows(pair, MID_HALO)
    e_mid = pair[:layers]
    b_mid = pair[layers:]
    low_rows = own_rows // 4
    ch = MID_HALO // 2
    padded = jnp.pad(e_low, ((0, 0), (ch, ch), (0, 0)))
    e_near = lax.dynamic_slice_in_dim(padded, gy * low_rows, low_rows + 2 * ch, 1)
    e_mid = e_mid + prolong(e_near)
    middle_p = crop_all(middle, hm, MID_HALO)
    dmid_p = crop(dmid, hm, MID_HALO)
    in_mid_p = row_mask(mid_rows, MID_HALO) & col_mask(cols_own // 2, COL_HALO // 2)
    e_mid = smooth(e_mid, b_mid, middle_p, dmid_p, in_mid_p, S1)

    lam = crop(lam, FINE_HALO, POST_HALO) + prolong(crop(e_mid, MID_HALO, POST_HALO // 2))
    fine_p = crop_all(fine, FINE_HALO, POST_HALO)
    dfine_p = crop(dfine, FINE_HALO, POST_HALO)
    src_p = crop(src_e, FINE_HALO, POST_HALO)
    in_fine_p = row_mask(own_rows, POST_HALO) & col_mask(cols_own, COL_HALO)
    lam = smooth(lam, src_p, fine_p, dfine_p, in_fine_p, S0)
    lam = crop(lam, POST_HALO, 0)

    own = lam[:, :, COL_HALO : COL_HALO + cols_own]
    column = jnp.sum(wsq[:, None, None] * forward_velocity * own, axis=0)
    parts = gather_blocks(column, "gz")
    summed = parts[0]
    for k in range(1, parts.shape[0]):
        summed = summed + parts[k]
    terms = -ground_fric * summed
    gradient = lax.dynamic_slice_in_dim(terms, gz * half_cols, half_cols, 1)
    return (own, gradient)


def n_layer_halos(u):
    count = lax.axis_size("gz")
    head = u[:1]
    tail = u[-1:]
    if count == 2:
        first = lax.axis_index("gz") == 0
        got = lax.ppermute(jnp.where(first, tail, head), "gz", [(0, 1), (1, 0)])
        zero = jnp.zeros_like(got)
        return jnp.where(first, zero, got), jnp.where(first, got, zero)
    lo = lax.ppermute(tail, "gz", [(i, i + 1) for i in range(count - 1)])
    hi = lax.ppermute(head, "gz", [(i + 1, i) for i in range(count - 1)])
    return lo, hi


def n_row_halos(u):
    count = lax.axis_size("gy")
    lo = lax.ppermute(u[:, -1:], "gy", [(i, i + 1) for i in range(count - 1)])
    hi = lax.ppermute(u[:, :1], "gy", [(i + 1, i) for i in range(count - 1)])
    return lo, hi


def n_neighbours(u):
    zlo, zhi = n_layer_halos(u)
    ylo, yhi = n_row_halos(u)
    zero = jnp.zeros_like(u[:, :, :1])
    zm = jnp.concatenate([zlo, u[:-1]], axis=0)
    zp = jnp.concatenate([u[1:], zhi], axis=0)
    ym = jnp.concatenate([ylo, u[:, :-1]], axis=1)
    yp = jnp.concatenate([u[:, 1:], yhi], axis=1)
    xm = jnp.concatenate([zero, u[:, :, :-1]], axis=2)
    xp = jnp.concatenate([u[:, :, 1:], zero], axis=2)
    return zm, zp, ym, yp, xm, xp


def n_face_set(eta):
    zm, zp, ym, yp, xm, xp = n_neighbours(eta)
    zlo = VERT * (0.5 * (eta + zm))
    zhi = VERT * (0.5 * (eta + zp))
    ylo = 0.5 * (eta + ym)
    yhi = 0.5 * (eta + yp)
    xlo = 0.5 * (eta + xm)
    xhi = 0.5 * (eta + xp)
    return (zlo, zhi, ylo, yhi, xlo, xhi)


def n_operate(u, coef):
    zlo, zhi, ylo, yhi, xlo, xhi, extra = coef
    zm, zp, ym, yp, xm, xp = n_neighbours(u)
    out = zlo * (u - zm) + zhi * (u - zp)
    out = out + ylo * (u - ym) + yhi * (u - yp)
    out = out + xlo * (u - xm) + xhi * (u - xp)
    return out + extra * u


def n_diagonal(coef):
    zlo, zhi, ylo, yhi, xlo, xhi, extra = coef
    return zlo + zhi + ylo + yhi + xlo + xhi + extra


def n_pick_matrix(cols):
    half = cols // 2
    src = lax.broadcasted_iota(jnp.int32, (cols, cols), 0)
    dst = lax.broadcasted_iota(jnp.int32, (cols, cols), 1)
    want = jnp.where(dst < half, 2 * dst, 2 * (dst - half) + 1)
    return (src == want).astype(jnp.float32)


def n_split_x(a):
    cols = a.shape[-1]
    both = jnp.dot(a, n_pick_matrix(cols), precision=HI)
    return both[..., : cols // 2], both[..., cols // 2 :]


def n_mean_four(a):
    e0, o0 = n_split_x(a[:, 0::2])
    e1, o1 = n_split_x(a[:, 1::2])
    return 0.25 * (e0 + e1 + o0 + o1)


def n_coarsen(coef):
    zlo, zhi, ylo, yhi, xlo, xhi, extra = coef
    xlo_e, _ = n_split_x(xlo[:, 0::2] + xlo[:, 1::2])
    _, xhi_o = n_split_x(xhi[:, 0::2] + xhi[:, 1::2])
    ylo_e, ylo_o = n_split_x(ylo[:, 0::2])
    yhi_e, yhi_o = n_split_x(yhi[:, 1::2])
    cxlo = 0.125 * xlo_e
    cxhi = 0.125 * xhi_o
    cylo = 0.125 * (ylo_e + ylo_o)
    cyhi = 0.125 * (yhi_e + yhi_o)
    return (n_mean_four(zlo), n_mean_four(zhi), cylo, cyhi, cxlo, cxhi, n_mean_four(extra))


def n_prolong(field):
    cols = field.shape[-1]
    src = lax.broadcasted_iota(jnp.int32, (cols, 2 * cols), 0)
    dst = lax.broadcasted_iota(jnp.int32, (cols, 2 * cols), 1)
    spread = (src == dst // 2).astype(jnp.float32)
    wide = jnp.dot(field, spread, precision=HI)
    return jnp.repeat(wide, 2, axis=1)


def n_sweep(field, rhs, coef, diag):
    return field + OMEGA * (rhs - n_operate(field, coef)) / diag


def n_body(viscosity, adjoint_source, forward_velocity, friction, ice_mask, grounded_mask):
    layers = viscosity.shape[0]
    cols = viscosity.shape[2]
    half_cols = cols // 2
    gz = lax.axis_index("gz")
    total_layers = layers * lax.axis_size("gz")
    layer = (gz * layers + jnp.arange(layers)).astype(jnp.float32)
    profile = (jnp.float32(total_layers) - layer) / jnp.float32(total_layers)
    wsq = profile * profile
    icef = ice_mask.astype(jnp.float32)
    groundf = grounded_mask.astype(jnp.float32)
    base = 0.05 + 2.0 * (1.0 - icef)
    ground_fric = groundf * friction
    stacked = jnp.concatenate([viscosity, adjoint_source, base[None], ground_fric[None]], axis=0)
    gathered = lax.all_gather(stacked, "gx", axis=0, tiled=False)
    count_x = gathered.shape[0]
    gathered = jnp.concatenate([gathered[i] for i in range(count_x)], axis=2)
    visc_all = gathered[:layers]
    source_all = gathered[layers : 2 * layers]
    base_all = gathered[2 * layers]
    gfr_all = gathered[2 * layers + 1]
    extra = base_all[None, :, :] + gfr_all[None, :, :] * wsq[:, None, None]
    fine = n_face_set(visc_all) + (extra,)
    dfine = n_diagonal(fine)
    middle = n_coarsen(fine)
    dmid = n_diagonal(middle)
    coarse = n_coarsen(middle)
    dcoarse = n_diagonal(coarse)
    lam = OMEGA * source_all / dfine
    for i in range(S0 - 1):
        lam = n_sweep(lam, source_all, fine, dfine)
    b_mid = n_mean_four(source_all - n_operate(lam, fine))
    e_mid = OMEGA * b_mid / dmid
    for i in range(S1 - 1):
        e_mid = n_sweep(e_mid, b_mid, middle, dmid)
    b_low = n_mean_four(b_mid - n_operate(e_mid, middle))
    e_low = OMEGA * b_low / dcoarse
    for i in range(S2 - 1):
        e_low = n_sweep(e_low, b_low, coarse, dcoarse)
    e_mid = e_mid + n_prolong(e_low)
    for i in range(S1):
        e_mid = n_sweep(e_mid, b_mid, middle, dmid)
    lam = lam + n_prolong(e_mid)
    for i in range(S0):
        lam = n_sweep(lam, source_all, fine, dfine)
    own = lax.dynamic_slice_in_dim(lam, lax.axis_index("gx") * cols, cols, 2)
    column = jnp.sum(wsq[:, None, None] * forward_velocity * own, axis=0)
    summed = lax.psum(column, "gz")
    terms = -ground_fric * summed
    gradient = lax.dynamic_slice_in_dim(terms, gz * half_cols, half_cols, 1)
    return (own, gradient)


def body(viscosity, *rest):
    layers, own_rows, cols_own = viscosity.shape
    cols_all = cols_own + 2 * COL_HALO
    wide_bytes = 4 * layers * (own_rows + 2 * FINE_HALO + 2) * cols_all
    if COL_HALO <= cols_own and FINE_HALO + 1 <= own_rows and MID_HALO <= own_rows // 2 and 20 * wide_bytes <= 40 * 2**20 and lax.axis_size("gy") <= 8:
        return body_wide(viscosity, *rest)
    return n_body(viscosity, *rest)


def solution(mesh):
    placed = (
        P("gz", "gy", "gx"),
        P("gz", "gy", "gx"),
        P("gz", "gy", "gx"),
        P("gy", "gx"),
        P("gy", "gx"),
        P("gy", "gx"),
    )
    return jax.shard_map(
        body,
        mesh=mesh,
        in_specs=placed,
        out_specs=(P("gz", "gy", "gx"), P("gy", ("gx", "gz"))),
        check_vma=False,
    )
```

```python
import jax
import jax.numpy as jnp
from jax import lax
from jax.sharding import PartitionSpec as P

S0 = 4
S1 = 4
S2 = 8


OMEGA = 0.8
VERT = 4.0
HI = lax.Precision.HIGHEST
FINE_HALO = 12
MID_HALO = 6
POST_HALO = 4
COL_HALO = 64


def layer_halos(u):
    count = lax.axis_size("gz")
    head = u[:1]
    tail = u[-1:]
    if count == 2:
        first = lax.axis_index("gz") == 0
        got = lax.ppermute(jnp.where(first, tail, head), "gz", [(0, 1), (1, 0)])
        zero = jnp.zeros_like(got)
        return jnp.where(first, zero, got), jnp.where(first, got, zero)
    lo = lax.ppermute(tail, "gz", [(i, i + 1) for i in range(count - 1)])
    hi = lax.ppermute(head, "gz", [(i + 1, i) for i in range(count - 1)])
    return lo, hi


def extend_rows(a, h):
    count = lax.axis_size("gy")
    lo = lax.ppermute(a[:, -h:], "gy", [(i, i + 1) for i in range(count - 1)])
    hi = lax.ppermute(a[:, :h], "gy", [(i + 1, i) for i in range(count - 1)])
    return jnp.concatenate([lo, a, hi], axis=1)


def gather_blocks(a, axis):
    count = lax.axis_size(axis)
    got = [a]
    for s in range(1, count):
        got.append(lax.ppermute(a, axis, [(i, (i + s) % count) for i in range(count)]))
    rev = jnp.stack(got[::-1], axis=0)
    return jnp.roll(rev, lax.axis_index(axis) + 1, axis=0)


def extend_cols(a, h):
    count = lax.axis_size("gx")
    lo = lax.ppermute(a[:, :, -h:], "gx", [(i, i + 1) for i in range(count - 1)])
    hi = lax.ppermute(a[:, :, :h], "gx", [(i + 1, i) for i in range(count - 1)])
    return jnp.concatenate([lo, a, hi], axis=2)


def col_mask(own_cols, h):
    g = lax.axis_index("gx") * own_cols - h + lax.broadcasted_iota(jnp.int32, (1, 1, own_cols + 2 * h), 2)
    return (g >= 0) & (g < own_cols * lax.axis_size("gx"))


def gather_pairs(a, axis):
    count = lax.axis_size(axis)
    if count & (count - 1):
        return gather_blocks(a, axis)
    me = lax.axis_index(axis)
    blocks = a[None]
    step = 1
    while step < count:
        other = lax.ppermute(blocks, axis, [(i, i ^ step) for i in range(count)])
        low = (me // step) % 2 == 0
        blocks = jnp.where(low, jnp.concatenate([blocks, other]), jnp.concatenate([other, blocks]))
        step *= 2
    return blocks


def crop(a, h_from, h_to):
    cut = h_from - h_to
    return a[:, cut : a.shape[1] - cut]


def row_mask(own_rows, h):
    g = lax.axis_index("gy") * own_rows - h + lax.broadcasted_iota(jnp.int32, (1, own_rows + 2 * h, 1), 1)
    return (g >= 0) & (g < own_rows * lax.axis_size("gy"))


def neighbours(u):
    zlo, zhi = layer_halos(u)
    zero_row = jnp.zeros_like(u[:, :1])
    zero_col = jnp.zeros_like(u[:, :, :1])
    zm = jnp.concatenate([zlo, u[:-1]], axis=0)
    zp = jnp.concatenate([u[1:], zhi], axis=0)
    ym = jnp.concatenate([zero_row, u[:, :-1]], axis=1)
    yp = jnp.concatenate([u[:, 1:], zero_row], axis=1)
    xm = jnp.concatenate([zero_col, u[:, :, :-1]], axis=2)
    xp = jnp.concatenate([u[:, :, 1:], zero_col], axis=2)
    return zm, zp, ym, yp, xm, xp


def face_set(eta):
    zm, zp, ym, yp, xm, xp = neighbours(eta)
    zlo = VERT * (0.5 * (eta + zm))
    zhi = VERT * (0.5 * (eta + zp))
    ylo = 0.5 * (eta + ym)
    yhi = 0.5 * (eta + yp)
    xlo = 0.5 * (eta + xm)
    xhi = 0.5 * (eta + xp)
    return (zlo, zhi, ylo, yhi, xlo, xhi)


def operate(u, coef):
    zlo, zhi, ylo, yhi, xlo, xhi, extra = coef
    zm, zp, ym, yp, xm, xp = neighbours(u)
    out = zlo * (u - zm) + zhi * (u - zp)
    out = out + ylo * (u - ym) + yhi * (u - yp)
    out = out + xlo * (u - xm) + xhi * (u - xp)
    return out + extra * u


def diagonal(coef):
    zlo, zhi, ylo, yhi, xlo, xhi, extra = coef
    return zlo + zhi + ylo + yhi + xlo + xhi + extra


def pick(n, parity):
    src = lax.broadcasted_iota(jnp.int32, (n, n // 2), 0)
    dst = lax.broadcasted_iota(jnp.int32, (n, n // 2), 1)
    return (src == 2 * dst + parity).astype(jnp.float32)


def cols(a, parity):
    return jnp.dot(a, pick(a.shape[-1], parity), precision=HI)


def rows(a, parity):
    return jnp.einsum("yr,zyx->zrx", pick(a.shape[1], parity), a, precision=HI)


def mean_four(a):
    r0 = rows(a, 0)
    r1 = rows(a, 1)
    return 0.25 * (cols(r0, 0) + cols(r1, 0) + cols(r0, 1) + cols(r1, 1))


def coarsen(coef):
    zlo, zhi, ylo, yhi, xlo, xhi, extra = coef
    cxlo = 0.125 * cols(rows(xlo, 0) + rows(xlo, 1), 0)
    cxhi = 0.125 * cols(rows(xhi, 0) + rows(xhi, 1), 1)
    ylo0 = rows(ylo, 0)
    yhi1 = rows(yhi, 1)
    cylo = 0.125 * (cols(ylo0, 0) + cols(ylo0, 1))
    cyhi = 0.125 * (cols(yhi1, 0) + cols(yhi1, 1))
    return (mean_four(zlo), mean_four(zhi), cylo, cyhi, cxlo, cxhi, mean_four(extra))


def coarsen_stacked(coef):
    layers = coef[0].shape[0]
    width = coef[0].shape[2]
    half = width // 2
    stack = jnp.concatenate(coef, axis=0)
    both_rows = jnp.concatenate([rows(stack, 0), rows(stack, 1)], axis=0)
    src = lax.broadcasted_iota(jnp.int32, (width, width), 0)
    dst = lax.broadcasted_iota(jnp.int32, (width, width), 1)
    want = jnp.where(dst < half, 2 * dst, 2 * (dst - half) + 1)
    picked = jnp.dot(both_rows, (src == want).astype(jnp.float32), precision=HI)
    count = len(coef)

    def part(k, odd_row, odd_col):
        at = (odd_row * count + k) * layers
        return picked[at : at + layers, :, odd_col * half : (odd_col + 1) * half]

    def four(k):
        return 0.25 * (part(k, 0, 0) + part(k, 1, 0) + part(k, 0, 1) + part(k, 1, 1))

    cxlo = 0.125 * (part(4, 0, 0) + part(4, 1, 0))
    cxhi = 0.125 * (part(5, 0, 1) + part(5, 1, 1))
    cylo = 0.125 * (part(2, 0, 0) + part(2, 0, 1))
    cyhi = 0.125 * (part(3, 1, 0) + part(3, 1, 1))
    return (four(0), four(1), cylo, cyhi, cxlo, cxhi, four(6))


def spread(n):
    src = lax.broadcasted_iota(jnp.int32, (n, 2 * n), 0)
    dst = lax.broadcasted_iota(jnp.int32, (n, 2 * n), 1)
    return (src == dst // 2).astype(jnp.float32)


def prolong(field):
    wide = jnp.dot(field, spread(field.shape[-1]), precision=HI)
    return jnp.einsum("ry,zrx->zyx", spread(field.shape[1]), wide, precision=HI)


def sweep(field, rhs, coef, diag, inside):
    new = field + OMEGA * (rhs - operate(field, coef)) / diag
    return jnp.where(inside, new, 0.0)


def smooth(field, rhs, coef, diag, inside, count):
    for i in range(count):
        field = sweep(field, rhs, coef, diag, inside)
    return field


def crop_all(arrs, h_from, h_to):
    return tuple(crop(a, h_from, h_to) for a in arrs)


def body_wide(viscosity, adjoint_source, forward_velocity, friction, ice_mask, grounded_mask):
    layers = viscosity.shape[0]
    own_rows = viscosity.shape[1]
    mid_rows = own_rows // 2
    cols_own = viscosity.shape[2]
    half_cols = cols_own // 2
    gz = lax.axis_index("gz")
    gy = lax.axis_index("gy")
    total_layers = layers * lax.axis_size("gz")
    layer = (gz * layers + jnp.arange(layers)).astype(jnp.float32)
    profile = (jnp.float32(total_layers) - layer) / jnp.float32(total_layers)
    wsq = profile * profile
    icef = ice_mask.astype(jnp.float32)
    groundf = grounded_mask.astype(jnp.float32)
    base = 0.05 + 2.0 * (1.0 - icef)
    ground_fric = groundf * friction
    stacked = jnp.concatenate([viscosity, adjoint_source, base[None], ground_fric[None]], axis=0)
    hv = FINE_HALO + 1
    ext = extend_rows(extend_cols(stacked, COL_HALO), hv)
    visc_e = ext[:layers]
    src_e = crop(ext[layers : 2 * layers], hv, FINE_HALO)
    base_e = crop(ext[2 * layers : 2 * layers + 1], hv, FINE_HALO)[0]
    gfr_e = crop(ext[2 * layers + 1 : 2 * layers + 2], hv, FINE_HALO)[0]
    extra = base_e[None, :, :] + gfr_e[None, :, :] * wsq[:, None, None]
    fine = crop_all(face_set(visc_e), hv, FINE_HALO) + (extra,)
    dfine = diagonal(fine)
    middle = coarsen_stacked(fine)
    dmid = diagonal(middle)
    coarse_own = coarsen_stacked(crop_all(middle, FINE_HALO // 2, 0))
    coarse_all = gather_pairs(jnp.concatenate(coarse_own, axis=0), "gy")
    coarse_all = jnp.concatenate([coarse_all[i] for i in range(coarse_all.shape[0])], axis=1)
    coarse = tuple(coarse_all[i * layers : (i + 1) * layers] for i in range(7))
    dcoarse = diagonal(coarse)
    in_fine = row_mask(own_rows, FINE_HALO) & col_mask(cols_own, COL_HALO)
    in_mid = row_mask(mid_rows, FINE_HALO // 2) & col_mask(cols_own // 2, COL_HALO // 2)

    lam = jnp.where(in_fine, OMEGA * src_e / dfine, 0.0)
    lam = smooth(lam, src_e, fine, dfine, in_fine, S0 - 1)
    b_mid = mean_four(src_e - operate(lam, fine))
    e_mid = jnp.where(in_mid, OMEGA * b_mid / dmid, 0.0)
    e_mid = smooth(e_mid, b_mid, middle, dmid, in_mid, S1 - 1)
    hm = FINE_HALO // 2
    res_mid = crop(b_mid - operate(e_mid, middle), hm, 0)
    b_low = gather_pairs(mean_four(res_mid), "gy")
    b_low = jnp.concatenate([b_low[i] for i in range(b_low.shape[0])], axis=1)
    ones = col_mask(cols_own // 4, COL_HALO // 4)
    e_low = jnp.where(ones, OMEGA * b_low / dcoarse, 0.0)
    e_low = smooth(e_low, b_low, coarse, dcoarse, ones, S2 - 1)

    pair = jnp.concatenate([crop(e_mid, hm, 0), crop(b_mid, hm, 0)], axis=0)
    pair = extend_rows(pair, MID_HALO)
    e_mid = pair[:layers]
    b_mid = pair[layers:]
    low_rows = own_rows // 4
    ch = MID_HALO // 2
    padded = jnp.pad(e_low, ((0, 0), (ch, ch), (0, 0)))
    e_near = lax.dynamic_slice_in_dim(padded, gy * low_rows, low_rows + 2 * ch, 1)
    e_mid = e_mid + prolong(e_near)
    middle_p = crop_all(middle, hm, MID_HALO)
    dmid_p = crop(dmid, hm, MID_HALO)
    in_mid_p = row_mask(mid_rows, MID_HALO) & col_mask(cols_own // 2, COL_HALO // 2)
    e_mid = smooth(e_mid, b_mid, middle_p, dmid_p, in_mid_p, S1)

    lam = crop(lam, FINE_HALO, POST_HALO) + prolong(crop(e_mid, MID_HALO, POST_HALO // 2))
    fine_p = crop_all(fine, FINE_HALO, POST_HALO)
    dfine_p = crop(dfine, FINE_HALO, POST_HALO)
    src_p = crop(src_e, FINE_HALO, POST_HALO)
    in_fine_p = row_mask(own_rows, POST_HALO) & col_mask(cols_own, COL_HALO)
    lam = smooth(lam, src_p, fine_p, dfine_p, in_fine_p, S0)
    lam = crop(lam, POST_HALO, 0)

    own = lam[:, :, COL_HALO : COL_HALO + cols_own]
    column = jnp.sum(wsq[:, None, None] * forward_velocity * own, axis=0)
    parts = gather_blocks(column, "gz")
    summed = parts[0]
    for k in range(1, parts.shape[0]):
        summed = summed + parts[k]
    terms = -ground_fric * summed
    gradient = lax.dynamic_slice_in_dim(terms, gz * half_cols, half_cols, 1)
    return (own, gradient)


def n_layer_halos(u):
    count = lax.axis_size("gz")
    head = u[:1]
    tail = u[-1:]
    if count == 2:
        first = lax.axis_index("gz") == 0
        got = lax.ppermute(jnp.where(first, tail, head), "gz", [(0, 1), (1, 0)])
        zero = jnp.zeros_like(got)
        return jnp.where(first, zero, got), jnp.where(first, got, zero)
    lo = lax.ppermute(tail, "gz", [(i, i + 1) for i in range(count - 1)])
    hi = lax.ppermute(head, "gz", [(i + 1, i) for i in range(count - 1)])
    return lo, hi


def n_row_halos(u):
    count = lax.axis_size("gy")
    lo = lax.ppermute(u[:, -1:], "gy", [(i, i + 1) for i in range(count - 1)])
    hi = lax.ppermute(u[:, :1], "gy", [(i + 1, i) for i in range(count - 1)])
    return lo, hi


def n_neighbours(u):
    zlo, zhi = n_layer_halos(u)
    ylo, yhi = n_row_halos(u)
    zero = jnp.zeros_like(u[:, :, :1])
    zm = jnp.concatenate([zlo, u[:-1]], axis=0)
    zp = jnp.concatenate([u[1:], zhi], axis=0)
    ym = jnp.concatenate([ylo, u[:, :-1]], axis=1)
    yp = jnp.concatenate([u[:, 1:], yhi], axis=1)
    xm = jnp.concatenate([zero, u[:, :, :-1]], axis=2)
    xp = jnp.concatenate([u[:, :, 1:], zero], axis=2)
    return zm, zp, ym, yp, xm, xp


def n_face_set(eta):
    zm, zp, ym, yp, xm, xp = n_neighbours(eta)
    zlo = VERT * (0.5 * (eta + zm))
    zhi = VERT * (0.5 * (eta + zp))
    ylo = 0.5 * (eta + ym)
    yhi = 0.5 * (eta + yp)
    xlo = 0.5 * (eta + xm)
    xhi = 0.5 * (eta + xp)
    return (zlo, zhi, ylo, yhi, xlo, xhi)


def n_operate(u, coef):
    zlo, zhi, ylo, yhi, xlo, xhi, extra = coef
    zm, zp, ym, yp, xm, xp = n_neighbours(u)
    out = zlo * (u - zm) + zhi * (u - zp)
    out = out + ylo * (u - ym) + yhi * (u - yp)
    out = out + xlo * (u - xm) + xhi * (u - xp)
    return out + extra * u


def n_diagonal(coef):
    zlo, zhi, ylo, yhi, xlo, xhi, extra = coef
    return zlo + zhi + ylo + yhi + xlo + xhi + extra


def n_pick_matrix(cols):
    half = cols // 2
    src = lax.broadcasted_iota(jnp.int32, (cols, cols), 0)
    dst = lax.broadcasted_iota(jnp.int32, (cols, cols), 1)
    want = jnp.where(dst < half, 2 * dst, 2 * (dst - half) + 1)
    return (src == want).astype(jnp.float32)


def n_split_x(a):
    cols = a.shape[-1]
    both = jnp.dot(a, n_pick_matrix(cols), precision=HI)
    return both[..., : cols // 2], both[..., cols // 2 :]


def n_mean_four(a):
    e0, o0 = n_split_x(a[:, 0::2])
    e1, o1 = n_split_x(a[:, 1::2])
    return 0.25 * (e0 + e1 + o0 + o1)


def n_coarsen(coef):
    zlo, zhi, ylo, yhi, xlo, xhi, extra = coef
    xlo_e, _ = n_split_x(xlo[:, 0::2] + xlo[:, 1::2])
    _, xhi_o = n_split_x(xhi[:, 0::2] + xhi[:, 1::2])
    ylo_e, ylo_o = n_split_x(ylo[:, 0::2])
    yhi_e, yhi_o = n_split_x(yhi[:, 1::2])
    cxlo = 0.125 * xlo_e
    cxhi = 0.125 * xhi_o
    cylo = 0.125 * (ylo_e + ylo_o)
    cyhi = 0.125 * (yhi_e + yhi_o)
    return (n_mean_four(zlo), n_mean_four(zhi), cylo, cyhi, cxlo, cxhi, n_mean_four(extra))


def n_prolong(field):
    cols = field.shape[-1]
    src = lax.broadcasted_iota(jnp.int32, (cols, 2 * cols), 0)
    dst = lax.broadcasted_iota(jnp.int32, (cols, 2 * cols), 1)
    spread = (src == dst // 2).astype(jnp.float32)
    wide = jnp.dot(field, spread, precision=HI)
    return jnp.repeat(wide, 2, axis=1)


def n_sweep(field, rhs, coef, diag):
    return field + OMEGA * (rhs - n_operate(field, coef)) / diag


def n_body(viscosity, adjoint_source, forward_velocity, friction, ice_mask, grounded_mask):
    layers = viscosity.shape[0]
    cols = viscosity.shape[2]
    half_cols = cols // 2
    gz = lax.axis_index("gz")
    total_layers = layers * lax.axis_size("gz")
    layer = (gz * layers + jnp.arange(layers)).astype(jnp.float32)
    profile = (jnp.float32(total_layers) - layer) / jnp.float32(total_layers)
    wsq = profile * profile
    icef = ice_mask.astype(jnp.float32)
    groundf = grounded_mask.astype(jnp.float32)
    base = 0.05 + 2.0 * (1.0 - icef)
    ground_fric = groundf * friction
    stacked = jnp.concatenate([viscosity, adjoint_source, base[None], ground_fric[None]], axis=0)
    gathered = lax.all_gather(stacked, "gx", axis=0, tiled=False)
    count_x = gathered.shape[0]
    gathered = jnp.concatenate([gathered[i] for i in range(count_x)], axis=2)
    visc_all = gathered[:layers]
    source_all = gathered[layers : 2 * layers]
    base_all = gathered[2 * layers]
    gfr_all = gathered[2 * layers + 1]
    extra = base_all[None, :, :] + gfr_all[None, :, :] * wsq[:, None, None]
    fine = n_face_set(visc_all) + (extra,)
    dfine = n_diagonal(fine)
    middle = n_coarsen(fine)
    dmid = n_diagonal(middle)
    coarse = n_coarsen(middle)
    dcoarse = n_diagonal(coarse)
    lam = OMEGA * source_all / dfine
    for i in range(S0 - 1):
        lam = n_sweep(lam, source_all, fine, dfine)
    b_mid = n_mean_four(source_all - n_operate(lam, fine))
    e_mid = OMEGA * b_mid / dmid
    for i in range(S1 - 1):
        e_mid = n_sweep(e_mid, b_mid, middle, dmid)
    b_low = n_mean_four(b_mid - n_operate(e_mid, middle))
    e_low = OMEGA * b_low / dcoarse
    for i in range(S2 - 1):
        e_low = n_sweep(e_low, b_low, coarse, dcoarse)
    e_mid = e_mid + n_prolong(e_low)
    for i in range(S1):
        e_mid = n_sweep(e_mid, b_mid, middle, dmid)
    lam = lam + n_prolong(e_mid)
    for i in range(S0):
        lam = n_sweep(lam, source_all, fine, dfine)
    own = lax.dynamic_slice_in_dim(lam, lax.axis_index("gx") * cols, cols, 2)
    column = jnp.sum(wsq[:, None, None] * forward_velocity * own, axis=0)
    summed = lax.psum(column, "gz")
    terms = -ground_fric * summed
    gradient = lax.dynamic_slice_in_dim(terms, gz * half_cols, half_cols, 1)
    return (own, gradient)


def body(viscosity, *rest):
    layers, own_rows, cols_own = viscosity.shape
    cols_all = cols_own + 2 * COL_HALO
    wide_bytes = 4 * layers * (own_rows + 2 * FINE_HALO + 2) * cols_all
    if COL_HALO <= cols_own and FINE_HALO + 1 <= own_rows and MID_HALO <= own_rows // 2 and 20 * wide_bytes <= 40 * 2**20 and lax.axis_size("gy") <= 8:
        return body_wide(viscosity, *rest)
    return n_body(viscosity, *rest)


def solution(mesh):
    placed = (
        P("gz", "gy", "gx"),
        P("gz", "gy", "gx"),
        P("gz", "gy", "gx"),
        P("gy", "gx"),
        P("gy", "gx"),
        P("gy", "gx"),
    )
    return jax.shard_map(
        body,
        mesh=mesh,
        in_specs=placed,
        out_specs=(P("gz", "gy", "gx"), P("gy", ("gx", "gz"))),
        check_vma=False,
    )
```

```python
import jax
import jax.numpy as jnp
from jax import lax
from jax.sharding import PartitionSpec as P

S0 = 4
S1 = 4
S2 = 8


OMEGA = 0.8
VERT = 4.0
HI = lax.Precision.HIGHEST
FINE_HALO = 12
MID_HALO = 6
POST_HALO = 4
COL_HALO = 64


def layer_halos(u):
    count = lax.axis_size("gz")
    head = u[:1]
    tail = u[-1:]
    if count == 2:
        first = lax.axis_index("gz") == 0
        got = lax.ppermute(jnp.where(first, tail, head), "gz", [(0, 1), (1, 0)])
        zero = jnp.zeros_like(got)
        return jnp.where(first, zero, got), jnp.where(first, got, zero)
    lo = lax.ppermute(tail, "gz", [(i, i + 1) for i in range(count - 1)])
    hi = lax.ppermute(head, "gz", [(i + 1, i) for i in range(count - 1)])
    return lo, hi


def extend_rows(a, h):
    count = lax.axis_size("gy")
    lo = lax.ppermute(a[:, -h:], "gy", [(i, i + 1) for i in range(count - 1)])
    hi = lax.ppermute(a[:, :h], "gy", [(i + 1, i) for i in range(count - 1)])
    return jnp.concatenate([lo, a, hi], axis=1)


def gather_blocks(a, axis):
    count = lax.axis_size(axis)
    got = [a]
    for s in range(1, count):
        got.append(lax.ppermute(a, axis, [(i, (i + s) % count) for i in range(count)]))
    rev = jnp.stack(got[::-1], axis=0)
    return jnp.roll(rev, lax.axis_index(axis) + 1, axis=0)


def extend_cols(a, h):
    count = lax.axis_size("gx")
    lo = lax.ppermute(a[:, :, -h:], "gx", [(i, i + 1) for i in range(count - 1)])
    hi = lax.ppermute(a[:, :, :h], "gx", [(i + 1, i) for i in range(count - 1)])
    return jnp.concatenate([lo, a, hi], axis=2)


def col_mask(own_cols, h):
    g = lax.axis_index("gx") * own_cols - h + lax.broadcasted_iota(jnp.int32, (1, 1, own_cols + 2 * h), 2)
    return (g >= 0) & (g < own_cols * lax.axis_size("gx"))


def crop(a, h_from, h_to):
    cut = h_from - h_to
    return a[:, cut : a.shape[1] - cut]


def row_mask(own_rows, h):
    g = lax.axis_index("gy") * own_rows - h + lax.broadcasted_iota(jnp.int32, (1, own_rows + 2 * h, 1), 1)
    return (g >= 0) & (g < own_rows * lax.axis_size("gy"))


def neighbours(u):
    zlo, zhi = layer_halos(u)
    zero_row = jnp.zeros_like(u[:, :1])
    zero_col = jnp.zeros_like(u[:, :, :1])
    zm = jnp.concatenate([zlo, u[:-1]], axis=0)
    zp = jnp.concatenate([u[1:], zhi], axis=0)
    ym = jnp.concatenate([zero_row, u[:, :-1]], axis=1)
    yp = jnp.concatenate([u[:, 1:], zero_row], axis=1)
    xm = jnp.concatenate([zero_col, u[:, :, :-1]], axis=2)
    xp = jnp.concatenate([u[:, :, 1:], zero_col], axis=2)
    return zm, zp, ym, yp, xm, xp


def face_set(eta):
    zm, zp, ym, yp, xm, xp = neighbours(eta)
    zlo = VERT * (0.5 * (eta + zm))
    zhi = VERT * (0.5 * (eta + zp))
    ylo = 0.5 * (eta + ym)
    yhi = 0.5 * (eta + yp)
    xlo = 0.5 * (eta + xm)
    xhi = 0.5 * (eta + xp)
    return (zlo, zhi, ylo, yhi, xlo, xhi)


def operate(u, coef):
    zlo, zhi, ylo, yhi, xlo, xhi, extra = coef
    zm, zp, ym, yp, xm, xp = neighbours(u)
    out = zlo * (u - zm) + zhi * (u - zp)
    out = out + ylo * (u - ym) + yhi * (u - yp)
    out = out + xlo * (u - xm) + xhi * (u - xp)
    return out + extra * u


def diagonal(coef):
    zlo, zhi, ylo, yhi, xlo, xhi, extra = coef
    return zlo + zhi + ylo + yhi + xlo + xhi + extra


def pick(n, parity):
    src = lax.broadcasted_iota(jnp.int32, (n, n // 2), 0)
    dst = lax.broadcasted_iota(jnp.int32, (n, n // 2), 1)
    return (src == 2 * dst + parity).astype(jnp.float32)


def cols(a, parity):
    return jnp.dot(a, pick(a.shape[-1], parity), precision=HI)


def rows(a, parity):
    return jnp.einsum("yr,zyx->zrx", pick(a.shape[1], parity), a, precision=HI)


def mean_four(a):
    r0 = rows(a, 0)
    r1 = rows(a, 1)
    return 0.25 * (cols(r0, 0) + cols(r1, 0) + cols(r0, 1) + cols(r1, 1))


def coarsen(coef):
    zlo, zhi, ylo, yhi, xlo, xhi, extra = coef
    cxlo = 0.125 * cols(rows(xlo, 0) + rows(xlo, 1), 0)
    cxhi = 0.125 * cols(rows(xhi, 0) + rows(xhi, 1), 1)
    ylo0 = rows(ylo, 0)
    yhi1 = rows(yhi, 1)
    cylo = 0.125 * (cols(ylo0, 0) + cols(ylo0, 1))
    cyhi = 0.125 * (cols(yhi1, 0) + cols(yhi1, 1))
    return (mean_four(zlo), mean_four(zhi), cylo, cyhi, cxlo, cxhi, mean_four(extra))


def coarsen_stacked(coef):
    layers = coef[0].shape[0]
    width = coef[0].shape[2]
    half = width // 2
    stack = jnp.concatenate(coef, axis=0)
    both_rows = jnp.concatenate([rows(stack, 0), rows(stack, 1)], axis=0)
    src = lax.broadcasted_iota(jnp.int32, (width, width), 0)
    dst = lax.broadcasted_iota(jnp.int32, (width, width), 1)
    want = jnp.where(dst < half, 2 * dst, 2 * (dst - half) + 1)
    picked = jnp.dot(both_rows, (src == want).astype(jnp.float32), precision=HI)
    count = len(coef)

    def part(k, odd_row, odd_col):
        at = (odd_row * count + k) * layers
        return picked[at : at + layers, :, odd_col * half : (odd_col + 1) * half]

    def four(k):
        return 0.25 * (part(k, 0, 0) + part(k, 1, 0) + part(k, 0, 1) + part(k, 1, 1))

    cxlo = 0.125 * (part(4, 0, 0) + part(4, 1, 0))
    cxhi = 0.125 * (part(5, 0, 1) + part(5, 1, 1))
    cylo = 0.125 * (part(2, 0, 0) + part(2, 0, 1))
    cyhi = 0.125 * (part(3, 1, 0) + part(3, 1, 1))
    return (four(0), four(1), cylo, cyhi, cxlo, cxhi, four(6))


def spread(n):
    src = lax.broadcasted_iota(jnp.int32, (n, 2 * n), 0)
    dst = lax.broadcasted_iota(jnp.int32, (n, 2 * n), 1)
    return (src == dst // 2).astype(jnp.float32)


def prolong(field):
    wide = jnp.dot(field, spread(field.shape[-1]), precision=HI)
    return jnp.einsum("ry,zrx->zyx", spread(field.shape[1]), wide, precision=HI)


def sweep(field, rhs, coef, diag, inside):
    new = field + OMEGA * (rhs - operate(field, coef)) / diag
    return jnp.where(inside, new, 0.0)


def smooth(field, rhs, coef, diag, inside, count):
    for i in range(count):
        field = sweep(field, rhs, coef, diag, inside)
    return field


def crop_all(arrs, h_from, h_to):
    return tuple(crop(a, h_from, h_to) for a in arrs)


def body_wide(viscosity, adjoint_source, forward_velocity, friction, ice_mask, grounded_mask):
    layers = viscosity.shape[0]
    own_rows = viscosity.shape[1]
    mid_rows = own_rows // 2
    cols_own = viscosity.shape[2]
    half_cols = cols_own // 2
    gz = lax.axis_index("gz")
    gy = lax.axis_index("gy")
    total_layers = layers * lax.axis_size("gz")
    layer = (gz * layers + jnp.arange(layers)).astype(jnp.float32)
    profile = (jnp.float32(total_layers) - layer) / jnp.float32(total_layers)
    wsq = profile * profile
    icef = ice_mask.astype(jnp.float32)
    groundf = grounded_mask.astype(jnp.float32)
    base = 0.05 + 2.0 * (1.0 - icef)
    ground_fric = groundf * friction
    stacked = jnp.concatenate([viscosity, adjoint_source, base[None], ground_fric[None]], axis=0)
    hv = FINE_HALO + 1
    wide = extend_cols(stacked, COL_HALO)
    ext = extend_rows(jnp.concatenate([wide[:layers], wide[2 * layers :]], axis=0), hv)
    src_e = crop(extend_rows(wide[layers : 2 * layers], hv), hv, FINE_HALO)
    visc_e = ext[:layers]
    base_e = crop(ext[layers : layers + 1], hv, FINE_HALO)[0]
    gfr_e = crop(ext[layers + 1 : layers + 2], hv, FINE_HALO)[0]
    extra = base_e[None, :, :] + gfr_e[None, :, :] * wsq[:, None, None]
    fine = crop_all(face_set(visc_e), hv, FINE_HALO) + (extra,)
    dfine = diagonal(fine)
    middle = coarsen_stacked(fine)
    dmid = diagonal(middle)
    coarse_own = coarsen_stacked(crop_all(middle, FINE_HALO // 2, 0))
    coarse_all = gather_blocks(jnp.concatenate(coarse_own, axis=0), "gy")
    coarse_all = jnp.concatenate([coarse_all[i] for i in range(coarse_all.shape[0])], axis=1)
    coarse = tuple(coarse_all[i * layers : (i + 1) * layers] for i in range(7))
    dcoarse = diagonal(coarse)
    in_fine = row_mask(own_rows, FINE_HALO) & col_mask(cols_own, COL_HALO)
    in_mid = row_mask(mid_rows, FINE_HALO // 2) & col_mask(cols_own // 2, COL_HALO // 2)

    lam = jnp.where(in_fine, OMEGA * src_e / dfine, 0.0)
    lam = smooth(lam, src_e, fine, dfine, in_fine, S0 - 1)
    b_mid = mean_four(src_e - operate(lam, fine))
    e_mid = jnp.where(in_mid, OMEGA * b_mid / dmid, 0.0)
    e_mid = smooth(e_mid, b_mid, middle, dmid, in_mid, S1 - 1)
    hm = FINE_HALO // 2
    res_mid = crop(b_mid - operate(e_mid, middle), hm, 0)
    b_low = gather_blocks(mean_four(res_mid), "gy")
    b_low = jnp.concatenate([b_low[i] for i in range(b_low.shape[0])], axis=1)
    ones = col_mask(cols_own // 4, COL_HALO // 4)
    e_low = jnp.where(ones, OMEGA * b_low / dcoarse, 0.0)
    e_low = smooth(e_low, b_low, coarse, dcoarse, ones, S2 - 1)

    pair = jnp.concatenate([crop(e_mid, hm, 0), crop(b_mid, hm, 0)], axis=0)
    pair = extend_rows(pair, MID_HALO)
    e_mid = pair[:layers]
    b_mid = pair[layers:]
    low_rows = own_rows // 4
    ch = MID_HALO // 2
    padded = jnp.pad(e_low, ((0, 0), (ch, ch), (0, 0)))
    e_near = lax.dynamic_slice_in_dim(padded, gy * low_rows, low_rows + 2 * ch, 1)
    e_mid = e_mid + prolong(e_near)
    middle_p = crop_all(middle, hm, MID_HALO)
    dmid_p = crop(dmid, hm, MID_HALO)
    in_mid_p = row_mask(mid_rows, MID_HALO) & col_mask(cols_own // 2, COL_HALO // 2)
    e_mid = smooth(e_mid, b_mid, middle_p, dmid_p, in_mid_p, S1)

    lam = crop(lam, FINE_HALO, POST_HALO) + prolong(crop(e_mid, MID_HALO, POST_HALO // 2))
    fine_p = crop_all(fine, FINE_HALO, POST_HALO)
    dfine_p = crop(dfine, FINE_HALO, POST_HALO)
    src_p = crop(src_e, FINE_HALO, POST_HALO)
    in_fine_p = row_mask(own_rows, POST_HALO) & col_mask(cols_own, COL_HALO)
    lam = smooth(lam, src_p, fine_p, dfine_p, in_fine_p, S0)
    lam = crop(lam, POST_HALO, 0)

    own = lam[:, :, COL_HALO : COL_HALO + cols_own]
    column = jnp.sum(wsq[:, None, None] * forward_velocity * own, axis=0)
    parts = gather_blocks(column, "gz")
    summed = parts[0]
    for k in range(1, parts.shape[0]):
        summed = summed + parts[k]
    terms = -ground_fric * summed
    gradient = lax.dynamic_slice_in_dim(terms, gz * half_cols, half_cols, 1)
    return (own, gradient)


def n_layer_halos(u):
    count = lax.axis_size("gz")
    head = u[:1]
    tail = u[-1:]
    if count == 2:
        first = lax.axis_index("gz") == 0
        got = lax.ppermute(jnp.where(first, tail, head), "gz", [(0, 1), (1, 0)])
        zero = jnp.zeros_like(got)
        return jnp.where(first, zero, got), jnp.where(first, got, zero)
    lo = lax.ppermute(tail, "gz", [(i, i + 1) for i in range(count - 1)])
    hi = lax.ppermute(head, "gz", [(i + 1, i) for i in range(count - 1)])
    return lo, hi


def n_row_halos(u):
    count = lax.axis_size("gy")
    lo = lax.ppermute(u[:, -1:], "gy", [(i, i + 1) for i in range(count - 1)])
    hi = lax.ppermute(u[:, :1], "gy", [(i + 1, i) for i in range(count - 1)])
    return lo, hi


def n_neighbours(u):
    zlo, zhi = n_layer_halos(u)
    ylo, yhi = n_row_halos(u)
    zero = jnp.zeros_like(u[:, :, :1])
    zm = jnp.concatenate([zlo, u[:-1]], axis=0)
    zp = jnp.concatenate([u[1:], zhi], axis=0)
    ym = jnp.concatenate([ylo, u[:, :-1]], axis=1)
    yp = jnp.concatenate([u[:, 1:], yhi], axis=1)
    xm = jnp.concatenate([zero, u[:, :, :-1]], axis=2)
    xp = jnp.concatenate([u[:, :, 1:], zero], axis=2)
    return zm, zp, ym, yp, xm, xp


def n_face_set(eta):
    zm, zp, ym, yp, xm, xp = n_neighbours(eta)
    zlo = VERT * (0.5 * (eta + zm))
    zhi = VERT * (0.5 * (eta + zp))
    ylo = 0.5 * (eta + ym)
    yhi = 0.5 * (eta + yp)
    xlo = 0.5 * (eta + xm)
    xhi = 0.5 * (eta + xp)
    return (zlo, zhi, ylo, yhi, xlo, xhi)


def n_operate(u, coef):
    zlo, zhi, ylo, yhi, xlo, xhi, extra = coef
    zm, zp, ym, yp, xm, xp = n_neighbours(u)
    out = zlo * (u - zm) + zhi * (u - zp)
    out = out + ylo * (u - ym) + yhi * (u - yp)
    out = out + xlo * (u - xm) + xhi * (u - xp)
    return out + extra * u


def n_diagonal(coef):
    zlo, zhi, ylo, yhi, xlo, xhi, extra = coef
    return zlo + zhi + ylo + yhi + xlo + xhi + extra


def n_pick_matrix(cols):
    half = cols // 2
    src = lax.broadcasted_iota(jnp.int32, (cols, cols), 0)
    dst = lax.broadcasted_iota(jnp.int32, (cols, cols), 1)
    want = jnp.where(dst < half, 2 * dst, 2 * (dst - half) + 1)
    return (src == want).astype(jnp.float32)


def n_split_x(a):
    cols = a.shape[-1]
    both = jnp.dot(a, n_pick_matrix(cols), precision=HI)
    return both[..., : cols // 2], both[..., cols // 2 :]


def n_mean_four(a):
    e0, o0 = n_split_x(a[:, 0::2])
    e1, o1 = n_split_x(a[:, 1::2])
    return 0.25 * (e0 + e1 + o0 + o1)


def n_coarsen(coef):
    zlo, zhi, ylo, yhi, xlo, xhi, extra = coef
    xlo_e, _ = n_split_x(xlo[:, 0::2] + xlo[:, 1::2])
    _, xhi_o = n_split_x(xhi[:, 0::2] + xhi[:, 1::2])
    ylo_e, ylo_o = n_split_x(ylo[:, 0::2])
    yhi_e, yhi_o = n_split_x(yhi[:, 1::2])
    cxlo = 0.125 * xlo_e
    cxhi = 0.125 * xhi_o
    cylo = 0.125 * (ylo_e + ylo_o)
    cyhi = 0.125 * (yhi_e + yhi_o)
    return (n_mean_four(zlo), n_mean_four(zhi), cylo, cyhi, cxlo, cxhi, n_mean_four(extra))


def n_prolong(field):
    cols = field.shape[-1]
    src = lax.broadcasted_iota(jnp.int32, (cols, 2 * cols), 0)
    dst = lax.broadcasted_iota(jnp.int32, (cols, 2 * cols), 1)
    spread = (src == dst // 2).astype(jnp.float32)
    wide = jnp.dot(field, spread, precision=HI)
    return jnp.repeat(wide, 2, axis=1)


def n_sweep(field, rhs, coef, diag):
    return field + OMEGA * (rhs - n_operate(field, coef)) / diag


def n_body(viscosity, adjoint_source, forward_velocity, friction, ice_mask, grounded_mask):
    layers = viscosity.shape[0]
    cols = viscosity.shape[2]
    half_cols = cols // 2
    gz = lax.axis_index("gz")
    total_layers = layers * lax.axis_size("gz")
    layer = (gz * layers + jnp.arange(layers)).astype(jnp.float32)
    profile = (jnp.float32(total_layers) - layer) / jnp.float32(total_layers)
    wsq = profile * profile
    icef = ice_mask.astype(jnp.float32)
    groundf = grounded_mask.astype(jnp.float32)
    base = 0.05 + 2.0 * (1.0 - icef)
    ground_fric = groundf * friction
    stacked = jnp.concatenate([viscosity, adjoint_source, base[None], ground_fric[None]], axis=0)
    gathered = lax.all_gather(stacked, "gx", axis=0, tiled=False)
    count_x = gathered.shape[0]
    gathered = jnp.concatenate([gathered[i] for i in range(count_x)], axis=2)
    visc_all = gathered[:layers]
    source_all = gathered[layers : 2 * layers]
    base_all = gathered[2 * layers]
    gfr_all = gathered[2 * layers + 1]
    extra = base_all[None, :, :] + gfr_all[None, :, :] * wsq[:, None, None]
    fine = n_face_set(visc_all) + (extra,)
    dfine = n_diagonal(fine)
    middle = n_coarsen(fine)
    dmid = n_diagonal(middle)
    coarse = n_coarsen(middle)
    dcoarse = n_diagonal(coarse)
    lam = OMEGA * source_all / dfine
    for i in range(S0 - 1):
        lam = n_sweep(lam, source_all, fine, dfine)
    b_mid = n_mean_four(source_all - n_operate(lam, fine))
    e_mid = OMEGA * b_mid / dmid
    for i in range(S1 - 1):
        e_mid = n_sweep(e_mid, b_mid, middle, dmid)
    b_low = n_mean_four(b_mid - n_operate(e_mid, middle))
    e_low = OMEGA * b_low / dcoarse
    for i in range(S2 - 1):
        e_low = n_sweep(e_low, b_low, coarse, dcoarse)
    e_mid = e_mid + n_prolong(e_low)
    for i in range(S1):
        e_mid = n_sweep(e_mid, b_mid, middle, dmid)
    lam = lam + n_prolong(e_mid)
    for i in range(S0):
        lam = n_sweep(lam, source_all, fine, dfine)
    own = lax.dynamic_slice_in_dim(lam, lax.axis_index("gx") * cols, cols, 2)
    column = jnp.sum(wsq[:, None, None] * forward_velocity * own, axis=0)
    summed = lax.psum(column, "gz")
    terms = -ground_fric * summed
    gradient = lax.dynamic_slice_in_dim(terms, gz * half_cols, half_cols, 1)
    return (own, gradient)


def body(viscosity, *rest):
    layers, own_rows, cols_own = viscosity.shape
    cols_all = cols_own + 2 * COL_HALO
    wide_bytes = 4 * layers * (own_rows + 2 * FINE_HALO + 2) * cols_all
    if COL_HALO <= cols_own and FINE_HALO + 1 <= own_rows and MID_HALO <= own_rows // 2 and 20 * wide_bytes <= 40 * 2**20 and lax.axis_size("gy") <= 8:
        return body_wide(viscosity, *rest)
    return n_body(viscosity, *rest)


def solution(mesh):
    placed = (
        P("gz", "gy", "gx"),
        P("gz", "gy", "gx"),
        P("gz", "gy", "gx"),
        P("gy", "gx"),
        P("gy", "gx"),
        P("gy", "gx"),
    )
    return jax.shard_map(
        body,
        mesh=mesh,
        in_specs=placed,
        out_specs=(P("gz", "gy", "gx"), P("gy", ("gx", "gz"))),
        check_vma=False,
    )
```

```python
import jax
import jax.numpy as jnp
from jax import lax
from jax.sharding import PartitionSpec as P

S0 = 4
S1 = 4
S2 = 8


OMEGA = 0.8
VERT = 4.0
HI = lax.Precision.HIGHEST
FINE_HALO = 12
MID_HALO = 6
POST_HALO = 4
COL_HALO = 64


def layer_halos(u):
    count = lax.axis_size("gz")
    head = u[:1]
    tail = u[-1:]
    if count == 2:
        first = lax.axis_index("gz") == 0
        got = lax.ppermute(jnp.where(first, tail, head), "gz", [(0, 1), (1, 0)])
        zero = jnp.zeros_like(got)
        return jnp.where(first, zero, got), jnp.where(first, got, zero)
    lo = lax.ppermute(tail, "gz", [(i, i + 1) for i in range(count - 1)])
    hi = lax.ppermute(head, "gz", [(i + 1, i) for i in range(count - 1)])
    return lo, hi


def extend_rows(a, h):
    count = lax.axis_size("gy")
    lo = lax.ppermute(a[:, -h:], "gy", [(i, i + 1) for i in range(count - 1)])
    hi = lax.ppermute(a[:, :h], "gy", [(i + 1, i) for i in range(count - 1)])
    return jnp.concatenate([lo, a, hi], axis=1)


def gather_blocks(a, axis):
    count = lax.axis_size(axis)
    got = [a]
    for s in range(1, count):
        got.append(lax.ppermute(a, axis, [(i, (i + s) % count) for i in range(count)]))
    rev = jnp.stack(got[::-1], axis=0)
    return jnp.roll(rev, lax.axis_index(axis) + 1, axis=0)


def extend_cols(a, h):
    count = lax.axis_size("gx")
    lo = lax.ppermute(a[:, :, -h:], "gx", [(i, i + 1) for i in range(count - 1)])
    hi = lax.ppermute(a[:, :, :h], "gx", [(i + 1, i) for i in range(count - 1)])
    return jnp.concatenate([lo, a, hi], axis=2)


def col_mask(own_cols, h):
    g = lax.axis_index("gx") * own_cols - h + lax.broadcasted_iota(jnp.int32, (1, 1, own_cols + 2 * h), 2)
    return (g >= 0) & (g < own_cols * lax.axis_size("gx"))


def crop(a, h_from, h_to):
    cut = h_from - h_to
    return a[:, cut : a.shape[1] - cut]


def row_mask(own_rows, h):
    g = lax.axis_index("gy") * own_rows - h + lax.broadcasted_iota(jnp.int32, (1, own_rows + 2 * h, 1), 1)
    return (g >= 0) & (g < own_rows * lax.axis_size("gy"))


def neighbours(u):
    zlo, zhi = layer_halos(u)
    zero_row = jnp.zeros_like(u[:, :1])
    zero_col = jnp.zeros_like(u[:, :, :1])
    zm = jnp.concatenate([zlo, u[:-1]], axis=0)
    zp = jnp.concatenate([u[1:], zhi], axis=0)
    ym = jnp.concatenate([zero_row, u[:, :-1]], axis=1)
    yp = jnp.concatenate([u[:, 1:], zero_row], axis=1)
    xm = jnp.concatenate([zero_col, u[:, :, :-1]], axis=2)
    xp = jnp.concatenate([u[:, :, 1:], zero_col], axis=2)
    return zm, zp, ym, yp, xm, xp


def face_set(eta):
    zm, zp, ym, yp, xm, xp = neighbours(eta)
    zlo = VERT * (0.5 * (eta + zm))
    zhi = VERT * (0.5 * (eta + zp))
    ylo = 0.5 * (eta + ym)
    yhi = 0.5 * (eta + yp)
    xlo = 0.5 * (eta + xm)
    xhi = 0.5 * (eta + xp)
    return (zlo, zhi, ylo, yhi, xlo, xhi)


def operate(u, coef):
    zlo, zhi, ylo, yhi, xlo, xhi, extra = coef
    zm, zp, ym, yp, xm, xp = neighbours(u)
    out = zlo * (u - zm) + zhi * (u - zp)
    out = out + ylo * (u - ym) + yhi * (u - yp)
    out = out + xlo * (u - xm) + xhi * (u - xp)
    return out + extra * u


def diagonal(coef):
    zlo, zhi, ylo, yhi, xlo, xhi, extra = coef
    return zlo + zhi + ylo + yhi + xlo + xhi + extra


def pick(n, parity):
    src = lax.broadcasted_iota(jnp.int32, (n, n // 2), 0)
    dst = lax.broadcasted_iota(jnp.int32, (n, n // 2), 1)
    return (src == 2 * dst + parity).astype(jnp.float32)


def cols(a, parity):
    return jnp.dot(a, pick(a.shape[-1], parity), precision=HI)


def rows(a, parity):
    return jnp.einsum("yr,zyx->zrx", pick(a.shape[1], parity), a, precision=HI)


def mean_four(a):
    r0 = rows(a, 0)
    r1 = rows(a, 1)
    return 0.25 * (cols(r0, 0) + cols(r1, 0) + cols(r0, 1) + cols(r1, 1))


def coarsen(coef):
    zlo, zhi, ylo, yhi, xlo, xhi, extra = coef
    cxlo = 0.125 * cols(rows(xlo, 0) + rows(xlo, 1), 0)
    cxhi = 0.125 * cols(rows(xhi, 0) + rows(xhi, 1), 1)
    ylo0 = rows(ylo, 0)
    yhi1 = rows(yhi, 1)
    cylo = 0.125 * (cols(ylo0, 0) + cols(ylo0, 1))
    cyhi = 0.125 * (cols(yhi1, 0) + cols(yhi1, 1))
    return (mean_four(zlo), mean_four(zhi), cylo, cyhi, cxlo, cxhi, mean_four(extra))


def coarsen_stacked(coef):
    layers = coef[0].shape[0]
    width = coef[0].shape[2]
    half = width // 2
    stack = jnp.concatenate(coef, axis=0)
    both_rows = jnp.concatenate([rows(stack, 0), rows(stack, 1)], axis=0)
    src = lax.broadcasted_iota(jnp.int32, (width, width), 0)
    dst = lax.broadcasted_iota(jnp.int32, (width, width), 1)
    want = jnp.where(dst < half, 2 * dst, 2 * (dst - half) + 1)
    picked = jnp.dot(both_rows, (src == want).astype(jnp.float32), precision=HI)
    count = len(coef)

    def part(k, odd_row, odd_col):
        at = (odd_row * count + k) * layers
        return picked[at : at + layers, :, odd_col * half : (odd_col + 1) * half]

    def four(k):
        return 0.25 * (part(k, 0, 0) + part(k, 1, 0) + part(k, 0, 1) + part(k, 1, 1))

    cxlo = 0.125 * (part(4, 0, 0) + part(4, 1, 0))
    cxhi = 0.125 * (part(5, 0, 1) + part(5, 1, 1))
    cylo = 0.125 * (part(2, 0, 0) + part(2, 0, 1))
    cyhi = 0.125 * (part(3, 1, 0) + part(3, 1, 1))
    return (four(0), four(1), cylo, cyhi, cxlo, cxhi, four(6))


def spread(n):
    src = lax.broadcasted_iota(jnp.int32, (n, 2 * n), 0)
    dst = lax.broadcasted_iota(jnp.int32, (n, 2 * n), 1)
    return (src == dst // 2).astype(jnp.float32)


def prolong(field):
    wide = jnp.dot(field, spread(field.shape[-1]), precision=HI)
    return jnp.einsum("ry,zrx->zyx", spread(field.shape[1]), wide, precision=HI)


def sweep(field, rhs, coef, diag, inside):
    new = field + OMEGA * (rhs - operate(field, coef)) / diag
    return jnp.where(inside, new, 0.0)


def smooth(field, rhs, coef, diag, inside, count):
    for i in range(count):
        field = sweep(field, rhs, coef, diag, inside)
    return field


def crop_all(arrs, h_from, h_to):
    return tuple(crop(a, h_from, h_to) for a in arrs)


def body_wide(viscosity, adjoint_source, forward_velocity, friction, ice_mask, grounded_mask):
    layers = viscosity.shape[0]
    own_rows = viscosity.shape[1]
    mid_rows = own_rows // 2
    cols_own = viscosity.shape[2]
    half_cols = cols_own // 2
    gz = lax.axis_index("gz")
    gy = lax.axis_index("gy")
    total_layers = layers * lax.axis_size("gz")
    layer = (gz * layers + jnp.arange(layers)).astype(jnp.float32)
    profile = (jnp.float32(total_layers) - layer) / jnp.float32(total_layers)
    wsq = profile * profile
    icef = ice_mask.astype(jnp.float32)
    groundf = grounded_mask.astype(jnp.float32)
    base = 0.05 + 2.0 * (1.0 - icef)
    ground_fric = groundf * friction
    stacked = jnp.concatenate([viscosity, adjoint_source, base[None], ground_fric[None]], axis=0)
    hv = FINE_HALO + 1
    ext = extend_rows(extend_cols(jnp.concatenate([stacked[:layers], stacked[2 * layers :]], axis=0), COL_HALO), hv)
    src_e = crop(extend_rows(extend_cols(stacked[layers : 2 * layers], COL_HALO), hv), hv, FINE_HALO)
    visc_e = ext[:layers]
    base_e = crop(ext[layers : layers + 1], hv, FINE_HALO)[0]
    gfr_e = crop(ext[layers + 1 : layers + 2], hv, FINE_HALO)[0]
    extra = base_e[None, :, :] + gfr_e[None, :, :] * wsq[:, None, None]
    fine = crop_all(face_set(visc_e), hv, FINE_HALO) + (extra,)
    dfine = diagonal(fine)
    middle = coarsen_stacked(fine)
    dmid = diagonal(middle)
    coarse_own = coarsen_stacked(crop_all(middle, FINE_HALO // 2, 0))
    coarse_all = gather_blocks(jnp.concatenate(coarse_own, axis=0), "gy")
    coarse_all = jnp.concatenate([coarse_all[i] for i in range(coarse_all.shape[0])], axis=1)
    coarse = tuple(coarse_all[i * layers : (i + 1) * layers] for i in range(7))
    dcoarse = diagonal(coarse)
    in_fine = row_mask(own_rows, FINE_HALO) & col_mask(cols_own, COL_HALO)
    in_mid = row_mask(mid_rows, FINE_HALO // 2) & col_mask(cols_own // 2, COL_HALO // 2)

    lam = jnp.where(in_fine, OMEGA * src_e / dfine, 0.0)
    lam = smooth(lam, src_e, fine, dfine, in_fine, S0 - 1)
    b_mid = mean_four(src_e - operate(lam, fine))
    e_mid = jnp.where(in_mid, OMEGA * b_mid / dmid, 0.0)
    e_mid = smooth(e_mid, b_mid, middle, dmid, in_mid, S1 - 1)
    hm = FINE_HALO // 2
    res_mid = crop(b_mid - operate(e_mid, middle), hm, 0)
    b_low = gather_blocks(mean_four(res_mid), "gy")
    b_low = jnp.concatenate([b_low[i] for i in range(b_low.shape[0])], axis=1)
    ones = col_mask(cols_own // 4, COL_HALO // 4)
    e_low = jnp.where(ones, OMEGA * b_low / dcoarse, 0.0)
    e_low = smooth(e_low, b_low, coarse, dcoarse, ones, S2 - 1)

    pair = jnp.concatenate([crop(e_mid, hm, 0), crop(b_mid, hm, 0)], axis=0)
    pair = extend_rows(pair, MID_HALO)
    e_mid = pair[:layers]
    b_mid = pair[layers:]
    low_rows = own_rows // 4
    ch = MID_HALO // 2
    padded = jnp.pad(e_low, ((0, 0), (ch, ch), (0, 0)))
    e_near = lax.dynamic_slice_in_dim(padded, gy * low_rows, low_rows + 2 * ch, 1)
    e_mid = e_mid + prolong(e_near)
    middle_p = crop_all(middle, hm, MID_HALO)
    dmid_p = crop(dmid, hm, MID_HALO)
    in_mid_p = row_mask(mid_rows, MID_HALO) & col_mask(cols_own // 2, COL_HALO // 2)
    e_mid = smooth(e_mid, b_mid, middle_p, dmid_p, in_mid_p, S1)

    lam = crop(lam, FINE_HALO, POST_HALO) + prolong(crop(e_mid, MID_HALO, POST_HALO // 2))
    fine_p = crop_all(fine, FINE_HALO, POST_HALO)
    dfine_p = crop(dfine, FINE_HALO, POST_HALO)
    src_p = crop(src_e, FINE_HALO, POST_HALO)
    in_fine_p = row_mask(own_rows, POST_HALO) & col_mask(cols_own, COL_HALO)
    lam = smooth(lam, src_p, fine_p, dfine_p, in_fine_p, S0)
    lam = crop(lam, POST_HALO, 0)

    own = lam[:, :, COL_HALO : COL_HALO + cols_own]
    column = jnp.sum(wsq[:, None, None] * forward_velocity * own, axis=0)
    parts = gather_blocks(column, "gz")
    summed = parts[0]
    for k in range(1, parts.shape[0]):
        summed = summed + parts[k]
    terms = -ground_fric * summed
    gradient = lax.dynamic_slice_in_dim(terms, gz * half_cols, half_cols, 1)
    return (own, gradient)


def n_layer_halos(u):
    count = lax.axis_size("gz")
    head = u[:1]
    tail = u[-1:]
    if count == 2:
        first = lax.axis_index("gz") == 0
        got = lax.ppermute(jnp.where(first, tail, head), "gz", [(0, 1), (1, 0)])
        zero = jnp.zeros_like(got)
        return jnp.where(first, zero, got), jnp.where(first, got, zero)
    lo = lax.ppermute(tail, "gz", [(i, i + 1) for i in range(count - 1)])
    hi = lax.ppermute(head, "gz", [(i + 1, i) for i in range(count - 1)])
    return lo, hi


def n_row_halos(u):
    count = lax.axis_size("gy")
    lo = lax.ppermute(u[:, -1:], "gy", [(i, i + 1) for i in range(count - 1)])
    hi = lax.ppermute(u[:, :1], "gy", [(i + 1, i) for i in range(count - 1)])
    return lo, hi


def n_neighbours(u):
    zlo, zhi = n_layer_halos(u)
    ylo, yhi = n_row_halos(u)
    zero = jnp.zeros_like(u[:, :, :1])
    zm = jnp.concatenate([zlo, u[:-1]], axis=0)
    zp = jnp.concatenate([u[1:], zhi], axis=0)
    ym = jnp.concatenate([ylo, u[:, :-1]], axis=1)
    yp = jnp.concatenate([u[:, 1:], yhi], axis=1)
    xm = jnp.concatenate([zero, u[:, :, :-1]], axis=2)
    xp = jnp.concatenate([u[:, :, 1:], zero], axis=2)
    return zm, zp, ym, yp, xm, xp


def n_face_set(eta):
    zm, zp, ym, yp, xm, xp = n_neighbours(eta)
    zlo = VERT * (0.5 * (eta + zm))
    zhi = VERT * (0.5 * (eta + zp))
    ylo = 0.5 * (eta + ym)
    yhi = 0.5 * (eta + yp)
    xlo = 0.5 * (eta + xm)
    xhi = 0.5 * (eta + xp)
    return (zlo, zhi, ylo, yhi, xlo, xhi)


def n_operate(u, coef):
    zlo, zhi, ylo, yhi, xlo, xhi, extra = coef
    zm, zp, ym, yp, xm, xp = n_neighbours(u)
    out = zlo * (u - zm) + zhi * (u - zp)
    out = out + ylo * (u - ym) + yhi * (u - yp)
    out = out + xlo * (u - xm) + xhi * (u - xp)
    return out + extra * u


def n_diagonal(coef):
    zlo, zhi, ylo, yhi, xlo, xhi, extra = coef
    return zlo + zhi + ylo + yhi + xlo + xhi + extra


def n_pick_matrix(cols):
    half = cols // 2
    src = lax.broadcasted_iota(jnp.int32, (cols, cols), 0)
    dst = lax.broadcasted_iota(jnp.int32, (cols, cols), 1)
    want = jnp.where(dst < half, 2 * dst, 2 * (dst - half) + 1)
    return (src == want).astype(jnp.float32)


def n_split_x(a):
    cols = a.shape[-1]
    both = jnp.dot(a, n_pick_matrix(cols), precision=HI)
    return both[..., : cols // 2], both[..., cols // 2 :]


def n_mean_four(a):
    e0, o0 = n_split_x(a[:, 0::2])
    e1, o1 = n_split_x(a[:, 1::2])
    return 0.25 * (e0 + e1 + o0 + o1)


def n_coarsen(coef):
    zlo, zhi, ylo, yhi, xlo, xhi, extra = coef
    xlo_e, _ = n_split_x(xlo[:, 0::2] + xlo[:, 1::2])
    _, xhi_o = n_split_x(xhi[:, 0::2] + xhi[:, 1::2])
    ylo_e, ylo_o = n_split_x(ylo[:, 0::2])
    yhi_e, yhi_o = n_split_x(yhi[:, 1::2])
    cxlo = 0.125 * xlo_e
    cxhi = 0.125 * xhi_o
    cylo = 0.125 * (ylo_e + ylo_o)
    cyhi = 0.125 * (yhi_e + yhi_o)
    return (n_mean_four(zlo), n_mean_four(zhi), cylo, cyhi, cxlo, cxhi, n_mean_four(extra))


def n_prolong(field):
    cols = field.shape[-1]
    src = lax.broadcasted_iota(jnp.int32, (cols, 2 * cols), 0)
    dst = lax.broadcasted_iota(jnp.int32, (cols, 2 * cols), 1)
    spread = (src == dst // 2).astype(jnp.float32)
    wide = jnp.dot(field, spread, precision=HI)
    return jnp.repeat(wide, 2, axis=1)


def n_sweep(field, rhs, coef, diag):
    return field + OMEGA * (rhs - n_operate(field, coef)) / diag


def n_body(viscosity, adjoint_source, forward_velocity, friction, ice_mask, grounded_mask):
    layers = viscosity.shape[0]
    cols = viscosity.shape[2]
    half_cols = cols // 2
    gz = lax.axis_index("gz")
    total_layers = layers * lax.axis_size("gz")
    layer = (gz * layers + jnp.arange(layers)).astype(jnp.float32)
    profile = (jnp.float32(total_layers) - layer) / jnp.float32(total_layers)
    wsq = profile * profile
    icef = ice_mask.astype(jnp.float32)
    groundf = grounded_mask.astype(jnp.float32)
    base = 0.05 + 2.0 * (1.0 - icef)
    ground_fric = groundf * friction
    stacked = jnp.concatenate([viscosity, adjoint_source, base[None], ground_fric[None]], axis=0)
    gathered = lax.all_gather(stacked, "gx", axis=0, tiled=False)
    count_x = gathered.shape[0]
    gathered = jnp.concatenate([gathered[i] for i in range(count_x)], axis=2)
    visc_all = gathered[:layers]
    source_all = gathered[layers : 2 * layers]
    base_all = gathered[2 * layers]
    gfr_all = gathered[2 * layers + 1]
    extra = base_all[None, :, :] + gfr_all[None, :, :] * wsq[:, None, None]
    fine = n_face_set(visc_all) + (extra,)
    dfine = n_diagonal(fine)
    middle = n_coarsen(fine)
    dmid = n_diagonal(middle)
    coarse = n_coarsen(middle)
    dcoarse = n_diagonal(coarse)
    lam = OMEGA * source_all / dfine
    for i in range(S0 - 1):
        lam = n_sweep(lam, source_all, fine, dfine)
    b_mid = n_mean_four(source_all - n_operate(lam, fine))
    e_mid = OMEGA * b_mid / dmid
    for i in range(S1 - 1):
        e_mid = n_sweep(e_mid, b_mid, middle, dmid)
    b_low = n_mean_four(b_mid - n_operate(e_mid, middle))
    e_low = OMEGA * b_low / dcoarse
    for i in range(S2 - 1):
        e_low = n_sweep(e_low, b_low, coarse, dcoarse)
    e_mid = e_mid + n_prolong(e_low)
    for i in range(S1):
        e_mid = n_sweep(e_mid, b_mid, middle, dmid)
    lam = lam + n_prolong(e_mid)
    for i in range(S0):
        lam = n_sweep(lam, source_all, fine, dfine)
    own = lax.dynamic_slice_in_dim(lam, lax.axis_index("gx") * cols, cols, 2)
    column = jnp.sum(wsq[:, None, None] * forward_velocity * own, axis=0)
    summed = lax.psum(column, "gz")
    terms = -ground_fric * summed
    gradient = lax.dynamic_slice_in_dim(terms, gz * half_cols, half_cols, 1)
    return (own, gradient)


def body(viscosity, *rest):
    layers, own_rows, cols_own = viscosity.shape
    cols_all = cols_own + 2 * COL_HALO
    wide_bytes = 4 * layers * (own_rows + 2 * FINE_HALO + 2) * cols_all
    if COL_HALO <= cols_own and FINE_HALO + 1 <= own_rows and MID_HALO <= own_rows // 2 and 20 * wide_bytes <= 40 * 2**20 and lax.axis_size("gy") <= 8:
        return body_wide(viscosity, *rest)
    return n_body(viscosity, *rest)


def solution(mesh):
    placed = (
        P("gz", "gy", "gx"),
        P("gz", "gy", "gx"),
        P("gz", "gy", "gx"),
        P("gy", "gx"),
        P("gy", "gx"),
        P("gy", "gx"),
    )
    return jax.shard_map(
        body,
        mesh=mesh,
        in_specs=placed,
        out_specs=(P("gz", "gy", "gx"), P("gy", ("gx", "gz"))),
        check_vma=False,
    )
```

```python
import jax
import jax.numpy as jnp
from jax import lax
from jax.sharding import PartitionSpec as P

S0 = 4
S1 = 4
S2 = 8


OMEGA = 0.8
VERT = 4.0
HI = lax.Precision.HIGHEST
FINE_HALO = 12
MID_HALO = 6
POST_HALO = 4
COL_HALO = 64


def layer_halos(u):
    count = lax.axis_size("gz")
    head = u[:1]
    tail = u[-1:]
    if count == 2:
        first = lax.axis_index("gz") == 0
        got = lax.ppermute(jnp.where(first, tail, head), "gz", [(0, 1), (1, 0)])
        zero = jnp.zeros_like(got)
        return jnp.where(first, zero, got), jnp.where(first, got, zero)
    lo = lax.ppermute(tail, "gz", [(i, i + 1) for i in range(count - 1)])
    hi = lax.ppermute(head, "gz", [(i + 1, i) for i in range(count - 1)])
    return lo, hi


def extend_rows(a, h):
    count = lax.axis_size("gy")
    lo = lax.ppermute(a[:, -h:], "gy", [(i, i + 1) for i in range(count - 1)])
    hi = lax.ppermute(a[:, :h], "gy", [(i + 1, i) for i in range(count - 1)])
    return jnp.concatenate([lo, a, hi], axis=1)


def gather_blocks(a, axis):
    count = lax.axis_size(axis)
    got = [a]
    for s in range(1, count):
        got.append(lax.ppermute(a, axis, [(i, (i + s) % count) for i in range(count)]))
    rev = jnp.stack(got[::-1], axis=0)
    return jnp.roll(rev, lax.axis_index(axis) + 1, axis=0)


def extend_cols(a, h):
    count = lax.axis_size("gx")
    lo = lax.ppermute(a[:, :, -h:], "gx", [(i, i + 1) for i in range(count - 1)])
    hi = lax.ppermute(a[:, :, :h], "gx", [(i + 1, i) for i in range(count - 1)])
    return jnp.concatenate([lo, a, hi], axis=2)


def col_mask(own_cols, h):
    g = lax.axis_index("gx") * own_cols - h + lax.broadcasted_iota(jnp.int32, (1, 1, own_cols + 2 * h), 2)
    return (g >= 0) & (g < own_cols * lax.axis_size("gx"))


def crop(a, h_from, h_to):
    cut = h_from - h_to
    return a[:, cut : a.shape[1] - cut]


def row_mask(own_rows, h):
    g = lax.axis_index("gy") * own_rows - h + lax.broadcasted_iota(jnp.int32, (1, own_rows + 2 * h, 1), 1)
    return (g >= 0) & (g < own_rows * lax.axis_size("gy"))


def neighbours(u):
    zlo, zhi = layer_halos(u)
    zero_row = jnp.zeros_like(u[:, :1])
    zero_col = jnp.zeros_like(u[:, :, :1])
    zm = jnp.concatenate([zlo, u[:-1]], axis=0)
    zp = jnp.concatenate([u[1:], zhi], axis=0)
    ym = jnp.concatenate([zero_row, u[:, :-1]], axis=1)
    yp = jnp.concatenate([u[:, 1:], zero_row], axis=1)
    xm = jnp.concatenate([zero_col, u[:, :, :-1]], axis=2)
    xp = jnp.concatenate([u[:, :, 1:], zero_col], axis=2)
    return zm, zp, ym, yp, xm, xp


def face_set(eta):
    zm, zp, ym, yp, xm, xp = neighbours(eta)
    zlo = VERT * (0.5 * (eta + zm))
    zhi = VERT * (0.5 * (eta + zp))
    ylo = 0.5 * (eta + ym)
    yhi = 0.5 * (eta + yp)
    xlo = 0.5 * (eta + xm)
    xhi = 0.5 * (eta + xp)
    return (zlo, zhi, ylo, yhi, xlo, xhi)


def operate(u, coef):
    zlo, zhi, ylo, yhi, xlo, xhi, extra = coef
    zm, zp, ym, yp, xm, xp = neighbours(u)
    out = zlo * (u - zm) + zhi * (u - zp)
    out = out + ylo * (u - ym) + yhi * (u - yp)
    out = out + xlo * (u - xm) + xhi * (u - xp)
    return out + extra * u


def diagonal(coef):
    zlo, zhi, ylo, yhi, xlo, xhi, extra = coef
    return zlo + zhi + ylo + yhi + xlo + xhi + extra


def pick(n, parity):
    src = lax.broadcasted_iota(jnp.int32, (n, n // 2), 0)
    dst = lax.broadcasted_iota(jnp.int32, (n, n // 2), 1)
    return (src == 2 * dst + parity).astype(jnp.float32)


def cols(a, parity):
    return jnp.dot(a, pick(a.shape[-1], parity), precision=HI)


def rows(a, parity):
    return jnp.einsum("yr,zyx->zrx", pick(a.shape[1], parity), a, precision=HI)


def mean_four(a):
    r0 = rows(a, 0)
    r1 = rows(a, 1)
    return 0.25 * (cols(r0, 0) + cols(r1, 0) + cols(r0, 1) + cols(r1, 1))


def coarsen(coef):
    zlo, zhi, ylo, yhi, xlo, xhi, extra = coef
    cxlo = 0.125 * cols(rows(xlo, 0) + rows(xlo, 1), 0)
    cxhi = 0.125 * cols(rows(xhi, 0) + rows(xhi, 1), 1)
    ylo0 = rows(ylo, 0)
    yhi1 = rows(yhi, 1)
    cylo = 0.125 * (cols(ylo0, 0) + cols(ylo0, 1))
    cyhi = 0.125 * (cols(yhi1, 0) + cols(yhi1, 1))
    return (mean_four(zlo), mean_four(zhi), cylo, cyhi, cxlo, cxhi, mean_four(extra))


def coarsen_stacked(coef):
    layers = coef[0].shape[0]
    width = coef[0].shape[2]
    half = width // 2
    stack = jnp.concatenate(coef, axis=0)
    both_rows = jnp.concatenate([rows(stack, 0), rows(stack, 1)], axis=0)
    src = lax.broadcasted_iota(jnp.int32, (width, width), 0)
    dst = lax.broadcasted_iota(jnp.int32, (width, width), 1)
    want = jnp.where(dst < half, 2 * dst, 2 * (dst - half) + 1)
    picked = jnp.dot(both_rows, (src == want).astype(jnp.float32), precision=HI)
    count = len(coef)

    def part(k, odd_row, odd_col):
        at = (odd_row * count + k) * layers
        return picked[at : at + layers, :, odd_col * half : (odd_col + 1) * half]

    def four(k):
        return 0.25 * (part(k, 0, 0) + part(k, 1, 0) + part(k, 0, 1) + part(k, 1, 1))

    cxlo = 0.125 * (part(4, 0, 0) + part(4, 1, 0))
    cxhi = 0.125 * (part(5, 0, 1) + part(5, 1, 1))
    cylo = 0.125 * (part(2, 0, 0) + part(2, 0, 1))
    cyhi = 0.125 * (part(3, 1, 0) + part(3, 1, 1))
    return (four(0), four(1), cylo, cyhi, cxlo, cxhi, four(6))


def spread(n):
    src = lax.broadcasted_iota(jnp.int32, (n, 2 * n), 0)
    dst = lax.broadcasted_iota(jnp.int32, (n, 2 * n), 1)
    return (src == dst // 2).astype(jnp.float32)


def prolong(field):
    wide = jnp.dot(field, spread(field.shape[-1]), precision=HI)
    return jnp.einsum("ry,zrx->zyx", spread(field.shape[1]), wide, precision=HI)


def sweep(field, rhs, coef, diag, inside):
    new = field + OMEGA * (rhs - operate(field, coef)) / diag
    return jnp.where(inside, new, 0.0)


def smooth(field, rhs, coef, diag, inside, count):
    for i in range(count):
        field = sweep(field, rhs, coef, diag, inside)
    return field


def crop_all(arrs, h_from, h_to):
    return tuple(crop(a, h_from, h_to) for a in arrs)


def body_wide(viscosity, adjoint_source, forward_velocity, friction, ice_mask, grounded_mask):
    layers = viscosity.shape[0]
    own_rows = viscosity.shape[1]
    mid_rows = own_rows // 2
    cols_own = viscosity.shape[2]
    half_cols = cols_own // 2
    gz = lax.axis_index("gz")
    gy = lax.axis_index("gy")
    total_layers = layers * lax.axis_size("gz")
    layer = (gz * layers + jnp.arange(layers)).astype(jnp.float32)
    profile = (jnp.float32(total_layers) - layer) / jnp.float32(total_layers)
    wsq = profile * profile
    icef = ice_mask.astype(jnp.float32)
    groundf = grounded_mask.astype(jnp.float32)
    base = 0.05 + 2.0 * (1.0 - icef)
    ground_fric = groundf * friction
    stacked = jnp.concatenate([viscosity, adjoint_source, base[None], ground_fric[None]], axis=0)
    hv = FINE_HALO + 1
    wide = extend_cols(stacked, COL_HALO)
    ext = extend_rows(jnp.concatenate([wide[:layers], wide[2 * layers :]], axis=0), hv)
    src_e = crop(extend_rows(wide[layers : 2 * layers], hv), hv, FINE_HALO)
    visc_e = ext[:layers]
    base_e = crop(ext[layers : layers + 1], hv, FINE_HALO)[0]
    gfr_e = crop(ext[layers + 1 : layers + 2], hv, FINE_HALO)[0]
    extra = base_e[None, :, :] + gfr_e[None, :, :] * wsq[:, None, None]
    fine = crop_all(face_set(visc_e), hv, FINE_HALO) + (extra,)
    dfine = diagonal(fine)
    middle = coarsen_stacked(fine)
    dmid = diagonal(middle)
    coarse_own = coarsen_stacked(crop_all(middle, FINE_HALO // 2, 0))
    coarse_all = gather_blocks(jnp.concatenate(coarse_own, axis=0), "gy")
    coarse_all = jnp.concatenate([coarse_all[i] for i in range(coarse_all.shape[0])], axis=1)
    coarse = tuple(coarse_all[i * layers : (i + 1) * layers] for i in range(7))
    dcoarse = diagonal(coarse)
    in_fine = row_mask(own_rows, FINE_HALO) & col_mask(cols_own, COL_HALO)
    in_mid = row_mask(mid_rows, FINE_HALO // 2) & col_mask(cols_own // 2, COL_HALO // 2)

    lam = jnp.where(in_fine, OMEGA * src_e / dfine, 0.0)
    lam = smooth(lam, src_e, fine, dfine, in_fine, S0 - 1)
    b_mid = mean_four(src_e - operate(lam, fine))
    coarse_all, b_mid = lax.optimization_barrier((coarse_all, b_mid))
    coarse = tuple(coarse_all[i * layers : (i + 1) * layers] for i in range(7))
    dcoarse = diagonal(coarse)
    e_mid = jnp.where(in_mid, OMEGA * b_mid / dmid, 0.0)
    e_mid = smooth(e_mid, b_mid, middle, dmid, in_mid, S1 - 1)
    hm = FINE_HALO // 2
    res_mid = crop(b_mid - operate(e_mid, middle), hm, 0)
    b_low = gather_blocks(mean_four(res_mid), "gy")
    b_low = jnp.concatenate([b_low[i] for i in range(b_low.shape[0])], axis=1)
    ones = col_mask(cols_own // 4, COL_HALO // 4)
    e_low = jnp.where(ones, OMEGA * b_low / dcoarse, 0.0)
    e_low = smooth(e_low, b_low, coarse, dcoarse, ones, S2 - 1)

    pair = jnp.concatenate([crop(e_mid, hm, 0), crop(b_mid, hm, 0)], axis=0)
    pair = extend_rows(pair, MID_HALO)
    e_mid = pair[:layers]
    b_mid = pair[layers:]
    low_rows = own_rows // 4
    ch = MID_HALO // 2
    padded = jnp.pad(e_low, ((0, 0), (ch, ch), (0, 0)))
    e_near = lax.dynamic_slice_in_dim(padded, gy * low_rows, low_rows + 2 * ch, 1)
    e_mid = e_mid + prolong(e_near)
    middle_p = crop_all(middle, hm, MID_HALO)
    dmid_p = crop(dmid, hm, MID_HALO)
    in_mid_p = row_mask(mid_rows, MID_HALO) & col_mask(cols_own // 2, COL_HALO // 2)
    e_mid = smooth(e_mid, b_mid, middle_p, dmid_p, in_mid_p, S1)

    lam = crop(lam, FINE_HALO, POST_HALO) + prolong(crop(e_mid, MID_HALO, POST_HALO // 2))
    fine_p = crop_all(fine, FINE_HALO, POST_HALO)
    dfine_p = crop(dfine, FINE_HALO, POST_HALO)
    src_p = crop(src_e, FINE_HALO, POST_HALO)
    in_fine_p = row_mask(own_rows, POST_HALO) & col_mask(cols_own, COL_HALO)
    lam = smooth(lam, src_p, fine_p, dfine_p, in_fine_p, S0)
    lam = crop(lam, POST_HALO, 0)

    own = lam[:, :, COL_HALO : COL_HALO + cols_own]
    column = jnp.sum(wsq[:, None, None] * forward_velocity * own, axis=0)
    parts = gather_blocks(column, "gz")
    summed = parts[0]
    for k in range(1, parts.shape[0]):
        summed = summed + parts[k]
    terms = -ground_fric * summed
    gradient = lax.dynamic_slice_in_dim(terms, gz * half_cols, half_cols, 1)
    return (own, gradient)


def n_layer_halos(u):
    count = lax.axis_size("gz")
    head = u[:1]
    tail = u[-1:]
    if count == 2:
        first = lax.axis_index("gz") == 0
        got = lax.ppermute(jnp.where(first, tail, head), "gz", [(0, 1), (1, 0)])
        zero = jnp.zeros_like(got)
        return jnp.where(first, zero, got), jnp.where(first, got, zero)
    lo = lax.ppermute(tail, "gz", [(i, i + 1) for i in range(count - 1)])
    hi = lax.ppermute(head, "gz", [(i + 1, i) for i in range(count - 1)])
    return lo, hi


def n_row_halos(u):
    count = lax.axis_size("gy")
    lo = lax.ppermute(u[:, -1:], "gy", [(i, i + 1) for i in range(count - 1)])
    hi = lax.ppermute(u[:, :1], "gy", [(i + 1, i) for i in range(count - 1)])
    return lo, hi


def n_neighbours(u):
    zlo, zhi = n_layer_halos(u)
    ylo, yhi = n_row_halos(u)
    zero = jnp.zeros_like(u[:, :, :1])
    zm = jnp.concatenate([zlo, u[:-1]], axis=0)
    zp = jnp.concatenate([u[1:], zhi], axis=0)
    ym = jnp.concatenate([ylo, u[:, :-1]], axis=1)
    yp = jnp.concatenate([u[:, 1:], yhi], axis=1)
    xm = jnp.concatenate([zero, u[:, :, :-1]], axis=2)
    xp = jnp.concatenate([u[:, :, 1:], zero], axis=2)
    return zm, zp, ym, yp, xm, xp


def n_face_set(eta):
    zm, zp, ym, yp, xm, xp = n_neighbours(eta)
    zlo = VERT * (0.5 * (eta + zm))
    zhi = VERT * (0.5 * (eta + zp))
    ylo = 0.5 * (eta + ym)
    yhi = 0.5 * (eta + yp)
    xlo = 0.5 * (eta + xm)
    xhi = 0.5 * (eta + xp)
    return (zlo, zhi, ylo, yhi, xlo, xhi)


def n_operate(u, coef):
    zlo, zhi, ylo, yhi, xlo, xhi, extra = coef
    zm, zp, ym, yp, xm, xp = n_neighbours(u)
    out = zlo * (u - zm) + zhi * (u - zp)
    out = out + ylo * (u - ym) + yhi * (u - yp)
    out = out + xlo * (u - xm) + xhi * (u - xp)
    return out + extra * u


def n_diagonal(coef):
    zlo, zhi, ylo, yhi, xlo, xhi, extra = coef
    return zlo + zhi + ylo + yhi + xlo + xhi + extra


def n_pick_matrix(cols):
    half = cols // 2
    src = lax.broadcasted_iota(jnp.int32, (cols, cols), 0)
    dst = lax.broadcasted_iota(jnp.int32, (cols, cols), 1)
    want = jnp.where(dst < half, 2 * dst, 2 * (dst - half) + 1)
    return (src == want).astype(jnp.float32)


def n_split_x(a):
    cols = a.shape[-1]
    both = jnp.dot(a, n_pick_matrix(cols), precision=HI)
    return both[..., : cols // 2], both[..., cols // 2 :]


def n_mean_four(a):
    e0, o0 = n_split_x(a[:, 0::2])
    e1, o1 = n_split_x(a[:, 1::2])
    return 0.25 * (e0 + e1 + o0 + o1)


def n_coarsen(coef):
    zlo, zhi, ylo, yhi, xlo, xhi, extra = coef
    xlo_e, _ = n_split_x(xlo[:, 0::2] + xlo[:, 1::2])
    _, xhi_o = n_split_x(xhi[:, 0::2] + xhi[:, 1::2])
    ylo_e, ylo_o = n_split_x(ylo[:, 0::2])
    yhi_e, yhi_o = n_split_x(yhi[:, 1::2])
    cxlo = 0.125 * xlo_e
    cxhi = 0.125 * xhi_o
    cylo = 0.125 * (ylo_e + ylo_o)
    cyhi = 0.125 * (yhi_e + yhi_o)
    return (n_mean_four(zlo), n_mean_four(zhi), cylo, cyhi, cxlo, cxhi, n_mean_four(extra))


def n_prolong(field):
    cols = field.shape[-1]
    src = lax.broadcasted_iota(jnp.int32, (cols, 2 * cols), 0)
    dst = lax.broadcasted_iota(jnp.int32, (cols, 2 * cols), 1)
    spread = (src == dst // 2).astype(jnp.float32)
    wide = jnp.dot(field, spread, precision=HI)
    return jnp.repeat(wide, 2, axis=1)


def n_sweep(field, rhs, coef, diag):
    return field + OMEGA * (rhs - n_operate(field, coef)) / diag


def n_body(viscosity, adjoint_source, forward_velocity, friction, ice_mask, grounded_mask):
    layers = viscosity.shape[0]
    cols = viscosity.shape[2]
    half_cols = cols // 2
    gz = lax.axis_index("gz")
    total_layers = layers * lax.axis_size("gz")
    layer = (gz * layers + jnp.arange(layers)).astype(jnp.float32)
    profile = (jnp.float32(total_layers) - layer) / jnp.float32(total_layers)
    wsq = profile * profile
    icef = ice_mask.astype(jnp.float32)
    groundf = grounded_mask.astype(jnp.float32)
    base = 0.05 + 2.0 * (1.0 - icef)
    ground_fric = groundf * friction
    stacked = jnp.concatenate([viscosity, adjoint_source, base[None], ground_fric[None]], axis=0)
    gathered = lax.all_gather(stacked, "gx", axis=0, tiled=False)
    count_x = gathered.shape[0]
    gathered = jnp.concatenate([gathered[i] for i in range(count_x)], axis=2)
    visc_all = gathered[:layers]
    source_all = gathered[layers : 2 * layers]
    base_all = gathered[2 * layers]
    gfr_all = gathered[2 * layers + 1]
    extra = base_all[None, :, :] + gfr_all[None, :, :] * wsq[:, None, None]
    fine = n_face_set(visc_all) + (extra,)
    dfine = n_diagonal(fine)
    middle = n_coarsen(fine)
    dmid = n_diagonal(middle)
    coarse = n_coarsen(middle)
    dcoarse = n_diagonal(coarse)
    lam = OMEGA * source_all / dfine
    for i in range(S0 - 1):
        lam = n_sweep(lam, source_all, fine, dfine)
    b_mid = n_mean_four(source_all - n_operate(lam, fine))
    e_mid = OMEGA * b_mid / dmid
    for i in range(S1 - 1):
        e_mid = n_sweep(e_mid, b_mid, middle, dmid)
    b_low = n_mean_four(b_mid - n_operate(e_mid, middle))
    e_low = OMEGA * b_low / dcoarse
    for i in range(S2 - 1):
        e_low = n_sweep(e_low, b_low, coarse, dcoarse)
    e_mid = e_mid + n_prolong(e_low)
    for i in range(S1):
        e_mid = n_sweep(e_mid, b_mid, middle, dmid)
    lam = lam + n_prolong(e_mid)
    for i in range(S0):
        lam = n_sweep(lam, source_all, fine, dfine)
    own = lax.dynamic_slice_in_dim(lam, lax.axis_index("gx") * cols, cols, 2)
    column = jnp.sum(wsq[:, None, None] * forward_velocity * own, axis=0)
    summed = lax.psum(column, "gz")
    terms = -ground_fric * summed
    gradient = lax.dynamic_slice_in_dim(terms, gz * half_cols, half_cols, 1)
    return (own, gradient)


def body(viscosity, *rest):
    layers, own_rows, cols_own = viscosity.shape
    cols_all = cols_own + 2 * COL_HALO
    wide_bytes = 4 * layers * (own_rows + 2 * FINE_HALO + 2) * cols_all
    if COL_HALO <= cols_own and FINE_HALO + 1 <= own_rows and MID_HALO <= own_rows // 2 and 20 * wide_bytes <= 40 * 2**20 and lax.axis_size("gy") <= 8:
        return body_wide(viscosity, *rest)
    return n_body(viscosity, *rest)


def solution(mesh):
    placed = (
        P("gz", "gy", "gx"),
        P("gz", "gy", "gx"),
        P("gz", "gy", "gx"),
        P("gy", "gx"),
        P("gy", "gx"),
        P("gy", "gx"),
    )
    return jax.shard_map(
        body,
        mesh=mesh,
        in_specs=placed,
        out_specs=(P("gz", "gy", "gx"), P("gy", ("gx", "gz"))),
        check_vma=False,
    )
```

```python
import jax
import jax.numpy as jnp
from jax import lax
from jax.sharding import PartitionSpec as P

S0 = 4
S1 = 4
S2 = 8


OMEGA = 0.8
VERT = 4.0
HI = lax.Precision.HIGHEST
FINE_HALO = 12
MID_HALO = 6
POST_HALO = 4
COL_HALO = 64


def layer_halos(u):
    count = lax.axis_size("gz")
    head = u[:1]
    tail = u[-1:]
    if count == 2:
        first = lax.axis_index("gz") == 0
        got = lax.ppermute(jnp.where(first, tail, head), "gz", [(0, 1), (1, 0)])
        zero = jnp.zeros_like(got)
        return jnp.where(first, zero, got), jnp.where(first, got, zero)
    lo = lax.ppermute(tail, "gz", [(i, i + 1) for i in range(count - 1)])
    hi = lax.ppermute(head, "gz", [(i + 1, i) for i in range(count - 1)])
    return lo, hi


def extend_rows(a, h):
    count = lax.axis_size("gy")
    lo = lax.ppermute(a[:, -h:], "gy", [(i, i + 1) for i in range(count - 1)])
    hi = lax.ppermute(a[:, :h], "gy", [(i + 1, i) for i in range(count - 1)])
    return jnp.concatenate([lo, a, hi], axis=1)


def gather_blocks(a, axis):
    count = lax.axis_size(axis)
    got = [a]
    for s in range(1, count):
        got.append(lax.ppermute(a, axis, [(i, (i + s) % count) for i in range(count)]))
    rev = jnp.stack(got[::-1], axis=0)
    return jnp.roll(rev, lax.axis_index(axis) + 1, axis=0)


def extend_cols(a, h):
    count = lax.axis_size("gx")
    lo = lax.ppermute(a[:, :, -h:], "gx", [(i, i + 1) for i in range(count - 1)])
    hi = lax.ppermute(a[:, :, :h], "gx", [(i + 1, i) for i in range(count - 1)])
    return jnp.concatenate([lo, a, hi], axis=2)


def col_mask(own_cols, h):
    g = lax.axis_index("gx") * own_cols - h + lax.broadcasted_iota(jnp.int32, (1, 1, own_cols + 2 * h), 2)
    return (g >= 0) & (g < own_cols * lax.axis_size("gx"))


def crop(a, h_from, h_to):
    cut = h_from - h_to
    return a[:, cut : a.shape[1] - cut]


def row_mask(own_rows, h):
    g = lax.axis_index("gy") * own_rows - h + lax.broadcasted_iota(jnp.int32, (1, own_rows + 2 * h, 1), 1)
    return (g >= 0) & (g < own_rows * lax.axis_size("gy"))


def neighbours(u):
    zlo, zhi = layer_halos(u)
    zero_row = jnp.zeros_like(u[:, :1])
    zero_col = jnp.zeros_like(u[:, :, :1])
    zm = jnp.concatenate([zlo, u[:-1]], axis=0)
    zp = jnp.concatenate([u[1:], zhi], axis=0)
    ym = jnp.concatenate([zero_row, u[:, :-1]], axis=1)
    yp = jnp.concatenate([u[:, 1:], zero_row], axis=1)
    xm = jnp.concatenate([zero_col, u[:, :, :-1]], axis=2)
    xp = jnp.concatenate([u[:, :, 1:], zero_col], axis=2)
    return zm, zp, ym, yp, xm, xp


def face_set(eta):
    zm, zp, ym, yp, xm, xp = neighbours(eta)
    zlo = VERT * (0.5 * (eta + zm))
    zhi = VERT * (0.5 * (eta + zp))
    ylo = 0.5 * (eta + ym)
    yhi = 0.5 * (eta + yp)
    xlo = 0.5 * (eta + xm)
    xhi = 0.5 * (eta + xp)
    return (zlo, zhi, ylo, yhi, xlo, xhi)


def operate(u, coef):
    zlo, zhi, ylo, yhi, xlo, xhi, extra = coef
    zm, zp, ym, yp, xm, xp = neighbours(u)
    out = zlo * (u - zm) + zhi * (u - zp)
    out = out + ylo * (u - ym) + yhi * (u - yp)
    out = out + xlo * (u - xm) + xhi * (u - xp)
    return out + extra * u


def diagonal(coef):
    zlo, zhi, ylo, yhi, xlo, xhi, extra = coef
    return zlo + zhi + ylo + yhi + xlo + xhi + extra


def pick(n, parity):
    src = lax.broadcasted_iota(jnp.int32, (n, n // 2), 0)
    dst = lax.broadcasted_iota(jnp.int32, (n, n // 2), 1)
    return (src == 2 * dst + parity).astype(jnp.float32)


def cols(a, parity):
    return jnp.dot(a, pick(a.shape[-1], parity), precision=HI)


def rows(a, parity):
    return jnp.einsum("yr,zyx->zrx", pick(a.shape[1], parity), a, precision=HI)


def mean_four(a):
    r0 = rows(a, 0)
    r1 = rows(a, 1)
    return 0.25 * (cols(r0, 0) + cols(r1, 0) + cols(r0, 1) + cols(r1, 1))


def coarsen(coef):
    zlo, zhi, ylo, yhi, xlo, xhi, extra = coef
    cxlo = 0.125 * cols(rows(xlo, 0) + rows(xlo, 1), 0)
    cxhi = 0.125 * cols(rows(xhi, 0) + rows(xhi, 1), 1)
    ylo0 = rows(ylo, 0)
    yhi1 = rows(yhi, 1)
    cylo = 0.125 * (cols(ylo0, 0) + cols(ylo0, 1))
    cyhi = 0.125 * (cols(yhi1, 0) + cols(yhi1, 1))
    return (mean_four(zlo), mean_four(zhi), cylo, cyhi, cxlo, cxhi, mean_four(extra))


def coarsen_stacked(coef):
    layers = coef[0].shape[0]
    width = coef[0].shape[2]
    half = width // 2
    stack = jnp.concatenate(coef, axis=0)
    both_rows = jnp.concatenate([rows(stack, 0), rows(stack, 1)], axis=0)
    src = lax.broadcasted_iota(jnp.int32, (width, width), 0)
    dst = lax.broadcasted_iota(jnp.int32, (width, width), 1)
    want = jnp.where(dst < half, 2 * dst, 2 * (dst - half) + 1)
    picked = jnp.dot(both_rows, (src == want).astype(jnp.float32), precision=HI)
    count = len(coef)

    def part(k, odd_row, odd_col):
        at = (odd_row * count + k) * layers
        return picked[at : at + layers, :, odd_col * half : (odd_col + 1) * half]

    def four(k):
        return 0.25 * (part(k, 0, 0) + part(k, 1, 0) + part(k, 0, 1) + part(k, 1, 1))

    cxlo = 0.125 * (part(4, 0, 0) + part(4, 1, 0))
    cxhi = 0.125 * (part(5, 0, 1) + part(5, 1, 1))
    cylo = 0.125 * (part(2, 0, 0) + part(2, 0, 1))
    cyhi = 0.125 * (part(3, 1, 0) + part(3, 1, 1))
    return (four(0), four(1), cylo, cyhi, cxlo, cxhi, four(6))


def spread(n):
    src = lax.broadcasted_iota(jnp.int32, (n, 2 * n), 0)
    dst = lax.broadcasted_iota(jnp.int32, (n, 2 * n), 1)
    return (src == dst // 2).astype(jnp.float32)


def prolong(field):
    wide = jnp.dot(field, spread(field.shape[-1]), precision=HI)
    return jnp.einsum("ry,zrx->zyx", spread(field.shape[1]), wide, precision=HI)


def sweep(field, rhs, coef, diag, inside):
    new = field + OMEGA * (rhs - operate(field, coef)) / diag
    return jnp.where(inside, new, 0.0)


def smooth(field, rhs, coef, diag, inside, count):
    for i in range(count):
        field = sweep(field, rhs, coef, diag, inside)
    return field


def crop_all(arrs, h_from, h_to):
    return tuple(crop(a, h_from, h_to) for a in arrs)


def body_wide(viscosity, adjoint_source, forward_velocity, friction, ice_mask, grounded_mask):
    layers = viscosity.shape[0]
    own_rows = viscosity.shape[1]
    mid_rows = own_rows // 2
    cols_own = viscosity.shape[2]
    half_cols = cols_own // 2
    gz = lax.axis_index("gz")
    gy = lax.axis_index("gy")
    total_layers = layers * lax.axis_size("gz")
    layer = (gz * layers + jnp.arange(layers)).astype(jnp.float32)
    profile = (jnp.float32(total_layers) - layer) / jnp.float32(total_layers)
    wsq = profile * profile
    icef = ice_mask.astype(jnp.float32)
    groundf = grounded_mask.astype(jnp.float32)
    base = 0.05 + 2.0 * (1.0 - icef)
    ground_fric = groundf * friction
    stacked = jnp.concatenate([viscosity, adjoint_source, base[None], ground_fric[None]], axis=0)
    hv = FINE_HALO + 1
    wide = extend_cols(stacked, COL_HALO)
    ext = extend_rows(jnp.concatenate([wide[:layers], wide[2 * layers :]], axis=0), hv)
    src_e = crop(extend_rows(wide[layers : 2 * layers], hv), hv, FINE_HALO)
    visc_e = ext[:layers]
    base_e = crop(ext[layers : layers + 1], hv, FINE_HALO)[0]
    gfr_e = crop(ext[layers + 1 : layers + 2], hv, FINE_HALO)[0]
    extra = base_e[None, :, :] + gfr_e[None, :, :] * wsq[:, None, None]
    fine = crop_all(face_set(visc_e), hv, FINE_HALO) + (extra,)
    dfine = diagonal(fine)
    middle = coarsen_stacked(fine)
    dmid = diagonal(middle)
    coarse_own = coarsen_stacked(crop_all(middle, FINE_HALO // 2, 0))
    coarse_stack, src_e = lax.optimization_barrier((jnp.concatenate(coarse_own, axis=0), src_e))
    coarse_all = gather_blocks(coarse_stack, "gy")
    coarse_all = jnp.concatenate([coarse_all[i] for i in range(coarse_all.shape[0])], axis=1)
    coarse = tuple(coarse_all[i * layers : (i + 1) * layers] for i in range(7))
    dcoarse = diagonal(coarse)
    in_fine = row_mask(own_rows, FINE_HALO) & col_mask(cols_own, COL_HALO)
    in_mid = row_mask(mid_rows, FINE_HALO // 2) & col_mask(cols_own // 2, COL_HALO // 2)

    lam = jnp.where(in_fine, OMEGA * src_e / dfine, 0.0)
    lam = smooth(lam, src_e, fine, dfine, in_fine, S0 - 1)
    b_mid = mean_four(src_e - operate(lam, fine))
    coarse_all, b_mid = lax.optimization_barrier((coarse_all, b_mid))
    coarse = tuple(coarse_all[i * layers : (i + 1) * layers] for i in range(7))
    dcoarse = diagonal(coarse)
    e_mid = jnp.where(in_mid, OMEGA * b_mid / dmid, 0.0)
    e_mid = smooth(e_mid, b_mid, middle, dmid, in_mid, S1 - 1)
    hm = FINE_HALO // 2
    res_mid = crop(b_mid - operate(e_mid, middle), hm, 0)
    b_low = gather_blocks(mean_four(res_mid), "gy")
    b_low = jnp.concatenate([b_low[i] for i in range(b_low.shape[0])], axis=1)
    ones = col_mask(cols_own // 4, COL_HALO // 4)
    e_low = jnp.where(ones, OMEGA * b_low / dcoarse, 0.0)
    e_low = smooth(e_low, b_low, coarse, dcoarse, ones, S2 - 1)

    pair = jnp.concatenate([crop(e_mid, hm, 0), crop(b_mid, hm, 0)], axis=0)
    pair = extend_rows(pair, MID_HALO)
    e_mid = pair[:layers]
    b_mid = pair[layers:]
    low_rows = own_rows // 4
    ch = MID_HALO // 2
    padded = jnp.pad(e_low, ((0, 0), (ch, ch), (0, 0)))
    e_near = lax.dynamic_slice_in_dim(padded, gy * low_rows, low_rows + 2 * ch, 1)
    e_mid = e_mid + prolong(e_near)
    middle_p = crop_all(middle, hm, MID_HALO)
    dmid_p = crop(dmid, hm, MID_HALO)
    in_mid_p = row_mask(mid_rows, MID_HALO) & col_mask(cols_own // 2, COL_HALO // 2)
    e_mid = smooth(e_mid, b_mid, middle_p, dmid_p, in_mid_p, S1)

    lam = crop(lam, FINE_HALO, POST_HALO) + prolong(crop(e_mid, MID_HALO, POST_HALO // 2))
    fine_p = crop_all(fine, FINE_HALO, POST_HALO)
    dfine_p = crop(dfine, FINE_HALO, POST_HALO)
    src_p = crop(src_e, FINE_HALO, POST_HALO)
    in_fine_p = row_mask(own_rows, POST_HALO) & col_mask(cols_own, COL_HALO)
    lam = smooth(lam, src_p, fine_p, dfine_p, in_fine_p, S0)
    lam = crop(lam, POST_HALO, 0)

    own = lam[:, :, COL_HALO : COL_HALO + cols_own]
    column = jnp.sum(wsq[:, None, None] * forward_velocity * own, axis=0)
    parts = gather_blocks(column, "gz")
    summed = parts[0]
    for k in range(1, parts.shape[0]):
        summed = summed + parts[k]
    terms = -ground_fric * summed
    gradient = lax.dynamic_slice_in_dim(terms, gz * half_cols, half_cols, 1)
    return (own, gradient)


def n_layer_halos(u):
    count = lax.axis_size("gz")
    head = u[:1]
    tail = u[-1:]
    if count == 2:
        first = lax.axis_index("gz") == 0
        got = lax.ppermute(jnp.where(first, tail, head), "gz", [(0, 1), (1, 0)])
        zero = jnp.zeros_like(got)
        return jnp.where(first, zero, got), jnp.where(first, got, zero)
    lo = lax.ppermute(tail, "gz", [(i, i + 1) for i in range(count - 1)])
    hi = lax.ppermute(head, "gz", [(i + 1, i) for i in range(count - 1)])
    return lo, hi


def n_row_halos(u):
    count = lax.axis_size("gy")
    lo = lax.ppermute(u[:, -1:], "gy", [(i, i + 1) for i in range(count - 1)])
    hi = lax.ppermute(u[:, :1], "gy", [(i + 1, i) for i in range(count - 1)])
    return lo, hi


def n_neighbours(u):
    zlo, zhi = n_layer_halos(u)
    ylo, yhi = n_row_halos(u)
    zero = jnp.zeros_like(u[:, :, :1])
    zm = jnp.concatenate([zlo, u[:-1]], axis=0)
    zp = jnp.concatenate([u[1:], zhi], axis=0)
    ym = jnp.concatenate([ylo, u[:, :-1]], axis=1)
    yp = jnp.concatenate([u[:, 1:], yhi], axis=1)
    xm = jnp.concatenate([zero, u[:, :, :-1]], axis=2)
    xp = jnp.concatenate([u[:, :, 1:], zero], axis=2)
    return zm, zp, ym, yp, xm, xp


def n_face_set(eta):
    zm, zp, ym, yp, xm, xp = n_neighbours(eta)
    zlo = VERT * (0.5 * (eta + zm))
    zhi = VERT * (0.5 * (eta + zp))
    ylo = 0.5 * (eta + ym)
    yhi = 0.5 * (eta + yp)
    xlo = 0.5 * (eta + xm)
    xhi = 0.5 * (eta + xp)
    return (zlo, zhi, ylo, yhi, xlo, xhi)


def n_operate(u, coef):
    zlo, zhi, ylo, yhi, xlo, xhi, extra = coef
    zm, zp, ym, yp, xm, xp = n_neighbours(u)
    out = zlo * (u - zm) + zhi * (u - zp)
    out = out + ylo * (u - ym) + yhi * (u - yp)
    out = out + xlo * (u - xm) + xhi * (u - xp)
    return out + extra * u


def n_diagonal(coef):
    zlo, zhi, ylo, yhi, xlo, xhi, extra = coef
    return zlo + zhi + ylo + yhi + xlo + xhi + extra


def n_pick_matrix(cols):
    half = cols // 2
    src = lax.broadcasted_iota(jnp.int32, (cols, cols), 0)
    dst = lax.broadcasted_iota(jnp.int32, (cols, cols), 1)
    want = jnp.where(dst < half, 2 * dst, 2 * (dst - half) + 1)
    return (src == want).astype(jnp.float32)


def n_split_x(a):
    cols = a.shape[-1]
    both = jnp.dot(a, n_pick_matrix(cols), precision=HI)
    return both[..., : cols // 2], both[..., cols // 2 :]


def n_mean_four(a):
    e0, o0 = n_split_x(a[:, 0::2])
    e1, o1 = n_split_x(a[:, 1::2])
    return 0.25 * (e0 + e1 + o0 + o1)


def n_coarsen(coef):
    zlo, zhi, ylo, yhi, xlo, xhi, extra = coef
    xlo_e, _ = n_split_x(xlo[:, 0::2] + xlo[:, 1::2])
    _, xhi_o = n_split_x(xhi[:, 0::2] + xhi[:, 1::2])
    ylo_e, ylo_o = n_split_x(ylo[:, 0::2])
    yhi_e, yhi_o = n_split_x(yhi[:, 1::2])
    cxlo = 0.125 * xlo_e
    cxhi = 0.125 * xhi_o
    cylo = 0.125 * (ylo_e + ylo_o)
    cyhi = 0.125 * (yhi_e + yhi_o)
    return (n_mean_four(zlo), n_mean_four(zhi), cylo, cyhi, cxlo, cxhi, n_mean_four(extra))


def n_prolong(field):
    cols = field.shape[-1]
    src = lax.broadcasted_iota(jnp.int32, (cols, 2 * cols), 0)
    dst = lax.broadcasted_iota(jnp.int32, (cols, 2 * cols), 1)
    spread = (src == dst // 2).astype(jnp.float32)
    wide = jnp.dot(field, spread, precision=HI)
    return jnp.repeat(wide, 2, axis=1)


def n_sweep(field, rhs, coef, diag):
    return field + OMEGA * (rhs - n_operate(field, coef)) / diag


def n_body(viscosity, adjoint_source, forward_velocity, friction, ice_mask, grounded_mask):
    layers = viscosity.shape[0]
    cols = viscosity.shape[2]
    half_cols = cols // 2
    gz = lax.axis_index("gz")
    total_layers = layers * lax.axis_size("gz")
    layer = (gz * layers + jnp.arange(layers)).astype(jnp.float32)
    profile = (jnp.float32(total_layers) - layer) / jnp.float32(total_layers)
    wsq = profile * profile
    icef = ice_mask.astype(jnp.float32)
    groundf = grounded_mask.astype(jnp.float32)
    base = 0.05 + 2.0 * (1.0 - icef)
    ground_fric = groundf * friction
    stacked = jnp.concatenate([viscosity, adjoint_source, base[None], ground_fric[None]], axis=0)
    gathered = lax.all_gather(stacked, "gx", axis=0, tiled=False)
    count_x = gathered.shape[0]
    gathered = jnp.concatenate([gathered[i] for i in range(count_x)], axis=2)
    visc_all = gathered[:layers]
    source_all = gathered[layers : 2 * layers]
    base_all = gathered[2 * layers]
    gfr_all = gathered[2 * layers + 1]
    extra = base_all[None, :, :] + gfr_all[None, :, :] * wsq[:, None, None]
    fine = n_face_set(visc_all) + (extra,)
    dfine = n_diagonal(fine)
    middle = n_coarsen(fine)
    dmid = n_diagonal(middle)
    coarse = n_coarsen(middle)
    dcoarse = n_diagonal(coarse)
    lam = OMEGA * source_all / dfine
    for i in range(S0 - 1):
        lam = n_sweep(lam, source_all, fine, dfine)
    b_mid = n_mean_four(source_all - n_operate(lam, fine))
    e_mid = OMEGA * b_mid / dmid
    for i in range(S1 - 1):
        e_mid = n_sweep(e_mid, b_mid, middle, dmid)
    b_low = n_mean_four(b_mid - n_operate(e_mid, middle))
    e_low = OMEGA * b_low / dcoarse
    for i in range(S2 - 1):
        e_low = n_sweep(e_low, b_low, coarse, dcoarse)
    e_mid = e_mid + n_prolong(e_low)
    for i in range(S1):
        e_mid = n_sweep(e_mid, b_mid, middle, dmid)
    lam = lam + n_prolong(e_mid)
    for i in range(S0):
        lam = n_sweep(lam, source_all, fine, dfine)
    own = lax.dynamic_slice_in_dim(lam, lax.axis_index("gx") * cols, cols, 2)
    column = jnp.sum(wsq[:, None, None] * forward_velocity * own, axis=0)
    summed = lax.psum(column, "gz")
    terms = -ground_fric * summed
    gradient = lax.dynamic_slice_in_dim(terms, gz * half_cols, half_cols, 1)
    return (own, gradient)


def body(viscosity, *rest):
    layers, own_rows, cols_own = viscosity.shape
    cols_all = cols_own + 2 * COL_HALO
    wide_bytes = 4 * layers * (own_rows + 2 * FINE_HALO + 2) * cols_all
    if COL_HALO <= cols_own and FINE_HALO + 1 <= own_rows and MID_HALO <= own_rows // 2 and 20 * wide_bytes <= 40 * 2**20 and lax.axis_size("gy") <= 8:
        return body_wide(viscosity, *rest)
    return n_body(viscosity, *rest)


def solution(mesh):
    placed = (
        P("gz", "gy", "gx"),
        P("gz", "gy", "gx"),
        P("gz", "gy", "gx"),
        P("gy", "gx"),
        P("gy", "gx"),
        P("gy", "gx"),
    )
    return jax.shard_map(
        body,
        mesh=mesh,
        in_specs=placed,
        out_specs=(P("gz", "gy", "gx"), P("gy", ("gx", "gz"))),
        check_vma=False,
    )
```

```python
import jax
import jax.numpy as jnp
from jax import lax
from jax.sharding import PartitionSpec as P

S0 = 4
S1 = 4
S2 = 8


OMEGA = 0.8
VERT = 4.0
HI = lax.Precision.HIGHEST
FINE_HALO = 12
MID_HALO = 6
POST_HALO = 4
COL_HALO = 64


def layer_halos(u):
    count = lax.axis_size("gz")
    head = u[:1]
    tail = u[-1:]
    if count == 2:
        first = lax.axis_index("gz") == 0
        got = lax.ppermute(jnp.where(first, tail, head), "gz", [(0, 1), (1, 0)])
        zero = jnp.zeros_like(got)
        return jnp.where(first, zero, got), jnp.where(first, got, zero)
    lo = lax.ppermute(tail, "gz", [(i, i + 1) for i in range(count - 1)])
    hi = lax.ppermute(head, "gz", [(i + 1, i) for i in range(count - 1)])
    return lo, hi


def extend_rows(a, h):
    count = lax.axis_size("gy")
    lo = lax.ppermute(a[:, -h:], "gy", [(i, i + 1) for i in range(count - 1)])
    hi = lax.ppermute(a[:, :h], "gy", [(i + 1, i) for i in range(count - 1)])
    return jnp.concatenate([lo, a, hi], axis=1)


def gather_blocks(a, axis):
    count = lax.axis_size(axis)
    got = [a]
    for s in range(1, count):
        got.append(lax.ppermute(a, axis, [(i, (i + s) % count) for i in range(count)]))
    rev = jnp.stack(got[::-1], axis=0)
    return jnp.roll(rev, lax.axis_index(axis) + 1, axis=0)


def extend_cols(a, h):
    count = lax.axis_size("gx")
    lo = lax.ppermute(a[:, :, -h:], "gx", [(i, i + 1) for i in range(count - 1)])
    hi = lax.ppermute(a[:, :, :h], "gx", [(i + 1, i) for i in range(count - 1)])
    return jnp.concatenate([lo, a, hi], axis=2)


def col_mask(own_cols, h):
    g = lax.axis_index("gx") * own_cols - h + lax.broadcasted_iota(jnp.int32, (1, 1, own_cols + 2 * h), 2)
    return (g >= 0) & (g < own_cols * lax.axis_size("gx"))


def crop(a, h_from, h_to):
    cut = h_from - h_to
    return a[:, cut : a.shape[1] - cut]


def row_mask(own_rows, h):
    g = lax.axis_index("gy") * own_rows - h + lax.broadcasted_iota(jnp.int32, (1, own_rows + 2 * h, 1), 1)
    return (g >= 0) & (g < own_rows * lax.axis_size("gy"))


def neighbours(u):
    zlo, zhi = layer_halos(u)
    zero_row = jnp.zeros_like(u[:, :1])
    zero_col = jnp.zeros_like(u[:, :, :1])
    zm = jnp.concatenate([zlo, u[:-1]], axis=0)
    zp = jnp.concatenate([u[1:], zhi], axis=0)
    ym = jnp.concatenate([zero_row, u[:, :-1]], axis=1)
    yp = jnp.concatenate([u[:, 1:], zero_row], axis=1)
    xm = jnp.concatenate([zero_col, u[:, :, :-1]], axis=2)
    xp = jnp.concatenate([u[:, :, 1:], zero_col], axis=2)
    return zm, zp, ym, yp, xm, xp


def face_set(eta):
    zm, zp, ym, yp, xm, xp = neighbours(eta)
    zlo = VERT * (0.5 * (eta + zm))
    zhi = VERT * (0.5 * (eta + zp))
    ylo = 0.5 * (eta + ym)
    yhi = 0.5 * (eta + yp)
    xlo = 0.5 * (eta + xm)
    xhi = 0.5 * (eta + xp)
    return (zlo, zhi, ylo, yhi, xlo, xhi)


def operate(u, coef):
    zlo, zhi, ylo, yhi, xlo, xhi, extra = coef
    zm, zp, ym, yp, xm, xp = neighbours(u)
    out = zlo * (u - zm) + zhi * (u - zp)
    out = out + ylo * (u - ym) + yhi * (u - yp)
    out = out + xlo * (u - xm) + xhi * (u - xp)
    return out + extra * u


def diagonal(coef):
    zlo, zhi, ylo, yhi, xlo, xhi, extra = coef
    return zlo + zhi + ylo + yhi + xlo + xhi + extra


def pick(n, parity):
    src = lax.broadcasted_iota(jnp.int32, (n, n // 2), 0)
    dst = lax.broadcasted_iota(jnp.int32, (n, n // 2), 1)
    return (src == 2 * dst + parity).astype(jnp.float32)


def cols(a, parity):
    return jnp.dot(a, pick(a.shape[-1], parity), precision=HI)


def rows(a, parity):
    return jnp.einsum("yr,zyx->zrx", pick(a.shape[1], parity), a, precision=HI)


def mean_four(a):
    r0 = rows(a, 0)
    r1 = rows(a, 1)
    return 0.25 * (cols(r0, 0) + cols(r1, 0) + cols(r0, 1) + cols(r1, 1))


def coarsen(coef):
    zlo, zhi, ylo, yhi, xlo, xhi, extra = coef
    cxlo = 0.125 * cols(rows(xlo, 0) + rows(xlo, 1), 0)
    cxhi = 0.125 * cols(rows(xhi, 0) + rows(xhi, 1), 1)
    ylo0 = rows(ylo, 0)
    yhi1 = rows(yhi, 1)
    cylo = 0.125 * (cols(ylo0, 0) + cols(ylo0, 1))
    cyhi = 0.125 * (cols(yhi1, 0) + cols(yhi1, 1))
    return (mean_four(zlo), mean_four(zhi), cylo, cyhi, cxlo, cxhi, mean_four(extra))


def coarsen_stacked(coef):
    layers = coef[0].shape[0]
    width = coef[0].shape[2]
    half = width // 2
    stack = jnp.concatenate(coef, axis=0)
    both_rows = jnp.concatenate([rows(stack, 0), rows(stack, 1)], axis=0)
    src = lax.broadcasted_iota(jnp.int32, (width, width), 0)
    dst = lax.broadcasted_iota(jnp.int32, (width, width), 1)
    want = jnp.where(dst < half, 2 * dst, 2 * (dst - half) + 1)
    picked = jnp.dot(both_rows, (src == want).astype(jnp.float32), precision=HI)
    count = len(coef)

    def part(k, odd_row, odd_col):
        at = (odd_row * count + k) * layers
        return picked[at : at + layers, :, odd_col * half : (odd_col + 1) * half]

    def four(k):
        return 0.25 * (part(k, 0, 0) + part(k, 1, 0) + part(k, 0, 1) + part(k, 1, 1))

    cxlo = 0.125 * (part(4, 0, 0) + part(4, 1, 0))
    cxhi = 0.125 * (part(5, 0, 1) + part(5, 1, 1))
    cylo = 0.125 * (part(2, 0, 0) + part(2, 0, 1))
    cyhi = 0.125 * (part(3, 1, 0) + part(3, 1, 1))
    return (four(0), four(1), cylo, cyhi, cxlo, cxhi, four(6))


def spread(n):
    src = lax.broadcasted_iota(jnp.int32, (n, 2 * n), 0)
    dst = lax.broadcasted_iota(jnp.int32, (n, 2 * n), 1)
    return (src == dst // 2).astype(jnp.float32)


def prolong(field):
    wide = jnp.dot(field, spread(field.shape[-1]), precision=HI)
    return jnp.einsum("ry,zrx->zyx", spread(field.shape[1]), wide, precision=HI)


def sweep(field, rhs, coef, diag, inside):
    new = field + OMEGA * (rhs - operate(field, coef)) / diag
    return jnp.where(inside, new, 0.0)


def smooth(field, rhs, coef, diag, inside, count):
    for i in range(count):
        field = sweep(field, rhs, coef, diag, inside)
    return field


def crop_all(arrs, h_from, h_to):
    return tuple(crop(a, h_from, h_to) for a in arrs)


def body_wide(viscosity, adjoint_source, forward_velocity, friction, ice_mask, grounded_mask):
    layers = viscosity.shape[0]
    own_rows = viscosity.shape[1]
    mid_rows = own_rows // 2
    cols_own = viscosity.shape[2]
    half_cols = cols_own // 2
    gz = lax.axis_index("gz")
    gy = lax.axis_index("gy")
    total_layers = layers * lax.axis_size("gz")
    layer = (gz * layers + jnp.arange(layers)).astype(jnp.float32)
    profile = (jnp.float32(total_layers) - layer) / jnp.float32(total_layers)
    wsq = profile * profile
    icef = ice_mask.astype(jnp.float32)
    groundf = grounded_mask.astype(jnp.float32)
    base = 0.05 + 2.0 * (1.0 - icef)
    ground_fric = groundf * friction
    stacked = jnp.concatenate([viscosity, adjoint_source, base[None], ground_fric[None]], axis=0)
    hv = FINE_HALO + 1
    wide = extend_cols(stacked, COL_HALO)
    ext = extend_rows(jnp.concatenate([wide[:layers], wide[2 * layers :]], axis=0), hv)
    src_e = crop(extend_rows(wide[layers : 2 * layers], hv), hv, FINE_HALO)
    visc_e = ext[:layers]
    base_e = crop(ext[layers : layers + 1], hv, FINE_HALO)[0]
    gfr_e = crop(ext[layers + 1 : layers + 2], hv, FINE_HALO)[0]
    extra = base_e[None, :, :] + gfr_e[None, :, :] * wsq[:, None, None]
    fine = crop_all(face_set(visc_e), hv, FINE_HALO) + (extra,)
    dfine = diagonal(fine)
    middle = coarsen_stacked(fine)
    dmid = diagonal(middle)
    coarse_own = coarsen_stacked(crop_all(middle, FINE_HALO // 2, 0))
    coarse_stack, src_e = lax.optimization_barrier((jnp.concatenate(coarse_own, axis=0), src_e))
    coarse_all = gather_blocks(coarse_stack, "gy")
    coarse_all = jnp.concatenate([coarse_all[i] for i in range(coarse_all.shape[0])], axis=1)
    coarse = tuple(coarse_all[i * layers : (i + 1) * layers] for i in range(7))
    dcoarse = diagonal(coarse)
    in_fine = row_mask(own_rows, FINE_HALO) & col_mask(cols_own, COL_HALO)
    in_mid = row_mask(mid_rows, FINE_HALO // 2) & col_mask(cols_own // 2, COL_HALO // 2)

    lam = jnp.where(in_fine, OMEGA * src_e / dfine, 0.0)
    lam = smooth(lam, src_e, fine, dfine, in_fine, S0 - 1)
    b_mid = mean_four(src_e - operate(lam, fine))
    coarse_all, b_mid = lax.optimization_barrier((coarse_all, b_mid))
    b_mid_post = extend_rows(crop(b_mid, FINE_HALO // 2, 0), MID_HALO)
    coarse = tuple(coarse_all[i * layers : (i + 1) * layers] for i in range(7))
    dcoarse = diagonal(coarse)
    e_mid = jnp.where(in_mid, OMEGA * b_mid / dmid, 0.0)
    e_mid = smooth(e_mid, b_mid, middle, dmid, in_mid, S1 - 1)
    hm = FINE_HALO // 2
    res_mid = crop(b_mid - operate(e_mid, middle), hm, 0)
    b_low = gather_blocks(mean_four(res_mid), "gy")
    b_low = jnp.concatenate([b_low[i] for i in range(b_low.shape[0])], axis=1)
    ones = col_mask(cols_own // 4, COL_HALO // 4)
    e_low = jnp.where(ones, OMEGA * b_low / dcoarse, 0.0)
    e_low = smooth(e_low, b_low, coarse, dcoarse, ones, S2 - 1)

    e_mid = extend_rows(crop(e_mid, hm, 0), MID_HALO)
    b_mid = b_mid_post
    low_rows = own_rows // 4
    ch = MID_HALO // 2
    padded = jnp.pad(e_low, ((0, 0), (ch, ch), (0, 0)))
    e_near = lax.dynamic_slice_in_dim(padded, gy * low_rows, low_rows + 2 * ch, 1)
    e_mid = e_mid + prolong(e_near)
    middle_p = crop_all(middle, hm, MID_HALO)
    dmid_p = crop(dmid, hm, MID_HALO)
    in_mid_p = row_mask(mid_rows, MID_HALO) & col_mask(cols_own // 2, COL_HALO // 2)
    e_mid = smooth(e_mid, b_mid, middle_p, dmid_p, in_mid_p, S1)

    lam = crop(lam, FINE_HALO, POST_HALO) + prolong(crop(e_mid, MID_HALO, POST_HALO // 2))
    fine_p = crop_all(fine, FINE_HALO, POST_HALO)
    dfine_p = crop(dfine, FINE_HALO, POST_HALO)
    src_p = crop(src_e, FINE_HALO, POST_HALO)
    in_fine_p = row_mask(own_rows, POST_HALO) & col_mask(cols_own, COL_HALO)
    lam = smooth(lam, src_p, fine_p, dfine_p, in_fine_p, S0)
    lam = crop(lam, POST_HALO, 0)

    own = lam[:, :, COL_HALO : COL_HALO + cols_own]
    column = jnp.sum(wsq[:, None, None] * forward_velocity * own, axis=0)
    parts = gather_blocks(column, "gz")
    summed = parts[0]
    for k in range(1, parts.shape[0]):
        summed = summed + parts[k]
    terms = -ground_fric * summed
    gradient = lax.dynamic_slice_in_dim(terms, gz * half_cols, half_cols, 1)
    return (own, gradient)


def n_layer_halos(u):
    count = lax.axis_size("gz")
    head = u[:1]
    tail = u[-1:]
    if count == 2:
        first = lax.axis_index("gz") == 0
        got = lax.ppermute(jnp.where(first, tail, head), "gz", [(0, 1), (1, 0)])
        zero = jnp.zeros_like(got)
        return jnp.where(first, zero, got), jnp.where(first, got, zero)
    lo = lax.ppermute(tail, "gz", [(i, i + 1) for i in range(count - 1)])
    hi = lax.ppermute(head, "gz", [(i + 1, i) for i in range(count - 1)])
    return lo, hi


def n_row_halos(u):
    count = lax.axis_size("gy")
    lo = lax.ppermute(u[:, -1:], "gy", [(i, i + 1) for i in range(count - 1)])
    hi = lax.ppermute(u[:, :1], "gy", [(i + 1, i) for i in range(count - 1)])
    return lo, hi


def n_neighbours(u):
    zlo, zhi = n_layer_halos(u)
    ylo, yhi = n_row_halos(u)
    zero = jnp.zeros_like(u[:, :, :1])
    zm = jnp.concatenate([zlo, u[:-1]], axis=0)
    zp = jnp.concatenate([u[1:], zhi], axis=0)
    ym = jnp.concatenate([ylo, u[:, :-1]], axis=1)
    yp = jnp.concatenate([u[:, 1:], yhi], axis=1)
    xm = jnp.concatenate([zero, u[:, :, :-1]], axis=2)
    xp = jnp.concatenate([u[:, :, 1:], zero], axis=2)
    return zm, zp, ym, yp, xm, xp


def n_face_set(eta):
    zm, zp, ym, yp, xm, xp = n_neighbours(eta)
    zlo = VERT * (0.5 * (eta + zm))
    zhi = VERT * (0.5 * (eta + zp))
    ylo = 0.5 * (eta + ym)
    yhi = 0.5 * (eta + yp)
    xlo = 0.5 * (eta + xm)
    xhi = 0.5 * (eta + xp)
    return (zlo, zhi, ylo, yhi, xlo, xhi)


def n_operate(u, coef):
    zlo, zhi, ylo, yhi, xlo, xhi, extra = coef
    zm, zp, ym, yp, xm, xp = n_neighbours(u)
    out = zlo * (u - zm) + zhi * (u - zp)
    out = out + ylo * (u - ym) + yhi * (u - yp)
    out = out + xlo * (u - xm) + xhi * (u - xp)
    return out + extra * u


def n_diagonal(coef):
    zlo, zhi, ylo, yhi, xlo, xhi, extra = coef
    return zlo + zhi + ylo + yhi + xlo + xhi + extra


def n_pick_matrix(cols):
    half = cols // 2
    src = lax.broadcasted_iota(jnp.int32, (cols, cols), 0)
    dst = lax.broadcasted_iota(jnp.int32, (cols, cols), 1)
    want = jnp.where(dst < half, 2 * dst, 2 * (dst - half) + 1)
    return (src == want).astype(jnp.float32)


def n_split_x(a):
    cols = a.shape[-1]
    both = jnp.dot(a, n_pick_matrix(cols), precision=HI)
    return both[..., : cols // 2], both[..., cols // 2 :]


def n_mean_four(a):
    e0, o0 = n_split_x(a[:, 0::2])
    e1, o1 = n_split_x(a[:, 1::2])
    return 0.25 * (e0 + e1 + o0 + o1)


def n_coarsen(coef):
    zlo, zhi, ylo, yhi, xlo, xhi, extra = coef
    xlo_e, _ = n_split_x(xlo[:, 0::2] + xlo[:, 1::2])
    _, xhi_o = n_split_x(xhi[:, 0::2] + xhi[:, 1::2])
    ylo_e, ylo_o = n_split_x(ylo[:, 0::2])
    yhi_e, yhi_o = n_split_x(yhi[:, 1::2])
    cxlo = 0.125 * xlo_e
    cxhi = 0.125 * xhi_o
    cylo = 0.125 * (ylo_e + ylo_o)
    cyhi = 0.125 * (yhi_e + yhi_o)
    return (n_mean_four(zlo), n_mean_four(zhi), cylo, cyhi, cxlo, cxhi, n_mean_four(extra))


def n_prolong(field):
    cols = field.shape[-1]
    src = lax.broadcasted_iota(jnp.int32, (cols, 2 * cols), 0)
    dst = lax.broadcasted_iota(jnp.int32, (cols, 2 * cols), 1)
    spread = (src == dst // 2).astype(jnp.float32)
    wide = jnp.dot(field, spread, precision=HI)
    return jnp.repeat(wide, 2, axis=1)


def n_sweep(field, rhs, coef, diag):
    return field + OMEGA * (rhs - n_operate(field, coef)) / diag


def n_body(viscosity, adjoint_source, forward_velocity, friction, ice_mask, grounded_mask):
    layers = viscosity.shape[0]
    cols = viscosity.shape[2]
    half_cols = cols // 2
    gz = lax.axis_index("gz")
    total_layers = layers * lax.axis_size("gz")
    layer = (gz * layers + jnp.arange(layers)).astype(jnp.float32)
    profile = (jnp.float32(total_layers) - layer) / jnp.float32(total_layers)
    wsq = profile * profile
    icef = ice_mask.astype(jnp.float32)
    groundf = grounded_mask.astype(jnp.float32)
    base = 0.05 + 2.0 * (1.0 - icef)
    ground_fric = groundf * friction
    stacked = jnp.concatenate([viscosity, adjoint_source, base[None], ground_fric[None]], axis=0)
    gathered = lax.all_gather(stacked, "gx", axis=0, tiled=False)
    count_x = gathered.shape[0]
    gathered = jnp.concatenate([gathered[i] for i in range(count_x)], axis=2)
    visc_all = gathered[:layers]
    source_all = gathered[layers : 2 * layers]
    base_all = gathered[2 * layers]
    gfr_all = gathered[2 * layers + 1]
    extra = base_all[None, :, :] + gfr_all[None, :, :] * wsq[:, None, None]
    fine = n_face_set(visc_all) + (extra,)
    dfine = n_diagonal(fine)
    middle = n_coarsen(fine)
    dmid = n_diagonal(middle)
    coarse = n_coarsen(middle)
    dcoarse = n_diagonal(coarse)
    lam = OMEGA * source_all / dfine
    for i in range(S0 - 1):
        lam = n_sweep(lam, source_all, fine, dfine)
    b_mid = n_mean_four(source_all - n_operate(lam, fine))
    e_mid = OMEGA * b_mid / dmid
    for i in range(S1 - 1):
        e_mid = n_sweep(e_mid, b_mid, middle, dmid)
    b_low = n_mean_four(b_mid - n_operate(e_mid, middle))
    e_low = OMEGA * b_low / dcoarse
    for i in range(S2 - 1):
        e_low = n_sweep(e_low, b_low, coarse, dcoarse)
    e_mid = e_mid + n_prolong(e_low)
    for i in range(S1):
        e_mid = n_sweep(e_mid, b_mid, middle, dmid)
    lam = lam + n_prolong(e_mid)
    for i in range(S0):
        lam = n_sweep(lam, source_all, fine, dfine)
    own = lax.dynamic_slice_in_dim(lam, lax.axis_index("gx") * cols, cols, 2)
    column = jnp.sum(wsq[:, None, None] * forward_velocity * own, axis=0)
    summed = lax.psum(column, "gz")
    terms = -ground_fric * summed
    gradient = lax.dynamic_slice_in_dim(terms, gz * half_cols, half_cols, 1)
    return (own, gradient)


def body(viscosity, *rest):
    layers, own_rows, cols_own = viscosity.shape
    cols_all = cols_own + 2 * COL_HALO
    wide_bytes = 4 * layers * (own_rows + 2 * FINE_HALO + 2) * cols_all
    if COL_HALO <= cols_own and FINE_HALO + 1 <= own_rows and MID_HALO <= own_rows // 2 and 20 * wide_bytes <= 40 * 2**20 and lax.axis_size("gy") <= 8:
        return body_wide(viscosity, *rest)
    return n_body(viscosity, *rest)


def solution(mesh):
    placed = (
        P("gz", "gy", "gx"),
        P("gz", "gy", "gx"),
        P("gz", "gy", "gx"),
        P("gy", "gx"),
        P("gy", "gx"),
        P("gy", "gx"),
    )
    return jax.shard_map(
        body,
        mesh=mesh,
        in_specs=placed,
        out_specs=(P("gz", "gy", "gx"), P("gy", ("gx", "gz"))),
        check_vma=False,
    )
```
